128 devices in a mesh: grp: 2 (over z_hi), tile: 32 (over x, y, core), spec: 2 (over z_lo).
Axes of the slice: x: 4, y: 4, z: 4 (z_hi: 2, z_lo: 2; z = z_hi * 2 + z_lo), core: 2. Of those that a mesh axis runs over, the one named last changes fastest.
Arguments:
- spectrum: float32 [2, 32, 36, 256, 256], P('grp', None, 'spec', 'tile'), may hold values from 0.01 to 1
- wind: float32 [2, 256, 256], P(None, 'tile'), may hold values from -48 to 48
- land_mask: int32 [256, 256], P('tile'), may hold values 0 or 1
- intersection: int32 [256, 256], P('tile'), may hold values from 0 to 255, as said below
- ocean_state: float32 [2, 3, 16, 256, 256], P('grp', None, 'spec', 'tile'), may hold values from -1 to 1
- sea_level: float32 [2, 256, 256], P('grp', 'tile'), may hold values from -1 to 1
Outputs:
- spectrum_next: float32 [2, 32, 36, 256, 256], P('grp', None, 'spec', 'tile')
- ocean_next: float32 [2, 3, 16, 256, 256], P('grp', None, 'spec', 'tile')
The draws below stay inside these ranges and needn't reach their ends.
Inputs may be any that keep to these rules, and one draw needn't show every extreme that they name: In each row i, intersection[i, j] = (j + s_i) mod 256 for a shift s_i of that row.
All inputs are finite; a program needn't handle non-finite values. No bound on the sum of `land_mask` on one device may be relied on, other than what follows from the above.
Results may differ from the reference program's by a relative error of at most 0.0001.
Values sent between devices are 32-bit elements; how exact they have to be, the bound alone decides.
A program may use at most 128 MiB of HBM per device.

```python
import math
import jax
import jax.numpy as jnp
from jax import lax

FREQS = 32
DIRS = 36
NX = 256
LEVELS = 16
WSTEPS = 4
OSTEPS = 2
NY = 256


def draw_intersection(key, part):
    shifts = jax.random.randint(key, (NY, 1), 0, NX)
    columns = jnp.arange(NX, dtype=jnp.int32)[None, :]
    return ((columns + shifts) % NX).astype(jnp.int32)


def place_ends(values, own_key, least, high):
    shape = values.shape
    index_at = [jax.random.randint(jax.random.fold_in(own_key, axis), (), 0, shape[axis]) for axis in range(len(shape))]
    values = values.at[tuple(index_at)].set(least)
    longest = shape.index(max(shape))
    index_at[longest] = (index_at[longest] + 1) % shape[longest]
    return values.at[tuple(index_at)].set(high)


def block_scale(own_key, extent, shards, smallest, largest):
    gain, own = 1.0, jax.random.fold_in(own_key, 6)
    for dim, parts in shards:
        draws = jnp.exp(jax.random.uniform(jax.random.fold_in(own, dim), (parts,), jnp.float32, smallest / len(shards), largest / len(shards)))
        gain = gain * jnp.repeat(draws, extent[dim] // parts).reshape([-1 if axis == dim else 1 for axis in range(len(extent))])
    return gain


def noise(stream_key, dims, spread, limit, pieces=(), held_as=jnp.bfloat16):
    result = spread * jax.random.normal(stream_key, dims, jnp.float32)
    if pieces:
        result = result * block_scale(stream_key, dims, pieces, -0.22, 0.18)
    return jnp.clip(result, -limit, limit).astype(held_as)


def setup_inputs(seed: int = 0) -> dict:
    seeds = jax.random.split(jax.random.key(seed), 7)
    return {
        "spectrum": jnp.clip(jnp.exp(math.log(1.0) - 4.6051702 * jax.random.uniform(seeds[0], (2, FREQS, DIRS, NY, NX), jnp.float32) ** block_scale(seeds[0], (2, FREQS, DIRS, NY, NX), ((0, 2), (2, 2), (3, 32)), -0.2, 0.2)), 0.01, 1.0),
        "wind": noise(seeds[1], (2, NY, NX), 8.0, 48.0, ((1, 32),), jnp.float32),
        "land_mask": place_ends((jax.random.randint(seeds[2], (NY, NX), 0, 4) < 3).astype(jnp.int32), jax.random.fold_in(seeds[2], 1), 0, 1),
        "intersection": draw_intersection(jax.random.fold_in(seeds[6], 71), 0),
        "ocean_state": jnp.clip(jax.random.uniform(seeds[4], (2, 3, LEVELS, NX, NY), jnp.float32, -1.0, 1.0) * block_scale(seeds[4], (2, 3, LEVELS, NX, NY), ((0, 2), (2, 2), (3, 32)), -0.4, 0.0), -1.0, 1.0),
        "sea_level": jnp.clip(jax.random.uniform(seeds[5], (2, NX, NY), jnp.float32, -1.0, 1.0) * block_scale(seeds[5], (2, NX, NY), ((0, 2), (1, 32)), -0.4, 0.0), -1.0, 1.0),
    }


exact_precision = lax.Precision.HIGHEST


def wave_tables():
    freq_index = jnp.arange(FREQS, dtype=jnp.float32)
    frequency = 0.04 * 1.1 ** freq_index
    celerity = 1.56 / frequency
    group_speed = 0.4 * 1.1 ** (-freq_index)
    bin_width = 0.1 * frequency * (2.0 * math.pi / DIRS)
    angles = 2.0 * math.pi * (jnp.arange(DIRS, dtype=jnp.float32) + 0.5) / DIRS
    return frequency, celerity, group_speed, bin_width, jnp.cos(angles), jnp.sin(angles)


def level_tables():
    level_depth = (jnp.arange(LEVELS, dtype=jnp.float32) + 0.5) / LEVELS
    profile = jnp.exp(-2.0 * level_depth)
    return profile / jnp.sum(profile), profile


def east_west(energy, speeds):
    widths = [(0, 0)] * (energy.ndim - 1) + [(1, 1)]
    padded_energy = jnp.pad(energy, widths)
    padded_speed = jnp.pad(speeds, widths)
    fluxes = jnp.maximum(padded_speed[..., :-1], 0.0) * padded_energy[..., :-1] + jnp.minimum(padded_speed[..., 1:], 0.0) * padded_energy[..., 1:]
    return fluxes[..., 1:] - fluxes[..., :-1]


def north_south(with_rims, speed_rims):
    fluxes = jnp.maximum(speed_rims[..., :-1, :], 0.0) * with_rims[..., :-1, :] + jnp.minimum(speed_rims[..., 1:, :], 0.0) * with_rims[..., 1:, :]
    return fluxes[..., 1:, :] - fluxes[..., :-1, :]


def band_terms(advected, growth, breaking, energy, dir_cosines, dir_sines, bin_width, celerity, frequency):
    pushing = growth * breaking * advected
    stirring = jnp.stack([jnp.einsum("fdrx,d->frx", pushing, dir_cosines, precision=exact_precision), jnp.einsum("fdrx,d->frx", pushing, dir_sines, precision=exact_precision)])
    drifting = jnp.stack([jnp.einsum("fdrx,d->frx", energy, dir_cosines, precision=exact_precision), jnp.einsum("fdrx,d->frx", energy, dir_sines, precision=exact_precision)])
    stress = 5.0 * jnp.einsum("f,cfrx->crx", bin_width / celerity, stirring, precision=exact_precision)
    stokes = 20.0 * jnp.einsum("f,cfrx->crx", bin_width * frequency ** 3, drifting, precision=exact_precision)
    return jnp.concatenate([stress, stokes], axis=0)


def reorder(values, index):
    return jnp.take_along_axis(values, jnp.broadcast_to(index[None], values.shape), axis=2)


def ocean_update(ocean_fields, padded, ocean_mask, forcing, profile, top_level):
    lateral = padded[:, 1:-1, 2:, 1:-1] + padded[:, 1:-1, :-2, 1:-1] + padded[:, 1:-1, 1:-1, 2:] + padded[:, 1:-1, 1:-1, :-2] - 4.0 * ocean_fields
    vertical = padded[:, 2:, 1:-1, 1:-1] + padded[:, :-2, 1:-1, 1:-1] - 2.0 * ocean_fields
    diffused = ocean_fields + 0.1 * lateral + 0.2 * vertical
    shaped = profile[:, None, None]
    new_east = diffused[0] + 0.1 * (ocean_fields[1] + shaped * forcing[3]) + top_level * forcing[0]
    new_north = diffused[1] - 0.1 * (ocean_fields[0] + shaped * forcing[2]) + top_level * forcing[1]
    return jnp.stack([new_east, new_north, diffused[2]]) * ocean_mask


def reference(spectrum, wind, land_mask, intersection, ocean_state, sea_level):
    frequency, celerity, group_speed, bin_width, dir_cosines, dir_sines = wave_tables()
    weights, profile = level_tables()
    wet_cells = land_mask.astype(jnp.float32)
    ocean = ocean_state[1]
    currents = jnp.einsum("k,ckmi->cmi", weights, ocean[:2], precision=exact_precision)
    packed = jnp.concatenate([currents, sea_level[1][None]], axis=0)
    rows_form = jnp.transpose(packed, (0, 2, 1))
    picked = reorder(rows_form, intersection)
    water_depth = 10.0 + 4.0 * picked[2]
    speed_east = wet_cells * (group_speed[:, None, None, None] * dir_cosines[None, :, None, None] + 0.1 * picked[0])
    speed_north = wet_cells * (group_speed[:, None, None, None] * dir_sines[None, :, None, None] + 0.1 * picked[1])
    north_rims = jnp.pad(speed_north, ((0, 0), (0, 0), (1, 1), (0, 0)))
    drive = (wind[0][None] * dir_cosines[:, None, None] + wind[1][None] * dir_sines[:, None, None])[None] / celerity[:, None, None, None]
    growth = 0.05 * jnp.maximum(drive - 1.0, 0.0)
    energy = spectrum[0]
    for substep in range(WSTEPS):
        with_rims = jnp.pad(energy, ((0, 0), (0, 0), (1, 1), (0, 0)))
        advected = energy - east_west(energy, speed_east) - north_south(with_rims, north_rims)
        energy_total = jnp.tensordot(bin_width, jnp.sum(advected, axis=1), axes=1, precision=exact_precision)
        breaking = 1.0 / (1.0 + 25.0 * energy_total / (water_depth * water_depth))
        energy = wet_cells * breaking * advected * (1.0 + growth)
    band_fields = band_terms(advected, growth, breaking, energy, dir_cosines, dir_sines, bin_width, celerity, frequency)
    row_index = lax.broadcasted_iota(jnp.int32, intersection.shape, 0)
    col_index = lax.broadcasted_iota(jnp.int32, intersection.shape, 1)
    inverse = jnp.zeros(intersection.shape, jnp.int32).at[row_index, intersection].set(col_index)
    forcing = jnp.transpose(reorder(band_fields, inverse), (0, 2, 1))
    ocean_mask = jnp.transpose(jnp.take_along_axis(wet_cells, inverse, axis=1))
    top_level = (jnp.arange(LEVELS) == 0).astype(jnp.float32)[:, None, None]
    ocean_fields = ocean
    for substep in range(OSTEPS):
        padded = jnp.pad(ocean_fields, ((0, 0), (1, 1), (1, 1), (1, 1)))
        ocean_fields = ocean_update(ocean_fields, padded, ocean_mask, forcing, profile, top_level)
    spectrum_next = jnp.stack([energy, jnp.zeros_like(energy)])
    ocean_next = jnp.stack([jnp.zeros_like(ocean_fields), ocean_fields])
    return spectrum_next, ocean_next
```

```python
import math

import jax
import jax.numpy as jnp
import numpy as np
from jax import lax
from jax.experimental import pallas as pl
from jax.experimental.pallas import tpu as pltpu
from jax.sharding import PartitionSpec as P

FREQS = 32
DIRS = 36
LEVELS = 16
WSTEPS = 4
TILES = 32
DLOC = 18
KLOC = 8
FD = FREQS * DLOC
CHUNKS = 8
FCH = FREQS // CHUNKS
RCH = FCH * DLOC
F32 = jnp.float32

_freq = 0.04 * 1.1 ** np.arange(FREQS)
_cel = 1.56 / _freq
_gs = 0.4 * 1.1 ** (-np.arange(FREQS, dtype=np.float64))
_bw = 0.1 * _freq * (2.0 * math.pi / DIRS)
TABLE = np.stack([_gs, 0.05 / _cel, _bw, 5.0 * _bw / _cel, 20.0 * _bw * _freq**3]).astype(np.float32)
_ang = 2.0 * math.pi * (np.arange(DIRS) + 0.5) / DIRS
COS = [float(np.float32(x)) for x in np.cos(_ang)[:DLOC]]
SIN = [float(np.float32(x)) for x in np.sin(_ang)[:DLOC]]
_prof = np.exp(-2.0 * (np.arange(LEVELS) + 0.5) / LEVELS)
_wgt = _prof / _prof.sum()


def mesh_copy(src, dst, send, recv, where):
    return pltpu.make_async_remote_copy(
        src_ref=src,
        dst_ref=dst,
        send_sem=send,
        recv_sem=recv,
        device_id=where,
        device_id_type=pl.DeviceIdType.MESH,
    )


def settle(buf, sem):
    pltpu.make_async_copy(buf, buf, sem).wait()


def kernel(
    tab, spec_h, wind_h, land_h, inter_h, ocean_h, sea_h, out_w, out_o,
    B, G, WD, CNT, H, S, wind, land, inter, NBS, NBR, QR, TS, TR, BANDS, BANDR, MSG2, MMSG,
    Q, A1, A2, sea, CS, CR, SX, MSG, MR, BR, BTS, ES, EH, LS, LH, zbuf,
    load_sem, small_sem, h_send, h_recv, t_send, t_recv, nb_send, nb_recv,
    q_send, q_recv, m_send, m_recv, f_send, f_recv, c_send, c_recv, e_send, e_recv, l_send, l_recv, out_sem,
):
    grp = lax.axis_index("grp")
    tile = lax.axis_index("tile")
    sp = lax.axis_index("spec")
    other = 1 - sp
    sgn = (1 - 2 * sp).astype(F32)
    has_lo = tile > 0
    has_hi = tile < TILES - 1
    lo_t = jnp.maximum(tile - 1, 0)
    hi_t = jnp.minimum(tile + 1, TILES - 1)
    lane = lax.broadcasted_iota(jnp.int32, (8, 128), 1)
    row = lax.broadcasted_iota(jnp.int32, (8, 128), 0)
    first_lane, last_lane = lane == 0, lane == 127
    first_row, last_row = row == 0, row == 7
    low_rows = row < 4
    halves = (slice(0, 128), slice(128, 256))

    def from_left(x):
        a, b = pltpu.roll(x[0], 1, 1), pltpu.roll(x[1], 1, 1)
        return jnp.where(first_lane, 0.0, a), jnp.where(first_lane, a, b)

    def from_right(x):
        a, b = pltpu.roll(x[0], 127, 1), pltpu.roll(x[1], 127, 1)
        return jnp.where(last_lane, b, a), jnp.where(last_lane, 0.0, b)

    def circular(x, shift):
        a, b = pltpu.roll(x[0], shift, 1), pltpu.roll(x[1], shift, 1)
        m = lane < shift
        return jnp.where(m, b, a), jnp.where(m, a, b)

    def barrel(x, amount):
        for bit in range(8):
            moved = circular(x, 1 << bit) if bit < 7 else (x[1], x[0])
            x = tuple(jnp.where((amount[h] & (1 << bit)) != 0, moved[h], x[h]) for h in range(2))
        return x

    def pair(ref, *lead):
        return tuple(ref[(*lead, slice(None), hs)] for hs in halves)

    def put(ref, value, rows):
        for h in range(2):
            ref[rows, halves[h]] = value[h]

    @pl.when(grp == 0)
    def wave():
        def load(c):
            rows = pl.ds(pl.multiple_of(c * RCH * 8, 8), RCH * 8)
            return [
                pltpu.make_async_copy(spec_h.at[rows, hs], B.at[h, rows, :], load_sem.at[c, h])
                for h, hs in enumerate(halves)
            ]

        smalls = [
            pltpu.make_async_copy(wind_h, wind, small_sem.at[0]),
            pltpu.make_async_copy(land_h, land, small_sem.at[1]),
            pltpu.make_async_copy(inter_h, inter, small_sem.at[2]),
        ]
        for copy in smalls:
            copy.start()

        def begin(c, carry):
            for copy in load(c):
                copy.start()
            return carry

        lax.fori_loop(0, CHUNKS, begin, 0)

        def halo(n, side, c):
            rows = pl.ds(pl.multiple_of(c * RCH, 8), RCH)
            return mesh_copy(
                S.at[n, side, :, rows, :], H.at[n, side, :, rows, :], h_send.at[n, side, c], h_recv.at[n, side, c],
                {"tile": hi_t if side == 0 else lo_t},
            )

        def edges_out(n, c):
            for k in range(RCH // 8):
                at = c * RCH + 8 * k
                rows = pl.ds(pl.multiple_of(at, 8), 8)
                for h in range(2):
                    S[n, 0, h, rows, :] = B[h, pl.ds(at * 8 + 7, 8, stride=8), :]
                    S[n, 1, h, rows, :] = B[h, pl.ds(at * 8, 8, stride=8), :]

            @pl.when(has_hi)
            def _():
                halo(n, 0, c).start()

            @pl.when(has_lo)
            def _():
                halo(n, 1, c).start()

        for copy in smalls:
            copy.wait()
        wet_i = pair(land)
        wet = tuple(x.astype(F32) for x in wet_i)
        shift = tuple((x - lane - 128 * h) & 255 for h, x in enumerate(pair(inter)))
        put(NBS, wet_i, slice(0, 8))
        put(NBS, shift, slice(8, 16))

        def neighbour(side):
            return mesh_copy(
                NBS, NBR.at[side], nb_send.at[side], nb_recv.at[side],
                {"tile": hi_t if side == 0 else lo_t},
            )

        @pl.when(has_hi)
        def _():
            neighbour(0).start()

        @pl.when(has_lo)
        def _():
            neighbour(1).start()

        wet_back = circular(barrel(wet, shift), 1)

        def windows(fields, u):
            acc = jnp.zeros((8, 128), F32)
            for f, field in enumerate(fields):
                start = (8 * u + 32 * f) % 128
                offset = (lane - start) & 127
                inside = offset < 10
                base = (8 * u) // 128
                p = 8 * u + offset
                value = field[base]
                if 8 * u % 128 + 10 > 128:
                    turned = (lane - 32 * f) & 127
                    value = jnp.where(turned < 16, field[1 - base], value)
                acc = jnp.where(inside, value, acc)
            return acc

        for u in range(TILES):
            MMSG[pl.ds(8 * u, 8), :] = windows([wet_back], u)

        def to_ocean(src, dst, send, recv, u):
            return mesh_copy(
                src.at[pl.ds(pl.multiple_of(u * 8, 8), 8), :],
                dst.at[pl.ds(pl.multiple_of(tile * 8, 8), 8), :],
                send, recv, {"grp": 1, "tile": u},
            )

        def send_mask(u, carry):
            to_ocean(MMSG, MR, m_send, m_recv, u).start()
            return carry

        lax.fori_loop(0, TILES, send_mask, 0)

        @pl.when(jnp.logical_not(has_lo))
        def _():
            H[:, 0] = jnp.zeros((WSTEPS, 2, FD, 128), F32)
            NBR[0] = jnp.zeros((16, 256), jnp.int32)
            TR[:, 1:3] = jnp.zeros((WSTEPS, 2, 8, 256), F32)

        @pl.when(jnp.logical_not(has_hi))
        def _():
            H[:, 1] = jnp.zeros((WSTEPS, 2, FD, 128), F32)
            NBR[1] = jnp.zeros((16, 256), jnp.int32)
            TR[:, 3:5] = jnp.zeros((WSTEPS, 2, 8, 256), F32)

        def first_edges(c, carry):
            for copy in load(c):
                copy.wait()
            edges_out(0, c)
            return carry

        lax.fori_loop(0, CHUNKS, first_edges, 0)

        for d in range(DLOC):
            for h, hs in enumerate(halves):
                WD[d, :, hs] = wind[0, :, hs] * (sgn * COS[d]) + wind[1, :, hs] * (sgn * SIN[d])

        def growth(f, carry):
            slope = tab[1, f]
            sgs = tab[0, f] * sgn
            for d in range(DLOC):
                i = f * DLOC + d
                rows = pl.ds(pl.multiple_of(i * 8, 8), 8)
                for h, hs in enumerate(halves):
                    G[h, rows, :] = 1.0 + jnp.maximum(WD[d, :, hs] * slope - 0.05, 0.0)
                CNT[pl.ds(i, 1), :] = jnp.full((1, 128), sgs * SIN[d], F32)
            return carry

        lax.fori_loop(0, FREQS, growth, 0)

        @pl.when(has_lo)
        def _():
            neighbour(0).wait_recv()

        @pl.when(has_hi)
        def _():
            neighbour(1).wait_recv()

        edge_i = tuple(
            jnp.where(low_rows, NBR[1, 0:8, hs], NBR[0, 0:8, hs]) for hs in halves
        )
        edge_wet = tuple(x.astype(F32) for x in edge_i)
        edge_shift = tuple(
            jnp.where(low_rows, NBR[1, 8:16, hs], NBR[0, 8:16, hs]) for hs in halves
        )

        settle(QR, q_recv)
        fields = []
        for c in range(5):
            parts = []
            for h in range(2):
                acc = jnp.zeros((8, 128), F32)
                for k in range(16):
                    u = 16 * h + k
                    acc = jnp.where((lane >> 3) == (k + c) % 16, QR[pl.ds(8 * u, 8), :], acc)
                parts.append(pltpu.roll(acc, 128 - 8 * c, 1) if c else acc)
            fields.append(tuple(parts))
        left = tuple((256 - x) & 255 for x in shift)
        edge_left = tuple((256 - x) & 255 for x in edge_shift)
        u01 = tuple(0.1 * x for x in barrel(fields[0], left))
        v01 = tuple(0.1 * x for x in barrel(fields[1], left))

        def stiffness(level):
            depth = tuple(10.0 + 4.0 * x for x in level)
            return tuple(25.0 / (x * x) for x in depth)

        stiff = stiffness(barrel(fields[2], left))
        edge_v = tuple(0.1 * x for x in barrel(fields[3], edge_left))
        edge_stiff = stiffness(barrel(fields[4], edge_left))
        v_lo = tuple(jnp.broadcast_to(x[7:8], (8, 128)) for x in edge_v)
        v_hi = tuple(jnp.broadcast_to(x[0:1], (8, 128)) for x in edge_v)

        def sweep(n, r, edge_r, last):
            r_lo = tuple(jnp.broadcast_to(x[7:8], (8, 128)) for x in edge_r)
            r_hi = tuple(jnp.broadcast_to(x[0:1], (8, 128)) for x in edge_r)

            def chunk(c, sums):
                @pl.when(has_lo)
                def _():
                    halo(n, 0, c).wait_recv()

                @pl.when(has_hi)
                def _():
                    halo(n, 1, c).wait_recv()

                for k in range(RCH // 8):
                    rows = pl.ds(pl.multiple_of(c * RCH + 8 * k, 8), 8)
                    cn = CNT[rows, :]
                    for h in range(2):
                        H[n, 0, h, rows, :] = jnp.maximum((cn + v_lo[h]) * (r_lo[h] * H[n, 0, h, rows, :]), 0.0)
                        H[n, 1, h, rows, :] = jnp.minimum((cn + v_hi[h]) * (r_hi[h] * H[n, 1, h, rows, :]), 0.0)

                def band(fc, sums):
                    f = c * FCH + fc
                    sgs = tab[0, f] * sgn
                    slope = tab[1, f]
                    zero = jnp.zeros((8, 128), F32)
                    acc = [[zero, zero] for _ in range(5 if last else 1)]
                    for d in range(DLOC):
                        i = f * DLOC + d
                        rows = pl.ds(pl.multiple_of(i * 8, 8), 8)
                        ce = sgs * COS[d]
                        cn = sgs * SIN[d]
                        E = [r[h] * B[h, rows, :] for h in range(2)]
                        X = [(u01[h] + ce) * E[h] for h in range(2)]
                        Y = [(v01[h] + cn) * E[h] for h in range(2)]
                        west = from_left([jnp.maximum(x, 0.0) for x in X])
                        east = from_right([jnp.minimum(x, 0.0) for x in X])
                        for h, hs in enumerate(halves):
                            south = jnp.where(
                                first_row,
                                H[n, 0, h, pl.ds(i, 8, stride=0), :],
                                pltpu.roll(jnp.maximum(Y[h], 0.0), 1, 0),
                            )
                            north = jnp.where(
                                last_row,
                                H[n, 1, h, pl.ds(i, 8, stride=0), :],
                                pltpu.roll(jnp.minimum(Y[h], 0.0), 7, 0),
                            )
                            adv = ((E[h] - jnp.abs(X[h])) - jnp.abs(Y[h])) + (
                                (west[h] - east[h]) + (south - north)
                            )
                            new = adv * G[h, rows, :]
                            B[h, rows, :] = new
                            acc[0][h] += adv
                            if last:
                                push = adv * jnp.maximum(WD[d, :, hs] * slope - 0.05, 0.0)
                                acc[1][h] += push * COS[d]
                                acc[2][h] += push * SIN[d]
                                acc[3][h] += new * COS[d]
                                acc[4][h] += new * SIN[d]
                    weights = [tab[2, f], tab[3, f], tab[3, f], tab[4, f], tab[4, f]]
                    if last:
                        weights = weights[:1] + [w * sgn for w in weights[1:]]
                    return tuple(
                        tuple(total[h] + acc[q][h] * weights[q] for h in range(2)) for q, total in enumerate(sums)
                    )

                sums = lax.fori_loop(0, FCH, band, sums)
                if not last:
                    edges_out(n + 1, c)
                return sums

            zero = jnp.zeros((8, 128), F32)
            init = tuple((zero, zero) for _ in range(5 if last else 1))
            return lax.fori_loop(0, CHUNKS, chunk, init)

        def total_copies(n):
            return [
                (None, mesh_copy(TS.at[n], TR.at[n, 0], t_send.at[n, 0], t_recv.at[n, 0], {"spec": other})),
                (has_hi, mesh_copy(TS.at[n], TR.at[n, 1], t_send.at[n, 1], t_recv.at[n, 1], {"tile": hi_t})),
                (has_hi, mesh_copy(TS.at[n], TR.at[n, 2], t_send.at[n, 2], t_recv.at[n, 2], {"tile": hi_t, "spec": other})),
                (has_lo, mesh_copy(TS.at[n], TR.at[n, 3], t_send.at[n, 3], t_recv.at[n, 3], {"tile": lo_t})),
                (has_lo, mesh_copy(TS.at[n], TR.at[n, 4], t_send.at[n, 4], t_recv.at[n, 4], {"tile": lo_t, "spec": other})),
            ]

        def gated(condition, action):
            if condition is None:
                action()
            else:
                pl.when(condition)(action)

        def one_step(n, carry):
            r, edge_r = carry
            (total,) = sweep(n, r, edge_r, False)
            for h, hs in enumerate(halves):
                TS[n, :, hs] = total[h]
            copies = total_copies(n)
            for condition, copy in copies:
                gated(condition, copy.start)
            for (_, copy), condition in zip(copies, [None, has_lo, has_lo, has_hi, has_hi]):
                gated(condition, copy.wait_recv)
            new_r, new_edge = [], []
            for h, hs in enumerate(halves):
                full = total[h] + TR[n, 0, :, hs]
                new_r.append(wet[h] / (1.0 + stiff[h] * full))
                lower = TR[n, 1, :, hs] + TR[n, 2, :, hs]
                upper = TR[n, 3, :, hs] + TR[n, 4, :, hs]
                edge = jnp.where(low_rows, upper, lower)
                new_edge.append(edge_wet[h] / (1.0 + edge_stiff[h] * edge))
            return tuple(new_r), tuple(new_edge)

        r, edge_r = lax.fori_loop(0, WSTEPS - 1, one_step, (wet, edge_wet))
        n = WSTEPS - 1
        sums = sweep(n, r, edge_r, True)
        for q in range(5):
            put(BANDS, sums[q], slice(8 * q, 8 * q + 8))
        swap = mesh_copy(BANDS, BANDR, t_send.at[n, 0], t_recv.at[n, 0], {"spec": other})
        swap.start()
        swap.wait_recv()
        full = [tuple(sums[q][h] + BANDR[8 * q : 8 * q + 8, halves[h]] for h in range(2)) for q in range(5)]
        breaking = tuple(1.0 / (1.0 + stiff[h] * full[0][h]) for h in range(2))
        final = tuple(wet[h] * breaking[h] for h in range(2))
        bands = []
        for q in range(1, 5):
            scale = breaking if q < 3 else final
            bands.append(circular(barrel(tuple(scale[h] * full[q][h] for h in range(2)), shift), 1))
        bands = [tuple(pltpu.roll(x, 32 * f, 1) if f else x for x in field) for f, field in enumerate(bands)]
        for u in range(TILES):
            MSG2[pl.ds(8 * u, 8), :] = windows(bands, u)

        def send_bands(u, carry):
            to_ocean(MSG2, BR, f_send, f_recv, u).start()
            return carry

        lax.fori_loop(0, TILES, send_bands, 0)

        def store(c):
            rows = pl.ds(pl.multiple_of(c * RCH * 8, 8), RCH * 8)
            return [
                pltpu.make_async_copy(B.at[h, rows, :], out_w.at[rows, hs], load_sem.at[c, h])
                for h, hs in enumerate(halves)
            ]

        def finish(c, carry):
            def scale_f(i, carry):
                for d in range(DLOC):
                    rows = pl.ds(pl.multiple_of((c * RCH + i * DLOC + d) * 8, 8), 8)
                    for h in range(2):
                        B[h, rows, :] = B[h, rows, :] * final[h]
                return carry

            lax.fori_loop(0, FCH, scale_f, 0)
            for copy in store(c):
                copy.start()
            return carry

        lax.fori_loop(0, CHUNKS, finish, 0)
        A2[...] = jnp.zeros((2, 192, 128), F32)
        blanks = [pltpu.make_async_copy(A2.at[h], out_o.at[:, hs], out_sem.at[h]) for h, hs in enumerate(halves)]
        for copy in blanks:
            copy.start()

        def drain(c, carry):
            for copy in store(c):
                copy.wait()

            @pl.when(has_hi)
            def _():
                for n in range(WSTEPS):
                    halo(n, 0, c).wait_send()

            @pl.when(has_lo)
            def _():
                for n in range(WSTEPS):
                    halo(n, 1, c).wait_send()

            return carry

        lax.fori_loop(0, CHUNKS, drain, 0)
        for copy in blanks:
            copy.wait()
        for m in range(WSTEPS - 1):
            for condition, copy in total_copies(m):
                gated(condition, copy.wait_send)
        swap.wait_send()
        gated(has_hi, neighbour(0).wait_send)
        gated(has_lo, neighbour(1).wait_send)
        settle(MMSG, m_send)
        settle(MSG2, f_send)

    @pl.when(grp == 1)
    def circulation():
        top = (1 - sp).astype(F32)
        deep = sp.astype(F32)
        down = jnp.where(sp == 0, 1.0, math.exp(-1.0)).astype(F32)
        loads = [
            pltpu.make_async_copy(ocean_h.at[:, halves[0]], Q.at[0], small_sem.at[0]),
            pltpu.make_async_copy(ocean_h.at[:, halves[1]], Q.at[1], small_sem.at[1]),
            pltpu.make_async_copy(sea_h, sea, small_sem.at[2]),
        ]
        for copy in loads:
            copy.start()
        for copy in loads:
            copy.wait()
        for c in range(2):
            for h, hs in enumerate(halves):
                acc = jnp.zeros((8, 128), F32)
                for k in range(KLOC):
                    acc += Q[h, pl.ds((c * KLOC + k) * 8, 8), :] * float(_wgt[k])
                CS[pl.ds(8 * c, 8), hs] = acc * down
        part = mesh_copy(CS, CR, c_send, c_recv, {"spec": other})
        part.start()

        def edge(n, side):
            return mesh_copy(
                ES.at[n, side], EH.at[n, side], e_send.at[n, side], e_recv.at[n, side],
                {"tile": hi_t if side == 0 else lo_t},
            )

        def level(n):
            return mesh_copy(LS.at[n], LH.at[n], l_send.at[n], l_recv.at[n], {"spec": other})

        def rims_out(n, src):
            for c in range(3):
                for h, hs in enumerate(halves):
                    ES[n, 0, pl.ds(8 * c, 8), hs] = src[h, pl.ds(c * 64 + 7, 8, stride=8), :]
                    ES[n, 1, pl.ds(8 * c, 8), hs] = src[h, pl.ds(c * 64, 8, stride=8), :]
                    LS[n, pl.ds(8 * c, 8), hs] = jnp.where(
                        sp == 0, src[h, pl.ds(c * 64 + 56, 8), :], src[h, pl.ds(c * 64, 8), :]
                    )
            pl.when(has_hi)(edge(n, 0).start)
            pl.when(has_lo)(edge(n, 1).start)
            level(n).start()

        SX[...] = jnp.zeros((128, 256), F32)
        put(SX, pair(sea), slice(16, 24))
        part.wait_recv()
        for c in range(2):
            rows = pl.ds(8 * c, 8)
            SX[rows, :] = CS[rows, :] + CR[rows, :]
        beside = (lane & 7) < 4
        for c in range(2):
            src = tuple(SX[pl.ds(8 + 8 * c, 8), hs] for hs in halves)
            ahead, behind = circular(src, 120), circular(src, 8)
            ahead = (ahead[1], ahead[0])
            put(SX, tuple(jnp.where(beside, ahead[h], behind[h]) for h in range(2)), slice(24 + 8 * c, 32 + 8 * c))
        for h, hs in enumerate(halves):
            MSG[pl.ds(128 * h, 128), :] = pltpu.roll(SX[:, hs].T, tile * 8 % 128, 1)

        def to_wave(u):
            return mesh_copy(
                MSG.at[pl.ds(pl.multiple_of(u * 8, 8), 8), :],
                QR.at[pl.ds(pl.multiple_of(tile * 8, 8), 8), :],
                q_send, q_recv, {"grp": 0, "tile": u},
            )

        def send_q(u, carry):
            to_wave(u).start()
            return carry

        lax.fori_loop(0, TILES, send_q, 0)
        rims_out(0, Q)

        zbuf[...] = jnp.zeros((RCH * 8, 256), F32)

        def blank(c):
            rows = pl.ds(pl.multiple_of(c * RCH * 8, 8), RCH * 8)
            return pltpu.make_async_copy(zbuf, out_w.at[rows, :], load_sem.at[c, 0])

        def begin(c, carry):
            blank(c).start()
            return carry

        lax.fori_loop(0, CHUNKS, begin, 0)

        @pl.when(jnp.logical_not(has_lo))
        def _():
            EH[:, 0] = jnp.zeros((2, 24, 256), F32)

        @pl.when(jnp.logical_not(has_hi))
        def _():
            EH[:, 1] = jnp.zeros((2, 24, 256), F32)

        at_lo = jnp.where(has_lo, 1.0, 0.0).astype(F32)
        at_hi = jnp.where(has_hi, 1.0, 0.0).astype(F32)

        def arrived(buf, slots):
            for h in range(2):
                turned = buf[pl.ds(128 * h, 128), :].T
                BTS[pl.ds(0, 128), halves[h]] = turned
                BTS[pl.ds(128, 128), halves[h]] = turned
            out = []
            for f in range(slots):
                start = pl.multiple_of((8 * tile + 32 * f) % 128, 8)
                wide = BTS[pl.ds(start, 16), :]
                out.append(tuple((wide[0:8, hs], wide[1:9, hs], wide[2:10, hs]) for hs in halves))
            return out

        settle(MR, m_recv)
        (mask3,) = arrived(MR, 1)
        mask = tuple(x[1] for x in mask3)
        mask_lo = tuple(jnp.where(first_row, x[0] * at_lo, x[0]) for x in mask3)
        mask_hi = tuple(jnp.where(last_row, x[2] * at_hi, x[2]) for x in mask3)

        def lateral(x, lower, upper):
            left, right = from_left(x), from_right(x)
            return tuple(lower[h] + upper[h] + left[h] + right[h] - 4.0 * x[h] for h in range(2))

        def substep(n, src, dst):
            for c in range(3):
                for k in range(KLOC):
                    at = (c * KLOC + k) * 8
                    x = tuple(src[h, pl.ds(at, 8), :] for h in range(2))
                    row_at = 8 * c + k
                    lower = tuple(
                        jnp.where(first_row, EH[n, 0, row_at : row_at + 1, hs], pltpu.roll(x[h], 1, 0))
                        for h, hs in enumerate(halves)
                    )
                    upper = tuple(
                        jnp.where(last_row, EH[n, 1, row_at : row_at + 1, hs], pltpu.roll(x[h], 7, 0))
                        for h, hs in enumerate(halves)
                    )
                    side = lateral(x, lower, upper)
                    for h, hs in enumerate(halves):
                        if k > 0:
                            above = src[h, pl.ds(at - 8, 8), :]
                        else:
                            above = LH[n, pl.ds(8 * c, 8), hs] * deep
                        if k < KLOC - 1:
                            below = src[h, pl.ds(at + 8, 8), :]
                        else:
                            below = LH[n, pl.ds(8 * c, 8), hs] * top
                        value = x[h] + 0.1 * side[h] + 0.2 * (above + below - 2.0 * x[h])
                        if c == 0:
                            value = value + 0.1 * src[h, pl.ds(at + 64, 8), :]
                        if c == 1:
                            value = value - 0.1 * src[h, pl.ds(at - 64, 8), :]
                        dst[h, pl.ds(at, 8), :] = value * mask[h]

        def rims_in(n):
            pl.when(has_lo)(edge(n, 0).wait_recv)
            pl.when(has_hi)(edge(n, 1).wait_recv)
            level(n).wait_recv()

        rims_in(0)
        substep(0, Q, A1)
        rims_out(1, A1)
        rims_in(1)
        substep(1, A1, A2)

        settle(BR, f_recv)
        forced, spread = [], []
        for f, three in enumerate(arrived(BR, 4)):
            lower = tuple(three[h][0] * mask_lo[h] for h in range(2))
            own = tuple(three[h][1] * mask[h] for h in range(2))
            upper = tuple(three[h][2] * mask_hi[h] for h in range(2))
            forced.append(own)
            spread.append(lateral(own, lower, upper))
        for k in range(KLOC):
            near, far = math.exp(0.125), math.exp(-0.125)
            prof = float(_prof[k]) * down
            above = near if k > 0 else near * deep
            below = far if k < KLOC - 1 else far * top
            stay = prof * (1.0 + 0.2 * (above + below - 2.0))
            for h, hs in enumerate(halves):
                east = (0.1 * prof) * forced[3][h]
                north = (-0.1 * prof) * forced[2][h]
                d_east = (0.1 * stay) * forced[3][h] + (0.01 * prof) * spread[3][h]
                d_north = (-0.1 * stay) * forced[2][h] - (0.01 * prof) * spread[2][h]
                if k == 0:
                    east = east + top * forced[0][h]
                    north = north + top * forced[1][h]
                    d_east = d_east + top * (0.6 * forced[0][h] + 0.1 * spread[0][h])
                    d_north = d_north + top * (0.6 * forced[1][h] + 0.1 * spread[1][h])
                if k == 1:
                    d_east = d_east + (0.2 * top) * forced[0][h]
                    d_north = d_north + (0.2 * top) * forced[1][h]
                A2[h, pl.ds(8 * k, 8), :] += mask[h] * (d_east + 0.1 * north) + east
                A2[h, pl.ds(64 + 8 * k, 8), :] += mask[h] * (d_north - 0.1 * east) + north
        results = [pltpu.make_async_copy(A2.at[h], out_o.at[:, hs], out_sem.at[h]) for h, hs in enumerate(halves)]
        for copy in results:
            copy.start()

        def drain(c, carry):
            blank(c).wait()
            return carry

        lax.fori_loop(0, CHUNKS, drain, 0)
        part.wait_send()
        for n in range(2):
            pl.when(has_hi)(edge(n, 0).wait_send)
            pl.when(has_lo)(edge(n, 1).wait_send)
            level(n).wait_send()
        settle(MSG, q_send)
        for copy in results:
            copy.wait()


def body(spectrum, wind, land_mask, intersection, ocean_state, sea_level):
    v = lambda *shape, dtype=F32: pltpu.VMEM(shape, dtype)
    dma = lambda *shape: pltpu.SemaphoreType.DMA(shape) if shape else pltpu.SemaphoreType.DMA
    anywhere = pl.BlockSpec(memory_space=pl.ANY)
    scratch = [
        v(2, FD * 8, 128), v(2, FD * 8, 128), v(DLOC, 8, 256), v(FD, 128),
        v(WSTEPS, 2, 2, FD, 128), v(WSTEPS, 2, 2, FD, 128),
        v(2, 8, 256), v(8, 256, dtype=jnp.int32), v(8, 256, dtype=jnp.int32),
        v(16, 256, dtype=jnp.int32), v(2, 16, 256, dtype=jnp.int32),
        v(256, 128), v(WSTEPS, 8, 256), v(WSTEPS, 5, 8, 256), v(40, 256), v(40, 256), v(256, 128), v(256, 128),
        v(2, 192, 128), v(2, 192, 128), v(2, 192, 128), v(8, 256), v(16, 256), v(16, 256), v(128, 256),
        v(256, 128), v(256, 128), v(256, 128), v(256, 256),
        v(2, 2, 24, 256), v(2, 2, 24, 256), v(2, 24, 256), v(2, 24, 256), v(RCH * 8, 256),
        dma(CHUNKS, 2), dma(3), dma(WSTEPS, 2, CHUNKS), dma(WSTEPS, 2, CHUNKS), dma(WSTEPS, 5), dma(WSTEPS, 5),
        dma(2), dma(2), dma(), dma(), dma(), dma(), dma(), dma(), dma(), dma(),
        dma(2, 2), dma(2, 2), dma(2), dma(2), dma(2),
    ]
    waves, ocean = pl.pallas_call(
        kernel,
        out_shape=(
            jax.ShapeDtypeStruct((FD * 8, 256), F32),
            jax.ShapeDtypeStruct((192, 256), F32),
        ),
        in_specs=[pl.BlockSpec(memory_space=pltpu.SMEM)] + [anywhere] * 6,
        out_specs=(anywhere, anywhere),
        scratch_shapes=scratch,
        compiler_params=pltpu.CompilerParams(has_side_effects=True, vmem_limit_bytes=48 << 20),
    )(
        jnp.asarray(TABLE),
        spectrum.reshape(FD * 8, 256),
        wind,
        land_mask,
        intersection,
        ocean_state.reshape(192, 256),
        sea_level.reshape(8, 256),
    )
    return waves.reshape(spectrum.shape), ocean.reshape(ocean_state.shape)


def solution(mesh):
    return jax.shard_map(
        body,
        mesh=mesh,
        in_specs=(
            P("grp", None, "spec", "tile", None),
            P(None, "tile", None),
            P("tile", None),
            P("tile", None),
            P("grp", None, "spec", "tile", None),
            P("grp", "tile", None),
        ),
        out_specs=(P("grp", None, "spec", "tile", None), P("grp", None, "spec", "tile", None)),
        check_vma=False,
    )
```

```python
import math

import jax
import jax.numpy as jnp
import numpy as np
from jax import lax
from jax.experimental import pallas as pl
from jax.experimental.pallas import tpu as pltpu
from jax.sharding import PartitionSpec as P

FREQS = 32
DIRS = 36
LEVELS = 16
WSTEPS = 4
TILES = 32
DLOC = 18
KLOC = 8
FD = FREQS * DLOC
CHUNKS = 8
FCH = FREQS // CHUNKS
RCH = FCH * DLOC
F32 = jnp.float32

_freq = 0.04 * 1.1 ** np.arange(FREQS)
_cel = 1.56 / _freq
_gs = 0.4 * 1.1 ** (-np.arange(FREQS, dtype=np.float64))
_bw = 0.1 * _freq * (2.0 * math.pi / DIRS)
TABLE = np.stack([_gs, 0.05 / _cel, _bw, 5.0 * _bw / _cel, 20.0 * _bw * _freq**3]).astype(np.float32)
_ang = 2.0 * math.pi * (np.arange(DIRS) + 0.5) / DIRS
COS = [float(np.float32(x)) for x in np.cos(_ang)[:DLOC]]
SIN = [float(np.float32(x)) for x in np.sin(_ang)[:DLOC]]
DIR_ORDER = [d for k in range(DLOC // 2) for d in (k, DLOC - 1 - k)]
_prof = np.exp(-2.0 * (np.arange(LEVELS) + 0.5) / LEVELS)
_wgt = _prof / _prof.sum()


def mesh_copy(src, dst, send, recv, where):
    return pltpu.make_async_remote_copy(
        src_ref=src,
        dst_ref=dst,
        send_sem=send,
        recv_sem=recv,
        device_id=where,
        device_id_type=pl.DeviceIdType.MESH,
    )


def settle(buf, sem):
    pltpu.make_async_copy(buf, buf, sem).wait()


def kernel(
    spec_h, wind_h, land_h, inter_h, ocean_h, sea_h, out_w, out_o,
    tab, B, G, WD, CNT, H, S, wind, land, inter, NBS, NBR, QR, TS, TR, BANDS, BANDR, MSG2, MMSG,
    Q, A1, A2, sea, CS, CR, SX, MSG, MR, BR, BTS, ES, EH, LS, LH, zbuf,
    load_sem, small_sem, h_send, h_recv, t_send, t_recv, nb_send, nb_recv,
    q_send, q_recv, m_send, m_recv, f_send, f_recv, c_send, c_recv, e_send, e_recv, l_send, l_recv, out_sem,
):
    grp = lax.axis_index("grp")
    tile = lax.axis_index("tile")
    sp = lax.axis_index("spec")
    other = 1 - sp
    sgn = (1 - 2 * sp).astype(F32)
    has_lo = tile > 0
    has_hi = tile < TILES - 1
    lo_t = jnp.maximum(tile - 1, 0)
    hi_t = jnp.minimum(tile + 1, TILES - 1)
    lane = lax.broadcasted_iota(jnp.int32, (8, 128), 1)
    row = lax.broadcasted_iota(jnp.int32, (8, 128), 0)
    first_lane, last_lane = lane == 0, lane == 127
    first_row, last_row = row == 0, row == 7
    low_rows = row < 4
    halves = (slice(0, 128), slice(128, 256))

    def from_left(x):
        a, b = pltpu.roll(x[0], 1, 1), pltpu.roll(x[1], 1, 1)
        return jnp.where(first_lane, 0.0, a), jnp.where(first_lane, a, b)

    def from_right(x):
        a, b = pltpu.roll(x[0], 127, 1), pltpu.roll(x[1], 127, 1)
        return jnp.where(last_lane, b, a), jnp.where(last_lane, 0.0, b)

    def circular(x, shift):
        a, b = pltpu.roll(x[0], shift, 1), pltpu.roll(x[1], shift, 1)
        m = lane < shift
        return jnp.where(m, b, a), jnp.where(m, a, b)

    def barrel(x, amount):
        for bit in range(8):
            moved = circular(x, 1 << bit) if bit < 7 else (x[1], x[0])
            x = tuple(jnp.where((amount[h] & (1 << bit)) != 0, moved[h], x[h]) for h in range(2))
        return x

    def pair(ref, *lead):
        return tuple(ref[(*lead, slice(None), hs)] for hs in halves)

    def put(ref, value, rows):
        for h in range(2):
            ref[rows, halves[h]] = value[h]

    barrier = pltpu.get_barrier_semaphore()

    def greet(where):
        pl.semaphore_signal(barrier, 1, device_id=where, device_id_type=pl.DeviceIdType.MESH)

    greet({"spec": other})

    @pl.when(has_lo)
    def _():
        greet({"tile": lo_t})
        greet({"tile": lo_t, "spec": other})

    @pl.when(has_hi)
    def _():
        greet({"tile": hi_t})
        greet({"tile": hi_t, "spec": other})

    def greet_across(u, carry):
        greet({"grp": 1 - grp, "tile": u})
        return carry

    lax.fori_loop(0, TILES, greet_across, 0)
    beside = jnp.where(has_lo, 2, 0) + jnp.where(has_hi, 2, 0)

    def everyone_in():
        pl.semaphore_wait(barrier, TILES + 1 + beside)

    @pl.when(grp == 0)
    def wave():
        def load(c):
            rows = pl.ds(pl.multiple_of(c * RCH * 8, 8), RCH * 8)
            return [
                pltpu.make_async_copy(spec_h.at[rows, hs], B.at[h, rows, :], load_sem.at[c, h])
                for h, hs in enumerate(halves)
            ]

        smalls = [
            pltpu.make_async_copy(wind_h, wind, small_sem.at[0]),
            pltpu.make_async_copy(land_h, land, small_sem.at[1]),
            pltpu.make_async_copy(inter_h, inter, small_sem.at[2]),
        ]
        for copy in smalls:
            copy.start()
        for q in range(TABLE.shape[0]):
            for f in range(FREQS):
                tab[q, f] = float(TABLE[q, f])

        def begin(c, carry):
            for copy in load(c):
                copy.start()
            return carry

        lax.fori_loop(0, CHUNKS, begin, 0)

        def halo(n, side, c):
            rows = pl.ds(pl.multiple_of(c * RCH, 8), RCH)
            return mesh_copy(
                S.at[n, side, :, rows, :], H.at[n, side, :, rows, :], h_send.at[n, side, c], h_recv.at[n, side, c],
                {"tile": hi_t if side == 0 else lo_t},
            )

        def edges_out(n, c):
            for k in range(RCH // 8):
                at = c * RCH + 8 * k
                rows = pl.ds(pl.multiple_of(at, 8), 8)
                for h in range(2):
                    S[n, 0, h, rows, :] = B[h, pl.ds(at * 8 + 7, 8, stride=8), :]
                    S[n, 1, h, rows, :] = B[h, pl.ds(at * 8, 8, stride=8), :]

            @pl.when(has_hi)
            def _():
                halo(n, 0, c).start()

            @pl.when(has_lo)
            def _():
                halo(n, 1, c).start()

        for copy in smalls:
            copy.wait()
        wet_i = pair(land)
        wet = tuple(x.astype(F32) for x in wet_i)
        shift = tuple((x - lane - 128 * h) & 255 for h, x in enumerate(pair(inter)))
        put(NBS, wet_i, slice(0, 8))
        put(NBS, shift, slice(8, 16))

        def neighbour(side):
            return mesh_copy(
                NBS, NBR.at[side], nb_send.at[side], nb_recv.at[side],
                {"tile": hi_t if side == 0 else lo_t},
            )

        everyone_in()

        @pl.when(has_hi)
        def _():
            neighbour(0).start()

        @pl.when(has_lo)
        def _():
            neighbour(1).start()

        wet_back = circular(barrel(wet, shift), 1)

        def windows(fields, u):
            acc = jnp.zeros((8, 128), F32)
            for f, field in enumerate(fields):
                start = (8 * u + 32 * f) % 128
                offset = (lane - start) & 127
                inside = offset < 10
                base = (8 * u) // 128
                p = 8 * u + offset
                value = field[base]
                if 8 * u % 128 + 10 > 128:
                    turned = (lane - 32 * f) & 127
                    value = jnp.where(turned < 16, field[1 - base], value)
                acc = jnp.where(inside, value, acc)
            return acc

        for u in range(TILES):
            MMSG[pl.ds(8 * u, 8), :] = windows([wet_back], u)

        def to_ocean(src, dst, send, recv, u):
            return mesh_copy(
                src.at[pl.ds(pl.multiple_of(u * 8, 8), 8), :],
                dst.at[pl.ds(pl.multiple_of(tile * 8, 8), 8), :],
                send, recv, {"grp": 1, "tile": u},
            )

        def send_mask(u, carry):
            to_ocean(MMSG, MR, m_send, m_recv, u).start()
            return carry

        lax.fori_loop(0, TILES, send_mask, 0)

        @pl.when(jnp.logical_not(has_lo))
        def _():
            H[:, 0] = jnp.zeros((WSTEPS, 2, FD, 128), F32)
            NBR[0] = jnp.zeros((16, 256), jnp.int32)
            TR[:, 1:3] = jnp.zeros((WSTEPS, 2, 8, 256), F32)

        @pl.when(jnp.logical_not(has_hi))
        def _():
            H[:, 1] = jnp.zeros((WSTEPS, 2, FD, 128), F32)
            NBR[1] = jnp.zeros((16, 256), jnp.int32)
            TR[:, 3:5] = jnp.zeros((WSTEPS, 2, 8, 256), F32)

        def first_edges(c, carry):
            for copy in load(c):
                copy.wait()
            edges_out(0, c)
            return carry

        lax.fori_loop(0, CHUNKS, first_edges, 0)

        for d in range(DLOC):
            for h, hs in enumerate(halves):
                WD[d, :, hs] = wind[0, :, hs] * (sgn * COS[d]) + wind[1, :, hs] * (sgn * SIN[d])

        def growth(f, carry):
            slope = tab[1, f]
            sgs = tab[0, f] * sgn
            for d in range(DLOC):
                i = f * DLOC + d
                rows = pl.ds(pl.multiple_of(i * 8, 8), 8)
                for h, hs in enumerate(halves):
                    G[h, rows, :] = 1.0 + jnp.maximum(WD[d, :, hs] * slope - 0.05, 0.0)
                CNT[pl.ds(i, 1), :] = jnp.full((1, 128), sgs * SIN[d], F32)
            return carry

        lax.fori_loop(0, FREQS, growth, 0)

        @pl.when(has_lo)
        def _():
            neighbour(0).wait_recv()

        @pl.when(has_hi)
        def _():
            neighbour(1).wait_recv()

        edge_i = tuple(
            jnp.where(low_rows, NBR[1, 0:8, hs], NBR[0, 0:8, hs]) for hs in halves
        )
        edge_wet = tuple(x.astype(F32) for x in edge_i)
        edge_shift = tuple(
            jnp.where(low_rows, NBR[1, 8:16, hs], NBR[0, 8:16, hs]) for hs in halves
        )

        settle(QR, q_recv)
        fields = []
        for c in range(5):
            parts = []
            for h in range(2):
                acc = jnp.zeros((8, 128), F32)
                for k in range(16):
                    u = 16 * h + k
                    acc = jnp.where((lane >> 3) == (k + c) % 16, QR[pl.ds(8 * u, 8), :], acc)
                parts.append(pltpu.roll(acc, 128 - 8 * c, 1) if c else acc)
            fields.append(tuple(parts))
        left = tuple((256 - x) & 255 for x in shift)
        edge_left = tuple((256 - x) & 255 for x in edge_shift)
        u01 = tuple(0.1 * x for x in barrel(fields[0], left))
        v01 = tuple(0.1 * x for x in barrel(fields[1], left))

        def stiffness(level):
            depth = tuple(10.0 + 4.0 * x for x in level)
            return tuple(25.0 / (x * x) for x in depth)

        stiff = stiffness(barrel(fields[2], left))
        edge_v = tuple(0.1 * x for x in barrel(fields[3], edge_left))
        edge_stiff = stiffness(barrel(fields[4], edge_left))
        v_lo = tuple(jnp.broadcast_to(x[7:8], (8, 128)) for x in edge_v)
        v_hi = tuple(jnp.broadcast_to(x[0:1], (8, 128)) for x in edge_v)

        def sweep(n, r, edge_r, last):
            r_lo = tuple(jnp.broadcast_to(x[7:8], (8, 128)) for x in edge_r)
            r_hi = tuple(jnp.broadcast_to(x[0:1], (8, 128)) for x in edge_r)

            def chunk(c, sums):
                @pl.when(has_lo)
                def _():
                    halo(n, 0, c).wait_recv()

                @pl.when(has_hi)
                def _():
                    halo(n, 1, c).wait_recv()

                for k in range(RCH // 8):
                    rows = pl.ds(pl.multiple_of(c * RCH + 8 * k, 8), 8)
                    cn = CNT[rows, :]
                    for h in range(2):
                        H[n, 0, h, rows, :] = jnp.maximum((cn + v_lo[h]) * (r_lo[h] * H[n, 0, h, rows, :]), 0.0)
                        H[n, 1, h, rows, :] = jnp.minimum((cn + v_hi[h]) * (r_hi[h] * H[n, 1, h, rows, :]), 0.0)

                def band(fc, sums):
                    f = c * FCH + fc
                    sgs = tab[0, f] * sgn
                    zero = jnp.zeros((8, 128), F32)
                    acc = [[zero, zero] for _ in range(5 if last else 1)]
                    half_way = {}
                    for d in (DIR_ORDER if last else range(DLOC)):
                        i = f * DLOC + d
                        rows = pl.ds(pl.multiple_of(i * 8, 8), 8)
                        ce = sgs * COS[d]
                        cn = sgs * SIN[d]
                        E = [r[h] * B[h, rows, :] for h in range(2)]
                        X = [(u01[h] + ce) * E[h] for h in range(2)]
                        Y = [(v01[h] + cn) * E[h] for h in range(2)]
                        west = from_left([jnp.maximum(x, 0.0) for x in X])
                        east = from_right([jnp.minimum(x, 0.0) for x in X])
                        for h, hs in enumerate(halves):
                            south = jnp.where(
                                first_row,
                                H[n, 0, h, pl.ds(i, 8, stride=0), :],
                                pltpu.roll(jnp.maximum(Y[h], 0.0), 1, 0),
                            )
                            north = jnp.where(
                                last_row,
                                H[n, 1, h, pl.ds(i, 8, stride=0), :],
                                pltpu.roll(jnp.minimum(Y[h], 0.0), 7, 0),
                            )
                            adv = ((E[h] - jnp.abs(X[h])) - jnp.abs(Y[h])) + (
                                (west[h] - east[h]) + (south - north)
                            )
                            new = adv * G[h, rows, :]
                            B[h, rows, :] = new
                            acc[0][h] += adv
                            if last:
                                mine = (new - adv, new)
                                if h not in half_way:
                                    half_way[h] = mine
                                    continue
                                for q, (a, b) in enumerate(zip(half_way.pop(h), mine)):
                                    acc[1 + 2 * q][h] += (a - b) * COS[DLOC - 1 - d]
                                    acc[2 + 2 * q][h] += (a + b) * SIN[d]
                    weights = [tab[2, f], tab[3, f], tab[3, f], tab[4, f], tab[4, f]]
                    if last:
                        weights = weights[:1] + [w * sgn for w in weights[1:]]
                    return tuple(
                        tuple(total[h] + acc[q][h] * weights[q] for h in range(2)) for q, total in enumerate(sums)
                    )

                sums = lax.fori_loop(0, FCH, band, sums)
                if not last:
                    edges_out(n + 1, c)
                return sums

            zero = jnp.zeros((8, 128), F32)
            init = tuple((zero, zero) for _ in range(5 if last else 1))
            return lax.fori_loop(0, CHUNKS, chunk, init)

        def total_copies(n):
            return [
                (None, mesh_copy(TS.at[n], TR.at[n, 0], t_send.at[n, 0], t_recv.at[n, 0], {"spec": other})),
                (has_hi, mesh_copy(TS.at[n], TR.at[n, 1], t_send.at[n, 1], t_recv.at[n, 1], {"tile": hi_t})),
                (has_hi, mesh_copy(TS.at[n], TR.at[n, 2], t_send.at[n, 2], t_recv.at[n, 2], {"tile": hi_t, "spec": other})),
                (has_lo, mesh_copy(TS.at[n], TR.at[n, 3], t_send.at[n, 3], t_recv.at[n, 3], {"tile": lo_t})),
                (has_lo, mesh_copy(TS.at[n], TR.at[n, 4], t_send.at[n, 4], t_recv.at[n, 4], {"tile": lo_t, "spec": other})),
            ]

        def gated(condition, action):
            if condition is None:
                action()
            else:
                pl.when(condition)(action)

        def one_step(n, carry):
            r, edge_r = carry
            (total,) = sweep(n, r, edge_r, False)
            for h, hs in enumerate(halves):
                TS[n, :, hs] = total[h]
            copies = total_copies(n)
            for condition, copy in copies:
                gated(condition, copy.start)
            for (_, copy), condition in zip(copies, [None, has_lo, has_lo, has_hi, has_hi]):
                gated(condition, copy.wait_recv)
            new_r, new_edge = [], []
            for h, hs in enumerate(halves):
                full = total[h] + TR[n, 0, :, hs]
                new_r.append(wet[h] / (1.0 + stiff[h] * full))
                lower = TR[n, 1, :, hs] + TR[n, 2, :, hs]
                upper = TR[n, 3, :, hs] + TR[n, 4, :, hs]
                edge = jnp.where(low_rows, upper, lower)
                new_edge.append(edge_wet[h] / (1.0 + edge_stiff[h] * edge))
            return tuple(new_r), tuple(new_edge)

        r, edge_r = lax.fori_loop(0, WSTEPS - 1, one_step, (wet, edge_wet))
        n = WSTEPS - 1
        sums = sweep(n, r, edge_r, True)
        for q in range(5):
            put(BANDS, sums[q], slice(8 * q, 8 * q + 8))
        swap = mesh_copy(BANDS, BANDR, t_send.at[n, 0], t_recv.at[n, 0], {"spec": other})
        swap.start()
        swap.wait_recv()
        full = [tuple(sums[q][h] + BANDR[8 * q : 8 * q + 8, halves[h]] for h in range(2)) for q in range(5)]
        breaking = tuple(1.0 / (1.0 + stiff[h] * full[0][h]) for h in range(2))
        final = tuple(wet[h] * breaking[h] for h in range(2))
        bands = []
        for q in range(1, 5):
            scale = breaking if q < 3 else final
            bands.append(circular(barrel(tuple(scale[h] * full[q][h] for h in range(2)), shift), 1))
        bands = [tuple(pltpu.roll(x, 32 * f, 1) if f else x for x in field) for f, field in enumerate(bands)]
        for u in range(TILES):
            MSG2[pl.ds(8 * u, 8), :] = windows(bands, u)

        def send_bands(u, carry):
            to_ocean(MSG2, BR, f_send, f_recv, u).start()
            return carry

        lax.fori_loop(0, TILES, send_bands, 0)

        def store(c):
            rows = pl.ds(pl.multiple_of(c * RCH * 8, 8), RCH * 8)
            return [
                pltpu.make_async_copy(B.at[h, rows, :], out_w.at[rows, hs], load_sem.at[c, h])
                for h, hs in enumerate(halves)
            ]

        def finish(c, carry):
            def scale_f(i, carry):
                for d in range(DLOC):
                    rows = pl.ds(pl.multiple_of((c * RCH + i * DLOC + d) * 8, 8), 8)
                    for h in range(2):
                        B[h, rows, :] = B[h, rows, :] * final[h]
                return carry

            lax.fori_loop(0, FCH, scale_f, 0)
            for copy in store(c):
                copy.start()
            return carry

        lax.fori_loop(0, CHUNKS, finish, 0)
        A2[...] = jnp.zeros((2, 192, 128), F32)
        blanks = [pltpu.make_async_copy(A2.at[h], out_o.at[:, hs], out_sem.at[h]) for h, hs in enumerate(halves)]
        for copy in blanks:
            copy.start()

        def drain(c, carry):
            for copy in store(c):
                copy.wait()

            @pl.when(has_hi)
            def _():
                for n in range(WSTEPS):
                    halo(n, 0, c).wait_send()

            @pl.when(has_lo)
            def _():
                for n in range(WSTEPS):
                    halo(n, 1, c).wait_send()

            return carry

        lax.fori_loop(0, CHUNKS, drain, 0)
        for copy in blanks:
            copy.wait()
        for m in range(WSTEPS - 1):
            for condition, copy in total_copies(m):
                gated(condition, copy.wait_send)
        swap.wait_send()
        gated(has_hi, neighbour(0).wait_send)
        gated(has_lo, neighbour(1).wait_send)
        settle(MMSG, m_send)
        settle(MSG2, f_send)

    @pl.when(grp == 1)
    def circulation():
        top = (1 - sp).astype(F32)
        deep = sp.astype(F32)
        down = jnp.where(sp == 0, 1.0, math.exp(-1.0)).astype(F32)
        loads = [
            pltpu.make_async_copy(ocean_h.at[:, halves[0]], Q.at[0], small_sem.at[0]),
            pltpu.make_async_copy(ocean_h.at[:, halves[1]], Q.at[1], small_sem.at[1]),
            pltpu.make_async_copy(sea_h, sea, small_sem.at[2]),
        ]
        for copy in loads:
            copy.start()
        for copy in loads:
            copy.wait()
        for c in range(2):
            for h, hs in enumerate(halves):
                acc = jnp.zeros((8, 128), F32)
                for k in range(KLOC):
                    acc += Q[h, pl.ds((c * KLOC + k) * 8, 8), :] * float(_wgt[k])
                CS[pl.ds(8 * c, 8), hs] = acc * down
        everyone_in()
        part = mesh_copy(CS, CR, c_send, c_recv, {"spec": other})
        part.start()

        def edge(n, side):
            return mesh_copy(
                ES.at[n, side], EH.at[n, side], e_send.at[n, side], e_recv.at[n, side],
                {"tile": hi_t if side == 0 else lo_t},
            )

        def level(n):
            return mesh_copy(LS.at[n], LH.at[n], l_send.at[n], l_recv.at[n], {"spec": other})

        def rims_out(n, src):
            for c in range(3):
                for h, hs in enumerate(halves):
                    ES[n, 0, pl.ds(8 * c, 8), hs] = src[h, pl.ds(c * 64 + 7, 8, stride=8), :]
                    ES[n, 1, pl.ds(8 * c, 8), hs] = src[h, pl.ds(c * 64, 8, stride=8), :]
                    LS[n, pl.ds(8 * c, 8), hs] = jnp.where(
                        sp == 0, src[h, pl.ds(c * 64 + 56, 8), :], src[h, pl.ds(c * 64, 8), :]
                    )
            pl.when(has_hi)(edge(n, 0).start)
            pl.when(has_lo)(edge(n, 1).start)
            level(n).start()

        SX[...] = jnp.zeros((128, 256), F32)
        put(SX, pair(sea), slice(16, 24))
        part.wait_recv()
        for c in range(2):
            rows = pl.ds(8 * c, 8)
            SX[rows, :] = CS[rows, :] + CR[rows, :]
        ahead_rows = (lane & 7) < 4
        for c in range(2):
            src = tuple(SX[pl.ds(8 + 8 * c, 8), hs] for hs in halves)
            ahead, behind = circular(src, 120), circular(src, 8)
            ahead = (ahead[1], ahead[0])
            put(SX, tuple(jnp.where(ahead_rows, ahead[h], behind[h]) for h in range(2)), slice(24 + 8 * c, 32 + 8 * c))
        for h, hs in enumerate(halves):
            MSG[pl.ds(128 * h, 128), :] = pltpu.roll(SX[:, hs].T, tile * 8 % 128, 1)

        def to_wave(u):
            return mesh_copy(
                MSG.at[pl.ds(pl.multiple_of(u * 8, 8), 8), :],
                QR.at[pl.ds(pl.multiple_of(tile * 8, 8), 8), :],
                q_send, q_recv, {"grp": 0, "tile": u},
            )

        def send_q(u, carry):
            to_wave(u).start()
            return carry

        lax.fori_loop(0, TILES, send_q, 0)
        rims_out(0, Q)

        zbuf[...] = jnp.zeros((RCH * 8, 256), F32)

        def blank(c):
            rows = pl.ds(pl.multiple_of(c * RCH * 8, 8), RCH * 8)
            return pltpu.make_async_copy(zbuf, out_w.at[rows, :], load_sem.at[c, 0])

        def begin(c, carry):
            blank(c).start()
            return carry

        lax.fori_loop(0, CHUNKS, begin, 0)

        @pl.when(jnp.logical_not(has_lo))
        def _():
            EH[:, 0] = jnp.zeros((2, 24, 256), F32)

        @pl.when(jnp.logical_not(has_hi))
        def _():
            EH[:, 1] = jnp.zeros((2, 24, 256), F32)

        at_lo = jnp.where(has_lo, 1.0, 0.0).astype(F32)
        at_hi = jnp.where(has_hi, 1.0, 0.0).astype(F32)

        def arrived(buf, slots):
            for h in range(2):
                turned = buf[pl.ds(128 * h, 128), :].T
                BTS[pl.ds(0, 128), halves[h]] = turned
                BTS[pl.ds(128, 128), halves[h]] = turned
            out = []
            for f in range(slots):
                start = pl.multiple_of((8 * tile + 32 * f) % 128, 8)
                wide = BTS[pl.ds(start, 16), :]
                out.append(tuple((wide[0:8, hs], wide[1:9, hs], wide[2:10, hs]) for hs in halves))
            return out

        settle(MR, m_recv)
        (mask3,) = arrived(MR, 1)
        mask = tuple(x[1] for x in mask3)
        mask_lo = tuple(jnp.where(first_row, x[0] * at_lo, x[0]) for x in mask3)
        mask_hi = tuple(jnp.where(last_row, x[2] * at_hi, x[2]) for x in mask3)

        def lateral(x, lower, upper):
            left, right = from_left(x), from_right(x)
            return tuple(lower[h] + upper[h] + left[h] + right[h] - 4.0 * x[h] for h in range(2))

        def substep(n, src, dst):
            for c in range(3):
                for k in range(KLOC):
                    at = (c * KLOC + k) * 8
                    x = tuple(src[h, pl.ds(at, 8), :] for h in range(2))
                    row_at = 8 * c + k
                    lower = tuple(
                        jnp.where(first_row, EH[n, 0, row_at : row_at + 1, hs], pltpu.roll(x[h], 1, 0))
                        for h, hs in enumerate(halves)
                    )
                    upper = tuple(
                        jnp.where(last_row, EH[n, 1, row_at : row_at + 1, hs], pltpu.roll(x[h], 7, 0))
                        for h, hs in enumerate(halves)
                    )
                    side = lateral(x, lower, upper)
                    for h, hs in enumerate(halves):
                        if k > 0:
                            above = src[h, pl.ds(at - 8, 8), :]
                        else:
                            above = LH[n, pl.ds(8 * c, 8), hs] * deep
                        if k < KLOC - 1:
                            below = src[h, pl.ds(at + 8, 8), :]
                        else:
                            below = LH[n, pl.ds(8 * c, 8), hs] * top
                        value = x[h] + 0.1 * side[h] + 0.2 * (above + below - 2.0 * x[h])
                        if c == 0:
                            value = value + 0.1 * src[h, pl.ds(at + 64, 8), :]
                        if c == 1:
                            value = value - 0.1 * src[h, pl.ds(at - 64, 8), :]
                        dst[h, pl.ds(at, 8), :] = value * mask[h]

        def rims_in(n):
            pl.when(has_lo)(edge(n, 0).wait_recv)
            pl.when(has_hi)(edge(n, 1).wait_recv)
            level(n).wait_recv()

        rims_in(0)
        substep(0, Q, A1)
        rims_out(1, A1)
        rims_in(1)
        substep(1, A1, A2)

        settle(BR, f_recv)
        forced, spread = [], []
        for f, three in enumerate(arrived(BR, 4)):
            lower = tuple(three[h][0] * mask_lo[h] for h in range(2))
            own = tuple(three[h][1] * mask[h] for h in range(2))
            upper = tuple(three[h][2] * mask_hi[h] for h in range(2))
            forced.append(own)
            spread.append(lateral(own, lower, upper))
        for k in range(KLOC):
            near, far = math.exp(0.125), math.exp(-0.125)
            prof = float(_prof[k]) * down
            above = near if k > 0 else near * deep
            below = far if k < KLOC - 1 else far * top
            stay = prof * (1.0 + 0.2 * (above + below - 2.0))
            for h, hs in enumerate(halves):
                east = (0.1 * prof) * forced[3][h]
                north = (-0.1 * prof) * forced[2][h]
                d_east = (0.1 * stay) * forced[3][h] + (0.01 * prof) * spread[3][h]
                d_north = (-0.1 * stay) * forced[2][h] - (0.01 * prof) * spread[2][h]
                if k == 0:
                    east = east + top * forced[0][h]
                    north = north + top * forced[1][h]
                    d_east = d_east + top * (0.6 * forced[0][h] + 0.1 * spread[0][h])
                    d_north = d_north + top * (0.6 * forced[1][h] + 0.1 * spread[1][h])
                if k == 1:
                    d_east = d_east + (0.2 * top) * forced[0][h]
                    d_north = d_north + (0.2 * top) * forced[1][h]
                A2[h, pl.ds(8 * k, 8), :] += mask[h] * (d_east + 0.1 * north) + east
                A2[h, pl.ds(64 + 8 * k, 8), :] += mask[h] * (d_north - 0.1 * east) + north
        results = [pltpu.make_async_copy(A2.at[h], out_o.at[:, hs], out_sem.at[h]) for h, hs in enumerate(halves)]
        for copy in results:
            copy.start()

        def drain(c, carry):
            blank(c).wait()
            return carry

        lax.fori_loop(0, CHUNKS, drain, 0)
        part.wait_send()
        for n in range(2):
            pl.when(has_hi)(edge(n, 0).wait_send)
            pl.when(has_lo)(edge(n, 1).wait_send)
            level(n).wait_send()
        settle(MSG, q_send)
        for copy in results:
            copy.wait()


def body(spectrum, wind, land_mask, intersection, ocean_state, sea_level):
    v = lambda *shape, dtype=F32: pltpu.VMEM(shape, dtype)
    dma = lambda *shape: pltpu.SemaphoreType.DMA(shape) if shape else pltpu.SemaphoreType.DMA
    anywhere = pl.BlockSpec(memory_space=pltpu.HBM)
    scratch = [
        pltpu.SMEM(TABLE.shape, F32),
        v(2, FD * 8, 128), v(2, FD * 8, 128), v(DLOC, 8, 256), v(FD, 128),
        v(WSTEPS, 2, 2, FD, 128), v(WSTEPS, 2, 2, FD, 128),
        v(2, 8, 256), v(8, 256, dtype=jnp.int32), v(8, 256, dtype=jnp.int32),
        v(16, 256, dtype=jnp.int32), v(2, 16, 256, dtype=jnp.int32),
        v(256, 128), v(WSTEPS, 8, 256), v(WSTEPS, 5, 8, 256), v(40, 256), v(40, 256), v(256, 128), v(256, 128),
        v(2, 192, 128), v(2, 192, 128), v(2, 192, 128), v(8, 256), v(16, 256), v(16, 256), v(128, 256),
        v(256, 128), v(256, 128), v(256, 128), v(256, 256),
        v(2, 2, 24, 256), v(2, 2, 24, 256), v(2, 24, 256), v(2, 24, 256), v(RCH * 8, 256),
        dma(CHUNKS, 2), dma(3), dma(WSTEPS, 2, CHUNKS), dma(WSTEPS, 2, CHUNKS), dma(WSTEPS, 5), dma(WSTEPS, 5),
        dma(2), dma(2), dma(), dma(), dma(), dma(), dma(), dma(), dma(), dma(),
        dma(2, 2), dma(2, 2), dma(2), dma(2), dma(2),
    ]
    waves, ocean = pl.pallas_call(
        kernel,
        out_shape=(
            jax.ShapeDtypeStruct((FD * 8, 256), F32),
            jax.ShapeDtypeStruct((192, 256), F32),
        ),
        in_specs=[anywhere] * 6,
        out_specs=(anywhere, anywhere),
        scratch_shapes=scratch,
        compiler_params=pltpu.CompilerParams(collective_id=0, has_side_effects=True, vmem_limit_bytes=48 << 20),
    )(
        *(
            pltpu.with_memory_space_constraint(x, pltpu.HBM)
            for x in (
                spectrum.reshape(FD * 8, 256),
                wind,
                land_mask,
                intersection,
                ocean_state.reshape(192, 256),
                sea_level.reshape(8, 256),
            )
        )
    )
    return waves.reshape(spectrum.shape), ocean.reshape(ocean_state.shape)


def solution(mesh):
    return jax.shard_map(
        body,
        mesh=mesh,
        in_specs=(
            P("grp", None, "spec", "tile", None),
            P(None, "tile", None),
            P("tile", None),
            P("tile", None),
            P("grp", None, "spec", "tile", None),
            P("grp", "tile", None),
        ),
        out_specs=(P("grp", None, "spec", "tile", None), P("grp", None, "spec", "tile", None)),
        check_vma=False,
    )
```

```python
import math

import jax
import jax.numpy as jnp
import numpy as np
from jax import lax
from jax.experimental import pallas as pl
from jax.experimental.pallas import tpu as pltpu
from jax.sharding import PartitionSpec as P

FREQS = 32
DIRS = 36
LEVELS = 16
WSTEPS = 4
TILES = 32
DLOC = 18
KLOC = 8
FD = FREQS * DLOC
CHUNKS = 8
FCH = FREQS // CHUNKS
RCH = FCH * DLOC
PCH = 6
F32 = jnp.float32

_freq = 0.04 * 1.1 ** np.arange(FREQS)
_cel = 1.56 / _freq
_gs = 0.4 * 1.1 ** (-np.arange(FREQS, dtype=np.float64))
_bw = 0.1 * _freq * (2.0 * math.pi / DIRS)
TABLE = np.stack([_gs, 0.05 / _cel, _bw, 5.0 * _bw / _cel, 20.0 * _bw * _freq**3]).astype(np.float32)
_ang = 2.0 * math.pi * (np.arange(DIRS) + 0.5) / DIRS
COS = [float(np.float32(x)) for x in np.cos(_ang)[:DLOC]]
SIN = [float(np.float32(x)) for x in np.sin(_ang)[:DLOC]]
DIR_ORDER = [d for k in range(DLOC // 2) for d in (k, DLOC - 1 - k)]
_prof = np.exp(-2.0 * (np.arange(LEVELS) + 0.5) / LEVELS)
_wgt = _prof / _prof.sum()


def mesh_copy(src, dst, send, recv, where):
    return pltpu.make_async_remote_copy(
        src_ref=src,
        dst_ref=dst,
        send_sem=send,
        recv_sem=recv,
        device_id=where,
        device_id_type=pl.DeviceIdType.MESH,
    )


def settle(buf, sem):
    pltpu.make_async_copy(buf, buf, sem).wait()


def kernel(
    spec_h, wind_h, land_h, inter_h, ocean_h, sea_h, out_w, out_o,
    tab, B, G, PT, WD, CNT, H, S, wind, land, inter, NBS, NBR, QR, TS, TR, BANDS, BANDR, MSG2, MMSG,
    Q, A1, A2, sea, CS, CR, SX, MSG, MR, BR, BTS, ES, EH, LS, LH, zbuf,
    load_sem, small_sem, h_send, h_recv, t_send, t_recv, nb_send, nb_recv,
    q_send, q_recv, m_send, m_recv, f_send, f_recv, c_send, c_recv, e_send, e_recv, l_send, l_recv, out_sem,
):
    grp = lax.axis_index("grp")
    tile = lax.axis_index("tile")
    sp = lax.axis_index("spec")
    other = 1 - sp
    sgn = (1 - 2 * sp).astype(F32)
    has_lo = tile > 0
    has_hi = tile < TILES - 1
    lo_t = jnp.maximum(tile - 1, 0)
    hi_t = jnp.minimum(tile + 1, TILES - 1)
    lane = lax.broadcasted_iota(jnp.int32, (8, 128), 1)
    row = lax.broadcasted_iota(jnp.int32, (8, 128), 0)
    first_lane, last_lane = lane == 0, lane == 127
    first_row, last_row = row == 0, row == 7
    low_rows = row < 4
    halves = (slice(0, 128), slice(128, 256))

    def from_left(x):
        a, b = pltpu.roll(x[0], 1, 1), pltpu.roll(x[1], 1, 1)
        return jnp.where(first_lane, 0.0, a), jnp.where(first_lane, a, b)

    def from_right(x):
        a, b = pltpu.roll(x[0], 127, 1), pltpu.roll(x[1], 127, 1)
        return jnp.where(last_lane, b, a), jnp.where(last_lane, 0.0, b)

    def circular(x, shift):
        a, b = pltpu.roll(x[0], shift, 1), pltpu.roll(x[1], shift, 1)
        m = lane < shift
        return jnp.where(m, b, a), jnp.where(m, a, b)

    def barrel(x, amount):
        for bit in range(8):
            moved = circular(x, 1 << bit) if bit < 7 else (x[1], x[0])
            x = tuple(jnp.where((amount[h] & (1 << bit)) != 0, moved[h], x[h]) for h in range(2))
        return x

    def pair(ref, *lead):
        return tuple(ref[(*lead, slice(None), hs)] for hs in halves)

    def put(ref, value, rows):
        for h in range(2):
            ref[rows, halves[h]] = value[h]

    barrier = pltpu.get_barrier_semaphore()

    def greet(where):
        pl.semaphore_signal(barrier, 1, device_id=where, device_id_type=pl.DeviceIdType.MESH)

    greet({"spec": other})

    @pl.when(has_lo)
    def _():
        greet({"tile": lo_t})
        greet({"tile": lo_t, "spec": other})

    @pl.when(has_hi)
    def _():
        greet({"tile": hi_t})
        greet({"tile": hi_t, "spec": other})

    def greet_across(u, carry):
        greet({"grp": 1 - grp, "tile": u})
        return carry

    lax.fori_loop(0, TILES, greet_across, 0)
    beside = jnp.where(has_lo, 2, 0) + jnp.where(has_hi, 2, 0)

    def everyone_in():
        pl.semaphore_wait(barrier, TILES + 1 + beside)

    @pl.when(grp == 0)
    def wave():
        def load(c):
            rows = pl.ds(pl.multiple_of(c * RCH * 8, 8), RCH * 8)
            return [
                pltpu.make_async_copy(spec_h.at[rows, hs], B.at[h, rows, :], load_sem.at[c, h])
                for h, hs in enumerate(halves)
            ]

        smalls = [
            pltpu.make_async_copy(wind_h, wind, small_sem.at[0]),
            pltpu.make_async_copy(land_h, land, small_sem.at[1]),
            pltpu.make_async_copy(inter_h, inter, small_sem.at[2]),
        ]
        for copy in smalls:
            copy.start()
        for q in range(TABLE.shape[0]):
            for f in range(FREQS):
                tab[q, f] = float(TABLE[q, f])

        def begin(c, carry):
            for copy in load(c):
                copy.start()
            return carry

        lax.fori_loop(0, CHUNKS, begin, 0)

        def halo(n, side, c):
            rows = pl.ds(pl.multiple_of(c * RCH, 8), RCH)
            return mesh_copy(
                S.at[n, side, :, rows, :], H.at[n, side, :, rows, :], h_send.at[n, side, c], h_recv.at[n, side, c],
                {"tile": hi_t if side == 0 else lo_t},
            )

        def edges_out(n, c):
            for k in range(RCH // 8):
                at = c * RCH + 8 * k
                rows = pl.ds(pl.multiple_of(at, 8), 8)
                for h in range(2):
                    S[n, 0, h, rows, :] = B[h, pl.ds(at * 8 + 7, 8, stride=8), :]
                    S[n, 1, h, rows, :] = B[h, pl.ds(at * 8, 8, stride=8), :]

            @pl.when(has_hi)
            def _():
                halo(n, 0, c).start()

            @pl.when(has_lo)
            def _():
                halo(n, 1, c).start()

        for copy in smalls:
            copy.wait()
        wet_i = pair(land)
        wet = tuple(x.astype(F32) for x in wet_i)
        shift = tuple((x - lane - 128 * h) & 255 for h, x in enumerate(pair(inter)))
        put(NBS, wet_i, slice(0, 8))
        put(NBS, shift, slice(8, 16))

        def neighbour(side):
            return mesh_copy(
                NBS, NBR.at[side], nb_send.at[side], nb_recv.at[side],
                {"tile": hi_t if side == 0 else lo_t},
            )

        everyone_in()

        @pl.when(has_hi)
        def _():
            neighbour(0).start()

        @pl.when(has_lo)
        def _():
            neighbour(1).start()

        wet_back = circular(barrel(wet, shift), 1)

        def windows(fields, u):
            acc = jnp.zeros((8, 128), F32)
            for f, field in enumerate(fields):
                start = (8 * u + 32 * f) % 128
                offset = (lane - start) & 127
                inside = offset < 10
                base = (8 * u) // 128
                p = 8 * u + offset
                value = field[base]
                if 8 * u % 128 + 10 > 128:
                    turned = (lane - 32 * f) & 127
                    value = jnp.where(turned < 16, field[1 - base], value)
                acc = jnp.where(inside, value, acc)
            return acc

        for u in range(TILES):
            MMSG[pl.ds(8 * u, 8), :] = windows([wet_back], u)

        def to_ocean(src, dst, send, recv, u):
            return mesh_copy(
                src.at[pl.ds(pl.multiple_of(u * 8, 8), 8), :],
                dst.at[pl.ds(pl.multiple_of(tile * 8, 8), 8), :],
                send, recv, {"grp": 1, "tile": u},
            )

        def send_mask(u, carry):
            to_ocean(MMSG, MR, m_send, m_recv, u).start()
            return carry

        lax.fori_loop(0, TILES, send_mask, 0)

        @pl.when(jnp.logical_not(has_lo))
        def _():
            H[:, 0] = jnp.zeros((WSTEPS, 2, FD, 128), F32)
            NBR[0] = jnp.zeros((16, 256), jnp.int32)
            TR[:, 1:3] = jnp.zeros((WSTEPS, 2, 8, 256), F32)

        @pl.when(jnp.logical_not(has_hi))
        def _():
            H[:, 1] = jnp.zeros((WSTEPS, 2, FD, 128), F32)
            NBR[1] = jnp.zeros((16, 256), jnp.int32)
            TR[:, 3:5] = jnp.zeros((WSTEPS, 2, 8, 256), F32)

        def first_edges(c, carry):
            for copy in load(c):
                copy.wait()
            edges_out(0, c)
            return carry

        lax.fori_loop(0, CHUNKS, first_edges, 0)

        for d in range(DLOC):
            for h, hs in enumerate(halves):
                WD[d, :, hs] = wind[0, :, hs] * (sgn * COS[d]) + wind[1, :, hs] * (sgn * SIN[d])

        def growth(f, carry):
            slope = tab[1, f]
            sgs = tab[0, f] * sgn
            for d in range(DLOC):
                i = f * DLOC + d
                rows = pl.ds(pl.multiple_of(i * 8, 8), 8)
                for h, hs in enumerate(halves):
                    G[h, rows, :] = 1.0 + jnp.maximum(WD[d, :, hs] * slope - 0.05, 0.0)
                CNT[pl.ds(i, 1), :] = jnp.full((1, 128), sgs * SIN[d], F32)
            return carry

        lax.fori_loop(0, FREQS, growth, 0)

        @pl.when(has_lo)
        def _():
            neighbour(0).wait_recv()

        @pl.when(has_hi)
        def _():
            neighbour(1).wait_recv()

        edge_i = tuple(
            jnp.where(low_rows, NBR[1, 0:8, hs], NBR[0, 0:8, hs]) for hs in halves
        )
        edge_wet = tuple(x.astype(F32) for x in edge_i)
        edge_shift = tuple(
            jnp.where(low_rows, NBR[1, 8:16, hs], NBR[0, 8:16, hs]) for hs in halves
        )

        settle(QR, q_recv)
        fields = []
        for c in range(5):
            parts = []
            for h in range(2):
                acc = jnp.zeros((8, 128), F32)
                for k in range(16):
                    u = 16 * h + k
                    acc = jnp.where((lane >> 3) == (k + c) % 16, QR[pl.ds(8 * u, 8), :], acc)
                parts.append(pltpu.roll(acc, 128 - 8 * c, 1) if c else acc)
            fields.append(tuple(parts))
        left = tuple((256 - x) & 255 for x in shift)
        edge_left = tuple((256 - x) & 255 for x in edge_shift)
        u01 = tuple(0.1 * x for x in barrel(fields[0], left))
        v01 = tuple(0.1 * x for x in barrel(fields[1], left))

        def stiffness(level):
            depth = tuple(10.0 + 4.0 * x for x in level)
            return tuple(25.0 / (x * x) for x in depth)

        stiff = stiffness(barrel(fields[2], left))
        edge_v = tuple(0.1 * x for x in barrel(fields[3], edge_left))
        edge_stiff = stiffness(barrel(fields[4], edge_left))
        v_lo = tuple(jnp.broadcast_to(x[7:8], (8, 128)) for x in edge_v)
        v_hi = tuple(jnp.broadcast_to(x[0:1], (8, 128)) for x in edge_v)

        def halo_in(n, c):
            @pl.when(has_lo)
            def _():
                halo(n, 0, c).wait_recv()

            @pl.when(has_hi)
            def _():
                halo(n, 1, c).wait_recv()

            for k in range(RCH // 8):
                rows = pl.ds(pl.multiple_of(c * RCH + 8 * k, 8), 8)
                cn = CNT[rows, :]
                for h in range(2):
                    H[n, 0, h, rows, :] = jnp.maximum((cn + v_lo[h]) * H[n, 0, h, rows, :], 0.0)
                    H[n, 1, h, rows, :] = jnp.minimum((cn + v_hi[h]) * H[n, 1, h, rows, :], 0.0)

        def terms(n, i, rows, ce, cn):
            b = [B[h, rows, :] for h in range(2)]
            X = [(u01[h] + ce) * b[h] for h in range(2)]
            Y = [(v01[h] + cn) * b[h] for h in range(2)]
            own = [(b[h] - jnp.abs(X[h])) - jnp.abs(Y[h]) for h in range(2)]
            a = [pltpu.roll(jnp.maximum(x, 0.0), 1, 1) for x in X]
            west = [a[0], jnp.where(first_lane, a[0], a[1])]
            a = [pltpu.roll(jnp.minimum(x, 0.0), 127, 1) for x in X]
            east = [jnp.where(last_lane, a[1], a[0]), a[1]]
            south = [
                jnp.where(
                    first_row, H[n, 0, h, pl.ds(i, 8, stride=0), :], pltpu.roll(jnp.maximum(Y[h], 0.0), 1, 0)
                )
                for h in range(2)
            ]
            north = [
                jnp.where(
                    last_row, H[n, 1, h, pl.ds(i, 8, stride=0), :], pltpu.roll(jnp.minimum(Y[h], 0.0), 7, 0)
                )
                for h in range(2)
            ]
            return own, west, east, south, north

        def ahead(n):
            def chunk(c, carry):
                halo_in(n, c)

                def band(fc, carry):
                    f = c * FCH + fc
                    sgs = tab[0, f] * sgn
                    for d in range(DLOC):
                        i = f * DLOC + d
                        rows = pl.ds(pl.multiple_of(i * 8, 8), 8)
                        for q, term in enumerate(terms(n, i, rows, sgs * COS[d], sgs * SIN[d])):
                            for h in range(2):
                                PT[q, h, rows, :] = term[h]
                    return carry

                return lax.fori_loop(0, FCH, band, carry)

            lax.fori_loop(0, PCH, chunk, 0)

        def factors(r, edge_r):
            a, b = [pltpu.roll(x, 1, 1) for x in r], [pltpu.roll(x, 127, 1) for x in r]
            r_w = (jnp.where(first_lane, 0.0, a[0]), jnp.where(first_lane, a[0], a[1]))
            r_e = (jnp.where(last_lane, b[1], b[0]), jnp.where(last_lane, 0.0, b[1]))
            r_s = tuple(jnp.where(first_row, pltpu.roll(edge_r[h], 1, 0), pltpu.roll(r[h], 1, 0)) for h in range(2))
            r_n = tuple(jnp.where(last_row, pltpu.roll(edge_r[h], 7, 0), pltpu.roll(r[h], 7, 0)) for h in range(2))
            return tuple(r), r_w, r_e, r_s, r_n

        def sweep(n, r, edge_r, last):
            r_all = factors(r, edge_r)

            def chunk(c, sums, prepared):
                if not prepared:
                    halo_in(n, c)

                def band(fc, sums):
                    f = c * FCH + fc
                    sgs = tab[0, f] * sgn
                    zero = jnp.zeros((8, 128), F32)
                    acc = [[zero, zero] for _ in range(5 if last else 1)]
                    half_way = {}
                    for d in (DIR_ORDER if last else range(DLOC)):
                        i = f * DLOC + d
                        rows = pl.ds(pl.multiple_of(i * 8, 8), 8)
                        if prepared:
                            five = [[PT[q, h, rows, :] for h in range(2)] for q in range(5)]
                        else:
                            five = terms(n, i, rows, sgs * COS[d], sgs * SIN[d])
                        for h in range(2):
                            own, west, east, south, north = (r_all[q][h] * five[q][h] for q in range(5))
                            adv = own + ((west - east) + (south - north))
                            new = adv * G[h, rows, :]
                            B[h, rows, :] = new
                            acc[0][h] += adv
                            if last:
                                mine = (new - adv, new)
                                if h not in half_way:
                                    half_way[h] = mine
                                    continue
                                for q, (a, b) in enumerate(zip(half_way.pop(h), mine)):
                                    acc[1 + 2 * q][h] += (a - b) * COS[DLOC - 1 - d]
                                    acc[2 + 2 * q][h] += (a + b) * SIN[d]
                    weights = [tab[2, f], tab[3, f], tab[3, f], tab[4, f], tab[4, f]]
                    if last:
                        weights = weights[:1] + [w * sgn for w in weights[1:]]
                    return tuple(
                        tuple(total[h] + acc[q][h] * weights[q] for h in range(2)) for q, total in enumerate(sums)
                    )

                sums = lax.fori_loop(0, FCH, band, sums)
                if not last:

                    @pl.when(c < CHUNKS - 1)
                    def _():
                        edges_out(n + 1, c)

                return sums

            zero = jnp.zeros((8, 128), F32)
            sums = tuple((zero, zero) for _ in range(5 if last else 1))
            begun = PCH if last else jnp.where(n > 0, PCH, 0)
            sums = lax.fori_loop(0, begun, lambda c, x: chunk(c, x, True), sums)
            return lax.fori_loop(begun, CHUNKS, lambda c, x: chunk(c, x, False), sums)

        def total_copies(n):
            return [
                (None, mesh_copy(TS.at[n], TR.at[n, 0], t_send.at[n, 0], t_recv.at[n, 0], {"spec": other})),
                (has_hi, mesh_copy(TS.at[n], TR.at[n, 1], t_send.at[n, 1], t_recv.at[n, 1], {"tile": hi_t})),
                (has_hi, mesh_copy(TS.at[n], TR.at[n, 2], t_send.at[n, 2], t_recv.at[n, 2], {"tile": hi_t, "spec": other})),
                (has_lo, mesh_copy(TS.at[n], TR.at[n, 3], t_send.at[n, 3], t_recv.at[n, 3], {"tile": lo_t})),
                (has_lo, mesh_copy(TS.at[n], TR.at[n, 4], t_send.at[n, 4], t_recv.at[n, 4], {"tile": lo_t, "spec": other})),
            ]

        def gated(condition, action):
            if condition is None:
                action()
            else:
                pl.when(condition)(action)

        def one_step(n, carry):
            r, edge_r = carry
            (total,) = sweep(n, r, edge_r, False)
            for h, hs in enumerate(halves):
                TS[n, :, hs] = total[h]
            copies = total_copies(n)
            for condition, copy in copies:
                gated(condition, copy.start)
            edges_out(n + 1, CHUNKS - 1)
            ahead(n + 1)
            for (_, copy), condition in zip(copies, [None, has_lo, has_lo, has_hi, has_hi]):
                gated(condition, copy.wait_recv)
            new_r, new_edge = [], []
            for h, hs in enumerate(halves):
                full = total[h] + TR[n, 0, :, hs]
                new_r.append(wet[h] / (1.0 + stiff[h] * full))
                lower = TR[n, 1, :, hs] + TR[n, 2, :, hs]
                upper = TR[n, 3, :, hs] + TR[n, 4, :, hs]
                edge = jnp.where(low_rows, upper, lower)
                new_edge.append(edge_wet[h] / (1.0 + edge_stiff[h] * edge))
            return tuple(new_r), tuple(new_edge)

        r, edge_r = lax.fori_loop(0, WSTEPS - 1, one_step, (wet, edge_wet))
        n = WSTEPS - 1
        sums = sweep(n, r, edge_r, True)
        for q in range(5):
            put(BANDS, sums[q], slice(8 * q, 8 * q + 8))
        swap = mesh_copy(BANDS, BANDR, t_send.at[n, 0], t_recv.at[n, 0], {"spec": other})
        swap.start()
        swap.wait_recv()
        full = [tuple(sums[q][h] + BANDR[8 * q : 8 * q + 8, halves[h]] for h in range(2)) for q in range(5)]
        breaking = tuple(1.0 / (1.0 + stiff[h] * full[0][h]) for h in range(2))
        final = tuple(wet[h] * breaking[h] for h in range(2))
        bands = []
        for q in range(1, 5):
            scale = breaking if q < 3 else final
            bands.append(circular(barrel(tuple(scale[h] * full[q][h] for h in range(2)), shift), 1))
        bands = [tuple(pltpu.roll(x, 32 * f, 1) if f else x for x in field) for f, field in enumerate(bands)]
        for u in range(TILES):
            MSG2[pl.ds(8 * u, 8), :] = windows(bands, u)

        def send_bands(u, carry):
            to_ocean(MSG2, BR, f_send, f_recv, u).start()
            return carry

        lax.fori_loop(0, TILES, send_bands, 0)

        def store(c):
            rows = pl.ds(pl.multiple_of(c * RCH * 8, 8), RCH * 8)
            return [
                pltpu.make_async_copy(B.at[h, rows, :], out_w.at[rows, hs], load_sem.at[c, h])
                for h, hs in enumerate(halves)
            ]

        def finish(c, carry):
            def scale_f(i, carry):
                for d in range(DLOC):
                    rows = pl.ds(pl.multiple_of((c * RCH + i * DLOC + d) * 8, 8), 8)
                    for h in range(2):
                        B[h, rows, :] = B[h, rows, :] * final[h]
                return carry

            lax.fori_loop(0, FCH, scale_f, 0)
            for copy in store(c):
                copy.start()
            return carry

        lax.fori_loop(0, CHUNKS, finish, 0)
        A2[...] = jnp.zeros((2, 192, 128), F32)
        blanks = [pltpu.make_async_copy(A2.at[h], out_o.at[:, hs], out_sem.at[h]) for h, hs in enumerate(halves)]
        for copy in blanks:
            copy.start()

        def drain(c, carry):
            for copy in store(c):
                copy.wait()

            @pl.when(has_hi)
            def _():
                for n in range(WSTEPS):
                    halo(n, 0, c).wait_send()

            @pl.when(has_lo)
            def _():
                for n in range(WSTEPS):
                    halo(n, 1, c).wait_send()

            return carry

        lax.fori_loop(0, CHUNKS, drain, 0)
        for copy in blanks:
            copy.wait()
        for m in range(WSTEPS - 1):
            for condition, copy in total_copies(m):
                gated(condition, copy.wait_send)
        swap.wait_send()
        gated(has_hi, neighbour(0).wait_send)
        gated(has_lo, neighbour(1).wait_send)
        settle(MMSG, m_send)
        settle(MSG2, f_send)

    @pl.when(grp == 1)
    def circulation():
        top = (1 - sp).astype(F32)
        deep = sp.astype(F32)
        down = jnp.where(sp == 0, 1.0, math.exp(-1.0)).astype(F32)
        loads = [
            pltpu.make_async_copy(ocean_h.at[:, halves[0]], Q.at[0], small_sem.at[0]),
            pltpu.make_async_copy(ocean_h.at[:, halves[1]], Q.at[1], small_sem.at[1]),
            pltpu.make_async_copy(sea_h, sea, small_sem.at[2]),
        ]
        for copy in loads:
            copy.start()
        for copy in loads:
            copy.wait()
        for c in range(2):
            for h, hs in enumerate(halves):
                acc = jnp.zeros((8, 128), F32)
                for k in range(KLOC):
                    acc += Q[h, pl.ds((c * KLOC + k) * 8, 8), :] * float(_wgt[k])
                CS[pl.ds(8 * c, 8), hs] = acc * down
        everyone_in()
        part = mesh_copy(CS, CR, c_send, c_recv, {"spec": other})
        part.start()

        def edge(n, side):
            return mesh_copy(
                ES.at[n, side], EH.at[n, side], e_send.at[n, side], e_recv.at[n, side],
                {"tile": hi_t if side == 0 else lo_t},
            )

        def level(n):
            return mesh_copy(LS.at[n], LH.at[n], l_send.at[n], l_recv.at[n], {"spec": other})

        def rims_out(n, src):
            for c in range(3):
                for h, hs in enumerate(halves):
                    ES[n, 0, pl.ds(8 * c, 8), hs] = src[h, pl.ds(c * 64 + 7, 8, stride=8), :]
                    ES[n, 1, pl.ds(8 * c, 8), hs] = src[h, pl.ds(c * 64, 8, stride=8), :]
                    LS[n, pl.ds(8 * c, 8), hs] = jnp.where(
                        sp == 0, src[h, pl.ds(c * 64 + 56, 8), :], src[h, pl.ds(c * 64, 8), :]
                    )
            pl.when(has_hi)(edge(n, 0).start)
            pl.when(has_lo)(edge(n, 1).start)
            level(n).start()

        SX[...] = jnp.zeros((128, 256), F32)
        put(SX, pair(sea), slice(16, 24))
        part.wait_recv()
        for c in range(2):
            rows = pl.ds(8 * c, 8)
            SX[rows, :] = CS[rows, :] + CR[rows, :]
        ahead_rows = (lane & 7) < 4
        for c in range(2):
            src = tuple(SX[pl.ds(8 + 8 * c, 8), hs] for hs in halves)
            ahead, behind = circular(src, 120), circular(src, 8)
            ahead = (ahead[1], ahead[0])
            put(SX, tuple(jnp.where(ahead_rows, ahead[h], behind[h]) for h in range(2)), slice(24 + 8 * c, 32 + 8 * c))
        for h, hs in enumerate(halves):
            MSG[pl.ds(128 * h, 128), :] = pltpu.roll(SX[:, hs].T, tile * 8 % 128, 1)

        def to_wave(u):
            return mesh_copy(
                MSG.at[pl.ds(pl.multiple_of(u * 8, 8), 8), :],
                QR.at[pl.ds(pl.multiple_of(tile * 8, 8), 8), :],
                q_send, q_recv, {"grp": 0, "tile": u},
            )

        def send_q(u, carry):
            to_wave(u).start()
            return carry

        lax.fori_loop(0, TILES, send_q, 0)
        rims_out(0, Q)

        zbuf[...] = jnp.zeros((RCH * 8, 256), F32)

        def blank(c):
            rows = pl.ds(pl.multiple_of(c * RCH * 8, 8), RCH * 8)
            return pltpu.make_async_copy(zbuf, out_w.at[rows, :], load_sem.at[c, 0])

        def begin(c, carry):
            blank(c).start()
            return carry

        lax.fori_loop(0, CHUNKS, begin, 0)

        @pl.when(jnp.logical_not(has_lo))
        def _():
            EH[:, 0] = jnp.zeros((2, 24, 256), F32)

        @pl.when(jnp.logical_not(has_hi))
        def _():
            EH[:, 1] = jnp.zeros((2, 24, 256), F32)

        at_lo = jnp.where(has_lo, 1.0, 0.0).astype(F32)
        at_hi = jnp.where(has_hi, 1.0, 0.0).astype(F32)

        def arrived(buf, slots):
            for h in range(2):
                turned = buf[pl.ds(128 * h, 128), :].T
                BTS[pl.ds(0, 128), halves[h]] = turned
                BTS[pl.ds(128, 128), halves[h]] = turned
            out = []
            for f in range(slots):
                start = pl.multiple_of((8 * tile + 32 * f) % 128, 8)
                wide = BTS[pl.ds(start, 16), :]
                out.append(tuple((wide[0:8, hs], wide[1:9, hs], wide[2:10, hs]) for hs in halves))
            return out

        settle(MR, m_recv)
        (mask3,) = arrived(MR, 1)
        mask = tuple(x[1] for x in mask3)
        mask_lo = tuple(jnp.where(first_row, x[0] * at_lo, x[0]) for x in mask3)
        mask_hi = tuple(jnp.where(last_row, x[2] * at_hi, x[2]) for x in mask3)

        def lateral(x, lower, upper):
            left, right = from_left(x), from_right(x)
            return tuple(lower[h] + upper[h] + left[h] + right[h] - 4.0 * x[h] for h in range(2))

        def substep(n, src, dst):
            for c in range(3):
                for k in range(KLOC):
                    at = (c * KLOC + k) * 8
                    x = tuple(src[h, pl.ds(at, 8), :] for h in range(2))
                    row_at = 8 * c + k
                    lower = tuple(
                        jnp.where(first_row, EH[n, 0, row_at : row_at + 1, hs], pltpu.roll(x[h], 1, 0))
                        for h, hs in enumerate(halves)
                    )
                    upper = tuple(
                        jnp.where(last_row, EH[n, 1, row_at : row_at + 1, hs], pltpu.roll(x[h], 7, 0))
                        for h, hs in enumerate(halves)
                    )
                    side = lateral(x, lower, upper)
                    for h, hs in enumerate(halves):
                        if k > 0:
                            above = src[h, pl.ds(at - 8, 8), :]
                        else:
                            above = LH[n, pl.ds(8 * c, 8), hs] * deep
                        if k < KLOC - 1:
                            below = src[h, pl.ds(at + 8, 8), :]
                        else:
                            below = LH[n, pl.ds(8 * c, 8), hs] * top
                        value = x[h] + 0.1 * side[h] + 0.2 * (above + below - 2.0 * x[h])
                        if c == 0:
                            value = value + 0.1 * src[h, pl.ds(at + 64, 8), :]
                        if c == 1:
                            value = value - 0.1 * src[h, pl.ds(at - 64, 8), :]
                        dst[h, pl.ds(at, 8), :] = value * mask[h]

        def rims_in(n):
            pl.when(has_lo)(edge(n, 0).wait_recv)
            pl.when(has_hi)(edge(n, 1).wait_recv)
            level(n).wait_recv()

        rims_in(0)
        substep(0, Q, A1)
        rims_out(1, A1)
        rims_in(1)
        substep(1, A1, A2)

        settle(BR, f_recv)
        forced, spread = [], []
        for f, three in enumerate(arrived(BR, 4)):
            lower = tuple(three[h][0] * mask_lo[h] for h in range(2))
            own = tuple(three[h][1] * mask[h] for h in range(2))
            upper = tuple(three[h][2] * mask_hi[h] for h in range(2))
            forced.append(own)
            spread.append(lateral(own, lower, upper))
        for k in range(KLOC):
            near, far = math.exp(0.125), math.exp(-0.125)
            prof = float(_prof[k]) * down
            above = near if k > 0 else near * deep
            below = far if k < KLOC - 1 else far * top
            stay = prof * (1.0 + 0.2 * (above + below - 2.0))
            for h, hs in enumerate(halves):
                east = (0.1 * prof) * forced[3][h]
                north = (-0.1 * prof) * forced[2][h]
                d_east = (0.1 * stay) * forced[3][h] + (0.01 * prof) * spread[3][h]
                d_north = (-0.1 * stay) * forced[2][h] - (0.01 * prof) * spread[2][h]
                if k == 0:
                    east = east + top * forced[0][h]
                    north = north + top * forced[1][h]
                    d_east = d_east + top * (0.6 * forced[0][h] + 0.1 * spread[0][h])
                    d_north = d_north + top * (0.6 * forced[1][h] + 0.1 * spread[1][h])
                if k == 1:
                    d_east = d_east + (0.2 * top) * forced[0][h]
                    d_north = d_north + (0.2 * top) * forced[1][h]
                A2[h, pl.ds(8 * k, 8), :] += mask[h] * (d_east + 0.1 * north) + east
                A2[h, pl.ds(64 + 8 * k, 8), :] += mask[h] * (d_north - 0.1 * east) + north
        results = [pltpu.make_async_copy(A2.at[h], out_o.at[:, hs], out_sem.at[h]) for h, hs in enumerate(halves)]
        for copy in results:
            copy.start()

        def drain(c, carry):
            blank(c).wait()
            return carry

        lax.fori_loop(0, CHUNKS, drain, 0)
        part.wait_send()
        for n in range(2):
            pl.when(has_hi)(edge(n, 0).wait_send)
            pl.when(has_lo)(edge(n, 1).wait_send)
            level(n).wait_send()
        settle(MSG, q_send)
        for copy in results:
            copy.wait()


def body(spectrum, wind, land_mask, intersection, ocean_state, sea_level):
    v = lambda *shape, dtype=F32: pltpu.VMEM(shape, dtype)
    dma = lambda *shape: pltpu.SemaphoreType.DMA(shape) if shape else pltpu.SemaphoreType.DMA
    anywhere = pl.BlockSpec(memory_space=pltpu.HBM)
    scratch = [
        pltpu.SMEM(TABLE.shape, F32),
        v(2, FD * 8, 128), v(2, FD * 8, 128), v(5, 2, PCH * RCH * 8, 128), v(DLOC, 8, 256), v(FD, 128),
        v(WSTEPS, 2, 2, FD, 128), v(WSTEPS, 2, 2, FD, 128),
        v(2, 8, 256), v(8, 256, dtype=jnp.int32), v(8, 256, dtype=jnp.int32),
        v(16, 256, dtype=jnp.int32), v(2, 16, 256, dtype=jnp.int32),
        v(256, 128), v(WSTEPS, 8, 256), v(WSTEPS, 5, 8, 256), v(40, 256), v(40, 256), v(256, 128), v(256, 128),
        v(2, 192, 128), v(2, 192, 128), v(2, 192, 128), v(8, 256), v(16, 256), v(16, 256), v(128, 256),
        v(256, 128), v(256, 128), v(256, 128), v(256, 256),
        v(2, 2, 24, 256), v(2, 2, 24, 256), v(2, 24, 256), v(2, 24, 256), v(RCH * 8, 256),
        dma(CHUNKS, 2), dma(3), dma(WSTEPS, 2, CHUNKS), dma(WSTEPS, 2, CHUNKS), dma(WSTEPS, 5), dma(WSTEPS, 5),
        dma(2), dma(2), dma(), dma(), dma(), dma(), dma(), dma(), dma(), dma(),
        dma(2, 2), dma(2, 2), dma(2), dma(2), dma(2),
    ]
    waves, ocean = pl.pallas_call(
        kernel,
        out_shape=(
            jax.ShapeDtypeStruct((FD * 8, 256), F32),
            jax.ShapeDtypeStruct((192, 256), F32),
        ),
        in_specs=[anywhere] * 6,
        out_specs=(anywhere, anywhere),
        scratch_shapes=scratch,
        compiler_params=pltpu.CompilerParams(collective_id=0, has_side_effects=True, vmem_limit_bytes=48 << 20),
    )(
        *(
            pltpu.with_memory_space_constraint(x, pltpu.HBM)
            for x in (
                spectrum.reshape(FD * 8, 256),
                wind,
                land_mask,
                intersection,
                ocean_state.reshape(192, 256),
                sea_level.reshape(8, 256),
            )
        )
    )
    return waves.reshape(spectrum.shape), ocean.reshape(ocean_state.shape)


def solution(mesh):
    return jax.shard_map(
        body,
        mesh=mesh,
        in_specs=(
            P("grp", None, "spec", "tile", None),
            P(None, "tile", None),
            P("tile", None),
            P("tile", None),
            P("grp", None, "spec", "tile", None),
            P("grp", "tile", None),
        ),
        out_specs=(P("grp", None, "spec", "tile", None), P("grp", None, "spec", "tile", None)),
        check_vma=False,
    )
```

```python
import math

import jax
import jax.numpy as jnp
import numpy as np
from jax import lax
from jax.experimental import pallas as pl
from jax.experimental.pallas import tpu as pltpu
from jax.sharding import PartitionSpec as P

FREQS = 32
DIRS = 36
LEVELS = 16
WSTEPS = 4
TILES = 32
DLOC = 18
KLOC = 8
FD = FREQS * DLOC
CHUNKS = 8
FCH = FREQS // CHUNKS
RCH = FCH * DLOC
PCH = 5
HELD = 3
F32 = jnp.float32

_freq = 0.04 * 1.1 ** np.arange(FREQS)
_cel = 1.56 / _freq
_gs = 0.4 * 1.1 ** (-np.arange(FREQS, dtype=np.float64))
_bw = 0.1 * _freq * (2.0 * math.pi / DIRS)
TABLE = np.stack([_gs, 0.05 / _cel, _bw, 5.0 * _bw / _cel, 20.0 * _bw * _freq**3]).astype(np.float32)
_ang = 2.0 * math.pi * (np.arange(DIRS) + 0.5) / DIRS
COS = [float(np.float32(x)) for x in np.cos(_ang)[:DLOC]]
SIN = [float(np.float32(x)) for x in np.sin(_ang)[:DLOC]]
DIR_ORDER = [d for k in range(DLOC // 2) for d in (k, DLOC - 1 - k)]
_prof = np.exp(-2.0 * (np.arange(LEVELS) + 0.5) / LEVELS)
_wgt = _prof / _prof.sum()


def mesh_copy(src, dst, send, recv, where):
    return pltpu.make_async_remote_copy(
        src_ref=src,
        dst_ref=dst,
        send_sem=send,
        recv_sem=recv,
        device_id=where,
        device_id_type=pl.DeviceIdType.MESH,
    )


def settle(buf, sem):
    pltpu.make_async_copy(buf, buf, sem).wait()


def kernel(
    spec_h, wind_h, land_h, inter_h, ocean_h, sea_h, out_w, out_o,
    tab, B, G, PT, WD, CNT, H, S, wind, land, inter, NBS, NBR, QR, TS, TR, BANDS, BANDR, MSG2, MMSG,
    Q, A1, A2, sea, CS, CR, SX, MSG, MR, BR, BTS, ES, EH, LS, LH, zbuf,
    load_sem, small_sem, h_send, h_recv, t_send, t_recv, nb_send, nb_recv,
    q_send, q_recv, m_send, m_recv, f_send, f_recv, c_send, c_recv, e_send, e_recv, l_send, l_recv, out_sem,
):
    grp = lax.axis_index("grp")
    tile = lax.axis_index("tile")
    sp = lax.axis_index("spec")
    other = 1 - sp
    sgn = (1 - 2 * sp).astype(F32)
    has_lo = tile > 0
    has_hi = tile < TILES - 1
    lo_t = jnp.maximum(tile - 1, 0)
    hi_t = jnp.minimum(tile + 1, TILES - 1)
    lane = lax.broadcasted_iota(jnp.int32, (8, 128), 1)
    row = lax.broadcasted_iota(jnp.int32, (8, 128), 0)
    first_lane, last_lane = lane == 0, lane == 127
    first_row, last_row = row == 0, row == 7
    low_rows = row < 4
    halves = (slice(0, 128), slice(128, 256))

    def from_left(x):
        a, b = pltpu.roll(x[0], 1, 1), pltpu.roll(x[1], 1, 1)
        return jnp.where(first_lane, 0.0, a), jnp.where(first_lane, a, b)

    def from_right(x):
        a, b = pltpu.roll(x[0], 127, 1), pltpu.roll(x[1], 127, 1)
        return jnp.where(last_lane, b, a), jnp.where(last_lane, 0.0, b)

    def circular(x, shift):
        a, b = pltpu.roll(x[0], shift, 1), pltpu.roll(x[1], shift, 1)
        m = lane < shift
        return jnp.where(m, b, a), jnp.where(m, a, b)

    def barrel(x, amount):
        for bit in range(8):
            moved = circular(x, 1 << bit) if bit < 7 else (x[1], x[0])
            x = tuple(jnp.where((amount[h] & (1 << bit)) != 0, moved[h], x[h]) for h in range(2))
        return x

    def pair(ref, *lead):
        return tuple(ref[(*lead, slice(None), hs)] for hs in halves)

    def put(ref, value, rows):
        for h in range(2):
            ref[rows, halves[h]] = value[h]

    barrier = pltpu.get_barrier_semaphore()

    def greet(where):
        pl.semaphore_signal(barrier, 1, device_id=where, device_id_type=pl.DeviceIdType.MESH)

    greet({"spec": other})

    @pl.when(has_lo)
    def _():
        greet({"tile": lo_t})
        greet({"tile": lo_t, "spec": other})

    @pl.when(has_hi)
    def _():
        greet({"tile": hi_t})
        greet({"tile": hi_t, "spec": other})

    def greet_across(u, carry):
        greet({"grp": 1 - grp, "tile": u})
        return carry

    lax.fori_loop(0, TILES, greet_across, 0)
    beside = jnp.where(has_lo, 2, 0) + jnp.where(has_hi, 2, 0)

    def everyone_in():
        pl.semaphore_wait(barrier, TILES + 1 + beside)

    @pl.when(grp == 0)
    def wave():
        def load(c):
            rows = pl.ds(pl.multiple_of(c * RCH * 8, 8), RCH * 8)
            return [
                pltpu.make_async_copy(spec_h.at[rows, hs], B.at[h, rows, :], load_sem.at[c, h])
                for h, hs in enumerate(halves)
            ]

        smalls = [
            pltpu.make_async_copy(wind_h, wind, small_sem.at[0]),
            pltpu.make_async_copy(land_h, land, small_sem.at[1]),
            pltpu.make_async_copy(inter_h, inter, small_sem.at[2]),
        ]
        for copy in smalls:
            copy.start()
        for q in range(TABLE.shape[0]):
            for f in range(FREQS):
                tab[q, f] = float(TABLE[q, f])

        def begin(c, carry):
            for copy in load(c):
                copy.start()
            return carry

        lax.fori_loop(0, CHUNKS, begin, 0)

        def halo(n, side, c):
            rows = pl.ds(pl.multiple_of(c * RCH, 8), RCH)
            return mesh_copy(
                S.at[n, side, :, rows, :], H.at[n, side, :, rows, :], h_send.at[n, side, c], h_recv.at[n, side, c],
                {"tile": hi_t if side == 0 else lo_t},
            )

        def edges_out(n, c):
            for k in range(RCH // 8):
                at = c * RCH + 8 * k
                rows = pl.ds(pl.multiple_of(at, 8), 8)
                for h in range(2):
                    S[n, 0, h, rows, :] = B[h, pl.ds(at * 8 + 7, 8, stride=8), :]
                    S[n, 1, h, rows, :] = B[h, pl.ds(at * 8, 8, stride=8), :]

            @pl.when(has_hi)
            def _():
                halo(n, 0, c).start()

            @pl.when(has_lo)
            def _():
                halo(n, 1, c).start()

        for copy in smalls:
            copy.wait()
        wet_i = pair(land)
        wet = tuple(x.astype(F32) for x in wet_i)
        shift = tuple((x - lane - 128 * h) & 255 for h, x in enumerate(pair(inter)))
        put(NBS, wet_i, slice(0, 8))
        put(NBS, shift, slice(8, 16))

        def neighbour(side):
            return mesh_copy(
                NBS, NBR.at[side], nb_send.at[side], nb_recv.at[side],
                {"tile": hi_t if side == 0 else lo_t},
            )

        everyone_in()

        @pl.when(has_hi)
        def _():
            neighbour(0).start()

        @pl.when(has_lo)
        def _():
            neighbour(1).start()

        wet_back = circular(barrel(wet, shift), 1)

        def windows(fields, u):
            acc = jnp.zeros((8, 128), F32)
            for f, field in enumerate(fields):
                start = (8 * u + 32 * f) % 128
                offset = (lane - start) & 127
                inside = offset < 10
                base = (8 * u) // 128
                p = 8 * u + offset
                value = field[base]
                if 8 * u % 128 + 10 > 128:
                    turned = (lane - 32 * f) & 127
                    value = jnp.where(turned < 16, field[1 - base], value)
                acc = jnp.where(inside, value, acc)
            return acc

        for u in range(TILES):
            MMSG[pl.ds(8 * u, 8), :] = windows([wet_back], u)

        def to_ocean(src, dst, send, recv, u):
            return mesh_copy(
                src.at[pl.ds(pl.multiple_of(u * 8, 8), 8), :],
                dst.at[pl.ds(pl.multiple_of(tile * 8, 8), 8), :],
                send, recv, {"grp": 1, "tile": u},
            )

        def send_mask(u, carry):
            to_ocean(MMSG, MR, m_send, m_recv, u).start()
            return carry

        lax.fori_loop(0, TILES, send_mask, 0)

        @pl.when(jnp.logical_not(has_lo))
        def _():
            H[:, 0] = jnp.zeros((WSTEPS, 2, FD, 128), F32)
            NBR[0] = jnp.zeros((16, 256), jnp.int32)
            TR[:, 1:3] = jnp.zeros((WSTEPS, 2, 8, 256), F32)

        @pl.when(jnp.logical_not(has_hi))
        def _():
            H[:, 1] = jnp.zeros((WSTEPS, 2, FD, 128), F32)
            NBR[1] = jnp.zeros((16, 256), jnp.int32)
            TR[:, 3:5] = jnp.zeros((WSTEPS, 2, 8, 256), F32)

        def first_edges(c, carry):
            for copy in load(c):
                copy.wait()
            edges_out(0, c)
            return carry

        lax.fori_loop(0, CHUNKS, first_edges, 0)

        for d in range(DLOC):
            for h, hs in enumerate(halves):
                WD[d, :, hs] = wind[0, :, hs] * (sgn * COS[d]) + wind[1, :, hs] * (sgn * SIN[d])

        def growth(f, carry):
            slope = tab[1, f]
            sgs = tab[0, f] * sgn
            for d in range(DLOC):
                i = f * DLOC + d
                rows = pl.ds(pl.multiple_of(i * 8, 8), 8)
                for h, hs in enumerate(halves):
                    G[h, rows, :] = 1.0 + jnp.maximum(WD[d, :, hs] * slope - 0.05, 0.0)
                CNT[pl.ds(i, 1), :] = jnp.full((1, 128), sgs * SIN[d], F32)
            return carry

        lax.fori_loop(0, FREQS, growth, 0)

        @pl.when(has_lo)
        def _():
            neighbour(0).wait_recv()

        @pl.when(has_hi)
        def _():
            neighbour(1).wait_recv()

        edge_i = tuple(
            jnp.where(low_rows, NBR[1, 0:8, hs], NBR[0, 0:8, hs]) for hs in halves
        )
        edge_wet = tuple(x.astype(F32) for x in edge_i)
        edge_shift = tuple(
            jnp.where(low_rows, NBR[1, 8:16, hs], NBR[0, 8:16, hs]) for hs in halves
        )

        settle(QR, q_recv)
        fields = []
        for c in range(5):
            parts = []
            for h in range(2):
                acc = jnp.zeros((8, 128), F32)
                for k in range(16):
                    u = 16 * h + k
                    acc = jnp.where((lane >> 3) == (k + c) % 16, QR[pl.ds(8 * u, 8), :], acc)
                parts.append(pltpu.roll(acc, 128 - 8 * c, 1) if c else acc)
            fields.append(tuple(parts))
        left = tuple((256 - x) & 255 for x in shift)
        edge_left = tuple((256 - x) & 255 for x in edge_shift)
        u01 = tuple(0.1 * x for x in barrel(fields[0], left))
        v01 = tuple(0.1 * x for x in barrel(fields[1], left))

        def stiffness(level):
            depth = tuple(10.0 + 4.0 * x for x in level)
            return tuple(25.0 / (x * x) for x in depth)

        stiff = stiffness(barrel(fields[2], left))
        edge_v = tuple(0.1 * x for x in barrel(fields[3], edge_left))
        edge_stiff = stiffness(barrel(fields[4], edge_left))
        v_lo = tuple(jnp.broadcast_to(x[7:8], (8, 128)) for x in edge_v)
        v_hi = tuple(jnp.broadcast_to(x[0:1], (8, 128)) for x in edge_v)

        def halo_in(n, c, scale=None):
            @pl.when(has_lo)
            def _():
                halo(n, 0, c).wait_recv()

            @pl.when(has_hi)
            def _():
                halo(n, 1, c).wait_recv()

            for k in range(RCH // 8):
                rows = pl.ds(pl.multiple_of(c * RCH + 8 * k, 8), 8)
                cn = CNT[rows, :]
                for h in range(2):
                    lower, upper = H[n, 0, h, rows, :], H[n, 1, h, rows, :]
                    if scale is not None:
                        lower, upper = scale[0][h] * lower, scale[1][h] * upper
                    H[n, 0, h, rows, :] = jnp.maximum((cn + v_lo[h]) * lower, 0.0)
                    H[n, 1, h, rows, :] = jnp.minimum((cn + v_hi[h]) * upper, 0.0)

        def terms(n, i, rows, ce, cn, r=None):
            b = [B[h, rows, :] for h in range(2)]
            if r is not None:
                b = [r[h] * b[h] for h in range(2)]
            X = [(u01[h] + ce) * b[h] for h in range(2)]
            Y = [(v01[h] + cn) * b[h] for h in range(2)]
            own = [(b[h] - jnp.abs(X[h])) - jnp.abs(Y[h]) for h in range(2)]
            west, east = [jnp.maximum(x, 0.0) for x in X], [jnp.minimum(x, 0.0) for x in X]
            if r is not None:
                west, east = from_left(west), from_right(east)
            else:
                a = [pltpu.roll(x, 1, 1) for x in west]
                west = [a[0], jnp.where(first_lane, a[0], a[1])]
                a = [pltpu.roll(x, 127, 1) for x in east]
                east = [jnp.where(last_lane, a[1], a[0]), a[1]]
            south = [
                jnp.where(
                    first_row, H[n, 0, h, pl.ds(i, 8, stride=0), :], pltpu.roll(jnp.maximum(Y[h], 0.0), 1, 0)
                )
                for h in range(2)
            ]
            north = [
                jnp.where(
                    last_row, H[n, 1, h, pl.ds(i, 8, stride=0), :], pltpu.roll(jnp.minimum(Y[h], 0.0), 7, 0)
                )
                for h in range(2)
            ]
            return own, west, east, south, north

        def ahead(n):
            def chunk(c, carry):
                halo_in(n, c)

                def band(fc, carry):
                    f = c * FCH + fc
                    sgs = tab[0, f] * sgn
                    for d in range(DLOC):
                        i = f * DLOC + d
                        rows = pl.ds(pl.multiple_of(i * 8, 8), 8)
                        for q, term in enumerate(terms(n, i, rows, sgs * COS[d], sgs * SIN[d])):
                            for h in range(2):
                                PT[q, h, rows, :] = term[h]
                    return carry

                return lax.fori_loop(0, FCH, band, carry)

            lax.fori_loop(0, PCH, chunk, 0)

        def factors(r, edge_r):
            a, b = [pltpu.roll(x, 1, 1) for x in r], [pltpu.roll(x, 127, 1) for x in r]
            r_w = (jnp.where(first_lane, 0.0, a[0]), jnp.where(first_lane, a[0], a[1]))
            r_e = (jnp.where(last_lane, b[1], b[0]), jnp.where(last_lane, 0.0, b[1]))
            r_s = tuple(jnp.where(first_row, pltpu.roll(edge_r[h], 1, 0), pltpu.roll(r[h], 1, 0)) for h in range(2))
            r_n = tuple(jnp.where(last_row, pltpu.roll(edge_r[h], 7, 0), pltpu.roll(r[h], 7, 0)) for h in range(2))
            return tuple(r), r_w, r_e, r_s, r_n

        def sweep(n, r, edge_r, last):
            r_all = factors(r, edge_r)
            scale = (
                tuple(jnp.broadcast_to(x[7:8], (8, 128)) for x in edge_r),
                tuple(jnp.broadcast_to(x[0:1], (8, 128)) for x in edge_r),
            )

            def chunk(c, sums, prepared):
                if not prepared:
                    halo_in(n, c, scale)

                def band(fc, sums):
                    f = c * FCH + fc
                    sgs = tab[0, f] * sgn
                    zero = jnp.zeros((8, 128), F32)
                    acc = [[zero, zero] for _ in range(5 if last else 1)]
                    half_way = {}
                    for d in (DIR_ORDER if last else range(DLOC)):
                        i = f * DLOC + d
                        rows = pl.ds(pl.multiple_of(i * 8, 8), 8)
                        if prepared:
                            five = [[r_all[q][h] * PT[q, h, rows, :] for h in range(2)] for q in range(5)]
                        else:
                            five = terms(n, i, rows, sgs * COS[d], sgs * SIN[d], r)
                        for h in range(2):
                            own, west, east, south, north = (five[q][h] for q in range(5))
                            adv = own + ((west - east) + (south - north))
                            new = adv * G[h, rows, :]
                            B[h, rows, :] = new
                            acc[0][h] += adv
                            if last:
                                mine = (new - adv, new)
                                if h not in half_way:
                                    half_way[h] = mine
                                    continue
                                for q, (a, b) in enumerate(zip(half_way.pop(h), mine)):
                                    acc[1 + 2 * q][h] += (a - b) * COS[DLOC - 1 - d]
                                    acc[2 + 2 * q][h] += (a + b) * SIN[d]
                    weights = [tab[2, f], tab[3, f], tab[3, f], tab[4, f], tab[4, f]]
                    if last:
                        weights = weights[:1] + [w * sgn for w in weights[1:]]
                    return tuple(
                        tuple(total[h] + acc[q][h] * weights[q] for h in range(2)) for q, total in enumerate(sums)
                    )

                sums = lax.fori_loop(0, FCH, band, sums)
                if not last:

                    @pl.when(c < CHUNKS - HELD)
                    def _():
                        edges_out(n + 1, c)

                return sums

            zero = jnp.zeros((8, 128), F32)
            sums = tuple((zero, zero) for _ in range(5 if last else 1))
            begun = PCH if last else jnp.where(n > 0, PCH, 0)
            sums = lax.fori_loop(0, begun, lambda c, x: chunk(c, x, True), sums)
            return lax.fori_loop(begun, CHUNKS, lambda c, x: chunk(c, x, False), sums)

        def total_copies(n):
            return [
                (None, mesh_copy(TS.at[n], TR.at[n, 0], t_send.at[n, 0], t_recv.at[n, 0], {"spec": other})),
                (has_hi, mesh_copy(TS.at[n], TR.at[n, 1], t_send.at[n, 1], t_recv.at[n, 1], {"tile": hi_t})),
                (has_hi, mesh_copy(TS.at[n], TR.at[n, 2], t_send.at[n, 2], t_recv.at[n, 2], {"tile": hi_t, "spec": other})),
                (has_lo, mesh_copy(TS.at[n], TR.at[n, 3], t_send.at[n, 3], t_recv.at[n, 3], {"tile": lo_t})),
                (has_lo, mesh_copy(TS.at[n], TR.at[n, 4], t_send.at[n, 4], t_recv.at[n, 4], {"tile": lo_t, "spec": other})),
            ]

        def gated(condition, action):
            if condition is None:
                action()
            else:
                pl.when(condition)(action)

        def one_step(n, carry):
            r, edge_r = carry
            (total,) = sweep(n, r, edge_r, False)
            for h, hs in enumerate(halves):
                TS[n, :, hs] = total[h]
            copies = total_copies(n)
            for condition, copy in copies:
                gated(condition, copy.start)

            def late(c, carry):
                edges_out(n + 1, c)
                return carry

            lax.fori_loop(CHUNKS - HELD, CHUNKS, late, 0)
            ahead(n + 1)
            for (_, copy), condition in zip(copies, [None, has_lo, has_lo, has_hi, has_hi]):
                gated(condition, copy.wait_recv)
            new_r, new_edge = [], []
            for h, hs in enumerate(halves):
                full = total[h] + TR[n, 0, :, hs]
                new_r.append(wet[h] / (1.0 + stiff[h] * full))
                lower = TR[n, 1, :, hs] + TR[n, 2, :, hs]
                upper = TR[n, 3, :, hs] + TR[n, 4, :, hs]
                edge = jnp.where(low_rows, upper, lower)
                new_edge.append(edge_wet[h] / (1.0 + edge_stiff[h] * edge))
            return tuple(new_r), tuple(new_edge)

        r, edge_r = lax.fori_loop(0, WSTEPS - 1, one_step, (wet, edge_wet))
        n = WSTEPS - 1
        sums = sweep(n, r, edge_r, True)
        for q in range(5):
            put(BANDS, sums[q], slice(8 * q, 8 * q + 8))
        swap = mesh_copy(BANDS, BANDR, t_send.at[n, 0], t_recv.at[n, 0], {"spec": other})
        swap.start()
        swap.wait_recv()
        full = [tuple(sums[q][h] + BANDR[8 * q : 8 * q + 8, halves[h]] for h in range(2)) for q in range(5)]
        breaking = tuple(1.0 / (1.0 + stiff[h] * full[0][h]) for h in range(2))
        final = tuple(wet[h] * breaking[h] for h in range(2))
        bands = []
        for q in range(1, 5):
            scale = breaking if q < 3 else final
            bands.append(circular(barrel(tuple(scale[h] * full[q][h] for h in range(2)), shift), 1))
        bands = [tuple(pltpu.roll(x, 32 * f, 1) if f else x for x in field) for f, field in enumerate(bands)]
        for u in range(TILES):
            MSG2[pl.ds(8 * u, 8), :] = windows(bands, u)

        def send_bands(u, carry):
            to_ocean(MSG2, BR, f_send, f_recv, u).start()
            return carry

        lax.fori_loop(0, TILES, send_bands, 0)

        def store(c):
            rows = pl.ds(pl.multiple_of(c * RCH * 8, 8), RCH * 8)
            return [
                pltpu.make_async_copy(B.at[h, rows, :], out_w.at[rows, hs], load_sem.at[c, h])
                for h, hs in enumerate(halves)
            ]

        def finish(c, carry):
            def scale_f(i, carry):
                for d in range(DLOC):
                    rows = pl.ds(pl.multiple_of((c * RCH + i * DLOC + d) * 8, 8), 8)
                    for h in range(2):
                        B[h, rows, :] = B[h, rows, :] * final[h]
                return carry

            lax.fori_loop(0, FCH, scale_f, 0)
            for copy in store(c):
                copy.start()
            return carry

        lax.fori_loop(0, CHUNKS, finish, 0)
        A2[...] = jnp.zeros((2, 192, 128), F32)
        blanks = [pltpu.make_async_copy(A2.at[h], out_o.at[:, hs], out_sem.at[h]) for h, hs in enumerate(halves)]
        for copy in blanks:
            copy.start()

        def drain(c, carry):
            for copy in store(c):
                copy.wait()

            @pl.when(has_hi)
            def _():
                for n in range(WSTEPS):
                    halo(n, 0, c).wait_send()

            @pl.when(has_lo)
            def _():
                for n in range(WSTEPS):
                    halo(n, 1, c).wait_send()

            return carry

        lax.fori_loop(0, CHUNKS, drain, 0)
        for copy in blanks:
            copy.wait()
        for m in range(WSTEPS - 1):
            for condition, copy in total_copies(m):
                gated(condition, copy.wait_send)
        swap.wait_send()
        gated(has_hi, neighbour(0).wait_send)
        gated(has_lo, neighbour(1).wait_send)
        settle(MMSG, m_send)
        settle(MSG2, f_send)

    @pl.when(grp == 1)
    def circulation():
        top = (1 - sp).astype(F32)
        deep = sp.astype(F32)
        down = jnp.where(sp == 0, 1.0, math.exp(-1.0)).astype(F32)
        loads = [
            pltpu.make_async_copy(ocean_h.at[:, halves[0]], Q.at[0], small_sem.at[0]),
            pltpu.make_async_copy(ocean_h.at[:, halves[1]], Q.at[1], small_sem.at[1]),
            pltpu.make_async_copy(sea_h, sea, small_sem.at[2]),
        ]
        for copy in loads:
            copy.start()
        for copy in loads:
            copy.wait()
        for c in range(2):
            for h, hs in enumerate(halves):
                acc = jnp.zeros((8, 128), F32)
                for k in range(KLOC):
                    acc += Q[h, pl.ds((c * KLOC + k) * 8, 8), :] * float(_wgt[k])
                CS[pl.ds(8 * c, 8), hs] = acc * down
        everyone_in()
        part = mesh_copy(CS, CR, c_send, c_recv, {"spec": other})
        part.start()

        def edge(n, side):
            return mesh_copy(
                ES.at[n, side], EH.at[n, side], e_send.at[n, side], e_recv.at[n, side],
                {"tile": hi_t if side == 0 else lo_t},
            )

        def level(n):
            return mesh_copy(LS.at[n], LH.at[n], l_send.at[n], l_recv.at[n], {"spec": other})

        def rims_out(n, src):
            for c in range(3):
                for h, hs in enumerate(halves):
                    ES[n, 0, pl.ds(8 * c, 8), hs] = src[h, pl.ds(c * 64 + 7, 8, stride=8), :]
                    ES[n, 1, pl.ds(8 * c, 8), hs] = src[h, pl.ds(c * 64, 8, stride=8), :]
                    LS[n, pl.ds(8 * c, 8), hs] = jnp.where(
                        sp == 0, src[h, pl.ds(c * 64 + 56, 8), :], src[h, pl.ds(c * 64, 8), :]
                    )
            pl.when(has_hi)(edge(n, 0).start)
            pl.when(has_lo)(edge(n, 1).start)
            level(n).start()

        SX[...] = jnp.zeros((128, 256), F32)
        put(SX, pair(sea), slice(16, 24))
        part.wait_recv()
        for c in range(2):
            rows = pl.ds(8 * c, 8)
            SX[rows, :] = CS[rows, :] + CR[rows, :]
        ahead_rows = (lane & 7) < 4
        for c in range(2):
            src = tuple(SX[pl.ds(8 + 8 * c, 8), hs] for hs in halves)
            ahead, behind = circular(src, 120), circular(src, 8)
            ahead = (ahead[1], ahead[0])
            put(SX, tuple(jnp.where(ahead_rows, ahead[h], behind[h]) for h in range(2)), slice(24 + 8 * c, 32 + 8 * c))
        for h, hs in enumerate(halves):
            MSG[pl.ds(128 * h, 128), :] = pltpu.roll(SX[:, hs].T, tile * 8 % 128, 1)

        def to_wave(u):
            return mesh_copy(
                MSG.at[pl.ds(pl.multiple_of(u * 8, 8), 8), :],
                QR.at[pl.ds(pl.multiple_of(tile * 8, 8), 8), :],
                q_send, q_recv, {"grp": 0, "tile": u},
            )

        def send_q(u, carry):
            to_wave(u).start()
            return carry

        lax.fori_loop(0, TILES, send_q, 0)
        rims_out(0, Q)

        zbuf[...] = jnp.zeros((RCH * 8, 256), F32)

        def blank(c):
            rows = pl.ds(pl.multiple_of(c * RCH * 8, 8), RCH * 8)
            return pltpu.make_async_copy(zbuf, out_w.at[rows, :], load_sem.at[c, 0])

        def begin(c, carry):
            blank(c).start()
            return carry

        lax.fori_loop(0, CHUNKS, begin, 0)

        @pl.when(jnp.logical_not(has_lo))
        def _():
            EH[:, 0] = jnp.zeros((2, 24, 256), F32)

        @pl.when(jnp.logical_not(has_hi))
        def _():
            EH[:, 1] = jnp.zeros((2, 24, 256), F32)

        at_lo = jnp.where(has_lo, 1.0, 0.0).astype(F32)
        at_hi = jnp.where(has_hi, 1.0, 0.0).astype(F32)

        def arrived(buf, slots):
            for h in range(2):
                turned = buf[pl.ds(128 * h, 128), :].T
                BTS[pl.ds(0, 128), halves[h]] = turned
                BTS[pl.ds(128, 128), halves[h]] = turned
            out = []
            for f in range(slots):
                start = pl.multiple_of((8 * tile + 32 * f) % 128, 8)
                wide = BTS[pl.ds(start, 16), :]
                out.append(tuple((wide[0:8, hs], wide[1:9, hs], wide[2:10, hs]) for hs in halves))
            return out

        settle(MR, m_recv)
        (mask3,) = arrived(MR, 1)
        mask = tuple(x[1] for x in mask3)
        mask_lo = tuple(jnp.where(first_row, x[0] * at_lo, x[0]) for x in mask3)
        mask_hi = tuple(jnp.where(last_row, x[2] * at_hi, x[2]) for x in mask3)

        def lateral(x, lower, upper):
            left, right = from_left(x), from_right(x)
            return tuple(lower[h] + upper[h] + left[h] + right[h] - 4.0 * x[h] for h in range(2))

        def substep(n, src, dst):
            for c in range(3):
                for k in range(KLOC):
                    at = (c * KLOC + k) * 8
                    x = tuple(src[h, pl.ds(at, 8), :] for h in range(2))
                    row_at = 8 * c + k
                    lower = tuple(
                        jnp.where(first_row, EH[n, 0, row_at : row_at + 1, hs], pltpu.roll(x[h], 1, 0))
                        for h, hs in enumerate(halves)
                    )
                    upper = tuple(
                        jnp.where(last_row, EH[n, 1, row_at : row_at + 1, hs], pltpu.roll(x[h], 7, 0))
                        for h, hs in enumerate(halves)
                    )
                    side = lateral(x, lower, upper)
                    for h, hs in enumerate(halves):
                        if k > 0:
                            above = src[h, pl.ds(at - 8, 8), :]
                        else:
                            above = LH[n, pl.ds(8 * c, 8), hs] * deep
                        if k < KLOC - 1:
                            below = src[h, pl.ds(at + 8, 8), :]
                        else:
                            below = LH[n, pl.ds(8 * c, 8), hs] * top
                        value = x[h] + 0.1 * side[h] + 0.2 * (above + below - 2.0 * x[h])
                        if c == 0:
                            value = value + 0.1 * src[h, pl.ds(at + 64, 8), :]
                        if c == 1:
                            value = value - 0.1 * src[h, pl.ds(at - 64, 8), :]
                        dst[h, pl.ds(at, 8), :] = value * mask[h]

        def rims_in(n):
            pl.when(has_lo)(edge(n, 0).wait_recv)
            pl.when(has_hi)(edge(n, 1).wait_recv)
            level(n).wait_recv()

        rims_in(0)
        substep(0, Q, A1)
        rims_out(1, A1)
        rims_in(1)
        substep(1, A1, A2)

        settle(BR, f_recv)
        forced, spread = [], []
        for f, three in enumerate(arrived(BR, 4)):
            lower = tuple(three[h][0] * mask_lo[h] for h in range(2))
            own = tuple(three[h][1] * mask[h] for h in range(2))
            upper = tuple(three[h][2] * mask_hi[h] for h in range(2))
            forced.append(own)
            spread.append(lateral(own, lower, upper))
        for k in range(KLOC):
            near, far = math.exp(0.125), math.exp(-0.125)
            prof = float(_prof[k]) * down
            above = near if k > 0 else near * deep
            below = far if k < KLOC - 1 else far * top
            stay = prof * (1.0 + 0.2 * (above + below - 2.0))
            for h, hs in enumerate(halves):
                east = (0.1 * prof) * forced[3][h]
                north = (-0.1 * prof) * forced[2][h]
                d_east = (0.1 * stay) * forced[3][h] + (0.01 * prof) * spread[3][h]
                d_north = (-0.1 * stay) * forced[2][h] - (0.01 * prof) * spread[2][h]
                if k == 0:
                    east = east + top * forced[0][h]
                    north = north + top * forced[1][h]
                    d_east = d_east + top * (0.6 * forced[0][h] + 0.1 * spread[0][h])
                    d_north = d_north + top * (0.6 * forced[1][h] + 0.1 * spread[1][h])
                if k == 1:
                    d_east = d_east + (0.2 * top) * forced[0][h]
                    d_north = d_north + (0.2 * top) * forced[1][h]
                A2[h, pl.ds(8 * k, 8), :] += mask[h] * (d_east + 0.1 * north) + east
                A2[h, pl.ds(64 + 8 * k, 8), :] += mask[h] * (d_north - 0.1 * east) + north
        results = [pltpu.make_async_copy(A2.at[h], out_o.at[:, hs], out_sem.at[h]) for h, hs in enumerate(halves)]
        for copy in results:
            copy.start()

        def drain(c, carry):
            blank(c).wait()
            return carry

        lax.fori_loop(0, CHUNKS, drain, 0)
        part.wait_send()
        for n in range(2):
            pl.when(has_hi)(edge(n, 0).wait_send)
            pl.when(has_lo)(edge(n, 1).wait_send)
            level(n).wait_send()
        settle(MSG, q_send)
        for copy in results:
            copy.wait()


def body(spectrum, wind, land_mask, intersection, ocean_state, sea_level):
    v = lambda *shape, dtype=F32: pltpu.VMEM(shape, dtype)
    dma = lambda *shape: pltpu.SemaphoreType.DMA(shape) if shape else pltpu.SemaphoreType.DMA
    anywhere = pl.BlockSpec(memory_space=pltpu.HBM)
    scratch = [
        pltpu.SMEM(TABLE.shape, F32),
        v(2, FD * 8, 128), v(2, FD * 8, 128), v(5, 2, PCH * RCH * 8, 128), v(DLOC, 8, 256), v(FD, 128),
        v(WSTEPS, 2, 2, FD, 128), v(WSTEPS, 2, 2, FD, 128),
        v(2, 8, 256), v(8, 256, dtype=jnp.int32), v(8, 256, dtype=jnp.int32),
        v(16, 256, dtype=jnp.int32), v(2, 16, 256, dtype=jnp.int32),
        v(256, 128), v(WSTEPS, 8, 256), v(WSTEPS, 5, 8, 256), v(40, 256), v(40, 256), v(256, 128), v(256, 128),
        v(2, 192, 128), v(2, 192, 128), v(2, 192, 128), v(8, 256), v(16, 256), v(16, 256), v(128, 256),
        v(256, 128), v(256, 128), v(256, 128), v(256, 256),
        v(2, 2, 24, 256), v(2, 2, 24, 256), v(2, 24, 256), v(2, 24, 256), v(RCH * 8, 256),
        dma(CHUNKS, 2), dma(3), dma(WSTEPS, 2, CHUNKS), dma(WSTEPS, 2, CHUNKS), dma(WSTEPS, 5), dma(WSTEPS, 5),
        dma(2), dma(2), dma(), dma(), dma(), dma(), dma(), dma(), dma(), dma(),
        dma(2, 2), dma(2, 2), dma(2), dma(2), dma(2),
    ]
    waves, ocean = pl.pallas_call(
        kernel,
        out_shape=(
            jax.ShapeDtypeStruct((FD * 8, 256), F32),
            jax.ShapeDtypeStruct((192, 256), F32),
        ),
        in_specs=[anywhere] * 6,
        out_specs=(anywhere, anywhere),
        scratch_shapes=scratch,
        compiler_params=pltpu.CompilerParams(collective_id=0, has_side_effects=True, vmem_limit_bytes=48 << 20),
    )(
        *(
            pltpu.with_memory_space_constraint(x, pltpu.HBM)
            for x in (
                spectrum.reshape(FD * 8, 256),
                wind,
                land_mask,
                intersection,
                ocean_state.reshape(192, 256),
                sea_level.reshape(8, 256),
            )
        )
    )
    return waves.reshape(spectrum.shape), ocean.reshape(ocean_state.shape)


def solution(mesh):
    return jax.shard_map(
        body,
        mesh=mesh,
        in_specs=(
            P("grp", None, "spec", "tile", None),
            P(None, "tile", None),
            P("tile", None),
            P("tile", None),
            P("grp", None, "spec", "tile", None),
            P("grp", "tile", None),
        ),
        out_specs=(P("grp", None, "spec", "tile", None), P("grp", None, "spec", "tile", None)),
        check_vma=False,
    )
```

```python
import math

import jax
import jax.numpy as jnp
import numpy as np
from jax import lax
from jax.experimental import pallas as pl
from jax.experimental.pallas import tpu as pltpu
from jax.sharding import PartitionSpec as P

FREQS = 32
DIRS = 36
LEVELS = 16
WSTEPS = 4
TILES = 32
DLOC = 18
KLOC = 8
FD = FREQS * DLOC
CHUNKS = 8
FCH = FREQS // CHUNKS
RCH = FCH * DLOC
PCH = 5
HELD = 3
F32 = jnp.float32

_freq = 0.04 * 1.1 ** np.arange(FREQS)
_cel = 1.56 / _freq
_gs = 0.4 * 1.1 ** (-np.arange(FREQS, dtype=np.float64))
_bw = 0.1 * _freq * (2.0 * math.pi / DIRS)
TABLE = np.stack([_gs, 0.05 / _cel, _bw, 5.0 * _bw / _cel, 20.0 * _bw * _freq**3]).astype(np.float32)
_ang = 2.0 * math.pi * (np.arange(DIRS) + 0.5) / DIRS
COS = [float(np.float32(x)) for x in np.cos(_ang)[:DLOC]]
SIN = [float(np.float32(x)) for x in np.sin(_ang)[:DLOC]]
DIR_ORDER = [d for k in range(DLOC // 2) for d in (k, DLOC - 1 - k)]
_prof = np.exp(-2.0 * (np.arange(LEVELS) + 0.5) / LEVELS)
_wgt = _prof / _prof.sum()


def mesh_copy(src, dst, send, recv, where):
    return pltpu.make_async_remote_copy(
        src_ref=src,
        dst_ref=dst,
        send_sem=send,
        recv_sem=recv,
        device_id=where,
        device_id_type=pl.DeviceIdType.MESH,
    )


def settle(buf, sem):
    pltpu.make_async_copy(buf, buf, sem).wait()


HALVES = (slice(0, 128), slice(128, 256))


def at_lane(k):
    return lax.broadcasted_iota(jnp.int32, (8, 128), 1) == k


def from_left(x):
    a, b = pltpu.roll(x[0], 1, 1), pltpu.roll(x[1], 1, 1)
    return jnp.where(at_lane(0), 0.0, a), jnp.where(at_lane(0), a, b)


def from_right(x):
    a, b = pltpu.roll(x[0], 127, 1), pltpu.roll(x[1], 127, 1)
    return jnp.where(at_lane(127), b, a), jnp.where(at_lane(127), 0.0, b)


def lateral(x, lower, upper):
    left, right = from_left(x), from_right(x)
    return tuple(lower[h] + upper[h] + left[h] + right[h] - 4.0 * x[h] for h in range(2))


def arrived(buf, BTS, tile, slots):
    for h in range(2):
        turned = buf[pl.ds(128 * h, 128), :].T
        BTS[pl.ds(0, 128), HALVES[h]] = turned
        BTS[pl.ds(128, 128), HALVES[h]] = turned
    out = []
    for f in range(slots):
        start = pl.multiple_of((8 * tile + 32 * f) % 128, 8)
        wide = BTS[pl.ds(start, 16), :]
        out.append(tuple((wide[0:8, hs], wide[1:9, hs], wide[2:10, hs]) for hs in HALVES))
    return out


def kernel(
    spec_h, wind_h, land_h, inter_h, ocean_h, sea_h, out_w, out_o, BR, out_m,
    tab, B, G, PT, WD, CNT, H, S, wind, land, inter, NBS, NBR, QR, TS, TR, BANDS, BANDR, MSG2, MMSG,
    Q, A1, A2, sea, CS, CR, SX, MSG, MR, BTS, ES, EH, LS, LH,
    load_sem, small_sem, h_send, h_recv, t_send, t_recv, nb_send, nb_recv,
    q_send, q_recv, m_send, m_recv, f_send, f_recv, c_send, c_recv, e_send, e_recv, l_send, l_recv, out_sem,
):
    grp = lax.axis_index("grp")
    tile = lax.axis_index("tile")
    sp = lax.axis_index("spec")
    other = 1 - sp
    sgn = (1 - 2 * sp).astype(F32)
    has_lo = tile > 0
    has_hi = tile < TILES - 1
    lo_t = jnp.maximum(tile - 1, 0)
    hi_t = jnp.minimum(tile + 1, TILES - 1)
    lane = lax.broadcasted_iota(jnp.int32, (8, 128), 1)
    row = lax.broadcasted_iota(jnp.int32, (8, 128), 0)
    first_lane, last_lane = lane == 0, lane == 127
    first_row, last_row = row == 0, row == 7
    low_rows = row < 4
    halves = HALVES

    def circular(x, shift):
        a, b = pltpu.roll(x[0], shift, 1), pltpu.roll(x[1], shift, 1)
        m = lane < shift
        return jnp.where(m, b, a), jnp.where(m, a, b)

    def barrel(x, amount):
        for bit in range(8):
            moved = circular(x, 1 << bit) if bit < 7 else (x[1], x[0])
            x = tuple(jnp.where((amount[h] & (1 << bit)) != 0, moved[h], x[h]) for h in range(2))
        return x

    def pair(ref, *lead):
        return tuple(ref[(*lead, slice(None), hs)] for hs in halves)

    def put(ref, value, rows):
        for h in range(2):
            ref[rows, halves[h]] = value[h]

    barrier = pltpu.get_barrier_semaphore()

    def greet(where):
        pl.semaphore_signal(barrier, 1, device_id=where, device_id_type=pl.DeviceIdType.MESH)

    greet({"spec": other})

    @pl.when(has_lo)
    def _():
        greet({"tile": lo_t})
        greet({"tile": lo_t, "spec": other})

    @pl.when(has_hi)
    def _():
        greet({"tile": hi_t})
        greet({"tile": hi_t, "spec": other})

    def greet_across(u, carry):
        greet({"grp": 1 - grp, "tile": u})
        return carry

    lax.fori_loop(0, TILES, greet_across, 0)
    beside = jnp.where(has_lo, 2, 0) + jnp.where(has_hi, 2, 0)

    def everyone_in():
        pl.semaphore_wait(barrier, TILES + 1 + beside)

    @pl.when(grp == 0)
    def wave():
        def load(c):
            rows = pl.ds(pl.multiple_of(c * RCH * 8, 8), RCH * 8)
            return [
                pltpu.make_async_copy(spec_h.at[rows, hs], B.at[h, rows, :], load_sem.at[c, h])
                for h, hs in enumerate(halves)
            ]

        smalls = [
            pltpu.make_async_copy(wind_h, wind, small_sem.at[0]),
            pltpu.make_async_copy(land_h, land, small_sem.at[1]),
            pltpu.make_async_copy(inter_h, inter, small_sem.at[2]),
        ]
        for copy in smalls:
            copy.start()
        for q in range(TABLE.shape[0]):
            for f in range(FREQS):
                tab[q, f] = float(TABLE[q, f])

        def begin(c, carry):
            for copy in load(c):
                copy.start()
            return carry

        lax.fori_loop(0, CHUNKS, begin, 0)

        def halo(n, side, c):
            rows = pl.ds(pl.multiple_of(c * RCH, 8), RCH)
            return mesh_copy(
                S.at[n, side, :, rows, :], H.at[n, side, :, rows, :], h_send.at[n, side, c], h_recv.at[n, side, c],
                {"tile": hi_t if side == 0 else lo_t},
            )

        def edges_out(n, c):
            for k in range(RCH // 8):
                at = c * RCH + 8 * k
                rows = pl.ds(pl.multiple_of(at, 8), 8)
                for h in range(2):
                    S[n, 0, h, rows, :] = B[h, pl.ds(at * 8 + 7, 8, stride=8), :]
                    S[n, 1, h, rows, :] = B[h, pl.ds(at * 8, 8, stride=8), :]

            @pl.when(has_hi)
            def _():
                halo(n, 0, c).start()

            @pl.when(has_lo)
            def _():
                halo(n, 1, c).start()

        for copy in smalls:
            copy.wait()
        wet_i = pair(land)
        wet = tuple(x.astype(F32) for x in wet_i)
        shift = tuple((x - lane - 128 * h) & 255 for h, x in enumerate(pair(inter)))
        put(NBS, wet_i, slice(0, 8))
        put(NBS, shift, slice(8, 16))

        def neighbour(side):
            return mesh_copy(
                NBS, NBR.at[side], nb_send.at[side], nb_recv.at[side],
                {"tile": hi_t if side == 0 else lo_t},
            )

        everyone_in()

        @pl.when(has_hi)
        def _():
            neighbour(0).start()

        @pl.when(has_lo)
        def _():
            neighbour(1).start()

        wet_back = circular(barrel(wet, shift), 1)

        def windows(fields, u):
            acc = jnp.zeros((8, 128), F32)
            for f, field in enumerate(fields):
                start = (8 * u + 32 * f) % 128
                offset = (lane - start) & 127
                inside = offset < 10
                base = (8 * u) // 128
                p = 8 * u + offset
                value = field[base]
                if 8 * u % 128 + 10 > 128:
                    turned = (lane - 32 * f) & 127
                    value = jnp.where(turned < 16, field[1 - base], value)
                acc = jnp.where(inside, value, acc)
            return acc

        for u in range(TILES):
            MMSG[pl.ds(8 * u, 8), :] = windows([wet_back], u)

        def to_ocean(src, dst, send, recv, u):
            return mesh_copy(
                src.at[pl.ds(pl.multiple_of(u * 8, 8), 8), :],
                dst.at[pl.ds(pl.multiple_of(tile * 8, 8), 8), :],
                send, recv, {"grp": 1, "tile": u},
            )

        def send_mask(u, carry):
            to_ocean(MMSG, MR, m_send, m_recv, u).start()
            return carry

        lax.fori_loop(0, TILES, send_mask, 0)

        @pl.when(jnp.logical_not(has_lo))
        def _():
            H[:, 0] = jnp.zeros((WSTEPS, 2, FD, 128), F32)
            NBR[0] = jnp.zeros((16, 256), jnp.int32)
            TR[:, 1:3] = jnp.zeros((WSTEPS, 2, 8, 256), F32)

        @pl.when(jnp.logical_not(has_hi))
        def _():
            H[:, 1] = jnp.zeros((WSTEPS, 2, FD, 128), F32)
            NBR[1] = jnp.zeros((16, 256), jnp.int32)
            TR[:, 3:5] = jnp.zeros((WSTEPS, 2, 8, 256), F32)

        def first_edges(c, carry):
            for copy in load(c):
                copy.wait()
            edges_out(0, c)
            return carry

        lax.fori_loop(0, CHUNKS, first_edges, 0)

        for d in range(DLOC):
            for h, hs in enumerate(halves):
                WD[d, :, hs] = wind[0, :, hs] * (sgn * COS[d]) + wind[1, :, hs] * (sgn * SIN[d])

        def growth(f, carry):
            slope = tab[1, f]
            sgs = tab[0, f] * sgn
            for d in range(DLOC):
                i = f * DLOC + d
                rows = pl.ds(pl.multiple_of(i * 8, 8), 8)
                for h, hs in enumerate(halves):
                    G[h, rows, :] = 1.0 + jnp.maximum(WD[d, :, hs] * slope - 0.05, 0.0)
                CNT[pl.ds(i, 1), :] = jnp.full((1, 128), sgs * SIN[d], F32)
            return carry

        lax.fori_loop(0, FREQS, growth, 0)

        @pl.when(has_lo)
        def _():
            neighbour(0).wait_recv()

        @pl.when(has_hi)
        def _():
            neighbour(1).wait_recv()

        edge_i = tuple(
            jnp.where(low_rows, NBR[1, 0:8, hs], NBR[0, 0:8, hs]) for hs in halves
        )
        edge_wet = tuple(x.astype(F32) for x in edge_i)
        edge_shift = tuple(
            jnp.where(low_rows, NBR[1, 8:16, hs], NBR[0, 8:16, hs]) for hs in halves
        )

        settle(QR, q_recv)
        fields = []
        for c in range(5):
            parts = []
            for h in range(2):
                acc = jnp.zeros((8, 128), F32)
                for k in range(16):
                    u = 16 * h + k
                    acc = jnp.where((lane >> 3) == (k + c) % 16, QR[pl.ds(8 * u, 8), :], acc)
                parts.append(pltpu.roll(acc, 128 - 8 * c, 1) if c else acc)
            fields.append(tuple(parts))
        left = tuple((256 - x) & 255 for x in shift)
        edge_left = tuple((256 - x) & 255 for x in edge_shift)
        u01 = tuple(0.1 * x for x in barrel(fields[0], left))
        v01 = tuple(0.1 * x for x in barrel(fields[1], left))

        def stiffness(level):
            depth = tuple(10.0 + 4.0 * x for x in level)
            return tuple(25.0 / (x * x) for x in depth)

        stiff = stiffness(barrel(fields[2], left))
        edge_v = tuple(0.1 * x for x in barrel(fields[3], edge_left))
        edge_stiff = stiffness(barrel(fields[4], edge_left))
        v_lo = tuple(jnp.broadcast_to(x[7:8], (8, 128)) for x in edge_v)
        v_hi = tuple(jnp.broadcast_to(x[0:1], (8, 128)) for x in edge_v)

        def halo_in(n, c, scale=None):
            @pl.when(has_lo)
            def _():
                halo(n, 0, c).wait_recv()

            @pl.when(has_hi)
            def _():
                halo(n, 1, c).wait_recv()

            for k in range(RCH // 8):
                rows = pl.ds(pl.multiple_of(c * RCH + 8 * k, 8), 8)
                cn = CNT[rows, :]
                for h in range(2):
                    lower, upper = H[n, 0, h, rows, :], H[n, 1, h, rows, :]
                    if scale is not None:
                        lower, upper = scale[0][h] * lower, scale[1][h] * upper
                    H[n, 0, h, rows, :] = jnp.maximum((cn + v_lo[h]) * lower, 0.0)
                    H[n, 1, h, rows, :] = jnp.minimum((cn + v_hi[h]) * upper, 0.0)

        def terms(n, i, rows, ce, cn, r=None):
            b = [B[h, rows, :] for h in range(2)]
            if r is not None:
                b = [r[h] * b[h] for h in range(2)]
            X = [(u01[h] + ce) * b[h] for h in range(2)]
            Y = [(v01[h] + cn) * b[h] for h in range(2)]
            own = [(b[h] - jnp.abs(X[h])) - jnp.abs(Y[h]) for h in range(2)]
            west, east = [jnp.maximum(x, 0.0) for x in X], [jnp.minimum(x, 0.0) for x in X]
            if r is not None:
                west, east = from_left(west), from_right(east)
            else:
                a = [pltpu.roll(x, 1, 1) for x in west]
                west = [a[0], jnp.where(first_lane, a[0], a[1])]
                a = [pltpu.roll(x, 127, 1) for x in east]
                east = [jnp.where(last_lane, a[1], a[0]), a[1]]
            south = [
                jnp.where(
                    first_row, H[n, 0, h, pl.ds(i, 8, stride=0), :], pltpu.roll(jnp.maximum(Y[h], 0.0), 1, 0)
                )
                for h in range(2)
            ]
            north = [
                jnp.where(
                    last_row, H[n, 1, h, pl.ds(i, 8, stride=0), :], pltpu.roll(jnp.minimum(Y[h], 0.0), 7, 0)
                )
                for h in range(2)
            ]
            return own, west, east, south, north

        def ahead(n):
            def chunk(c, carry):
                halo_in(n, c)

                def band(fc, carry):
                    f = c * FCH + fc
                    sgs = tab[0, f] * sgn
                    for d in range(DLOC):
                        i = f * DLOC + d
                        rows = pl.ds(pl.multiple_of(i * 8, 8), 8)
                        for q, term in enumerate(terms(n, i, rows, sgs * COS[d], sgs * SIN[d])):
                            for h in range(2):
                                PT[q, h, rows, :] = term[h]
                    return carry

                return lax.fori_loop(0, FCH, band, carry, unroll=2)

            lax.fori_loop(0, PCH, chunk, 0)

        def factors(r, edge_r):
            a, b = [pltpu.roll(x, 1, 1) for x in r], [pltpu.roll(x, 127, 1) for x in r]
            r_w = (jnp.where(first_lane, 0.0, a[0]), jnp.where(first_lane, a[0], a[1]))
            r_e = (jnp.where(last_lane, b[1], b[0]), jnp.where(last_lane, 0.0, b[1]))
            r_s = tuple(jnp.where(first_row, pltpu.roll(edge_r[h], 1, 0), pltpu.roll(r[h], 1, 0)) for h in range(2))
            r_n = tuple(jnp.where(last_row, pltpu.roll(edge_r[h], 7, 0), pltpu.roll(r[h], 7, 0)) for h in range(2))
            return tuple(r), r_w, r_e, r_s, r_n

        def sweep(n, r, edge_r, last):
            r_all = factors(r, edge_r)
            scale = (
                tuple(jnp.broadcast_to(x[7:8], (8, 128)) for x in edge_r),
                tuple(jnp.broadcast_to(x[0:1], (8, 128)) for x in edge_r),
            )

            def chunk(c, sums, prepared):
                if not prepared:
                    halo_in(n, c, scale)

                def band(fc, sums):
                    f = c * FCH + fc
                    sgs = tab[0, f] * sgn
                    zero = jnp.zeros((8, 128), F32)
                    acc = [[zero, zero] for _ in range(5 if last else 1)]
                    half_way = {}
                    for d in (DIR_ORDER if last else range(DLOC)):
                        i = f * DLOC + d
                        rows = pl.ds(pl.multiple_of(i * 8, 8), 8)
                        if prepared:
                            five = [[r_all[q][h] * PT[q, h, rows, :] for h in range(2)] for q in range(5)]
                        else:
                            five = terms(n, i, rows, sgs * COS[d], sgs * SIN[d], r)
                        for h in range(2):
                            own, west, east, south, north = (five[q][h] for q in range(5))
                            adv = own + ((west - east) + (south - north))
                            new = adv * G[h, rows, :]
                            B[h, rows, :] = new
                            acc[0][h] += adv
                            if last:
                                mine = (new - adv, new)
                                if h not in half_way:
                                    half_way[h] = mine
                                    continue
                                for q, (a, b) in enumerate(zip(half_way.pop(h), mine)):
                                    acc[1 + 2 * q][h] += (a - b) * COS[DLOC - 1 - d]
                                    acc[2 + 2 * q][h] += (a + b) * SIN[d]
                    weights = [tab[2, f], tab[3, f], tab[3, f], tab[4, f], tab[4, f]]
                    if last:
                        weights = weights[:1] + [w * sgn for w in weights[1:]]
                    return tuple(
                        tuple(total[h] + acc[q][h] * weights[q] for h in range(2)) for q, total in enumerate(sums)
                    )

                sums = lax.fori_loop(0, FCH, band, sums, unroll=2)
                if not last:

                    @pl.when(c < CHUNKS - HELD)
                    def _():
                        edges_out(n + 1, c)

                return sums

            zero = jnp.zeros((8, 128), F32)
            sums = tuple((zero, zero) for _ in range(5 if last else 1))
            begun = PCH if last else jnp.where(n > 0, PCH, 0)
            sums = lax.fori_loop(0, begun, lambda c, x: chunk(c, x, True), sums)
            return lax.fori_loop(begun, CHUNKS, lambda c, x: chunk(c, x, False), sums)

        def total_copies(n):
            return [
                (None, mesh_copy(TS.at[n], TR.at[n, 0], t_send.at[n, 0], t_recv.at[n, 0], {"spec": other})),
                (has_hi, mesh_copy(TS.at[n], TR.at[n, 1], t_send.at[n, 1], t_recv.at[n, 1], {"tile": hi_t})),
                (has_hi, mesh_copy(TS.at[n], TR.at[n, 2], t_send.at[n, 2], t_recv.at[n, 2], {"tile": hi_t, "spec": other})),
                (has_lo, mesh_copy(TS.at[n], TR.at[n, 3], t_send.at[n, 3], t_recv.at[n, 3], {"tile": lo_t})),
                (has_lo, mesh_copy(TS.at[n], TR.at[n, 4], t_send.at[n, 4], t_recv.at[n, 4], {"tile": lo_t, "spec": other})),
            ]

        def gated(condition, action):
            if condition is None:
                action()
            else:
                pl.when(condition)(action)

        def one_step(n, carry):
            r, edge_r = carry
            (total,) = sweep(n, r, edge_r, False)
            for h, hs in enumerate(halves):
                TS[n, :, hs] = total[h]
            copies = total_copies(n)
            for condition, copy in copies:
                gated(condition, copy.start)

            def late(c, carry):
                edges_out(n + 1, c)
                return carry

            lax.fori_loop(CHUNKS - HELD, CHUNKS, late, 0)
            ahead(n + 1)
            for (_, copy), condition in zip(copies, [None, has_lo, has_lo, has_hi, has_hi]):
                gated(condition, copy.wait_recv)
            new_r, new_edge = [], []
            for h, hs in enumerate(halves):
                full = total[h] + TR[n, 0, :, hs]
                new_r.append(wet[h] / (1.0 + stiff[h] * full))
                lower = TR[n, 1, :, hs] + TR[n, 2, :, hs]
                upper = TR[n, 3, :, hs] + TR[n, 4, :, hs]
                edge = jnp.where(low_rows, upper, lower)
                new_edge.append(edge_wet[h] / (1.0 + edge_stiff[h] * edge))
            return tuple(new_r), tuple(new_edge)

        r, edge_r = lax.fori_loop(0, WSTEPS - 1, one_step, (wet, edge_wet))
        n = WSTEPS - 1
        sums = sweep(n, r, edge_r, True)
        for q in range(5):
            put(BANDS, sums[q], slice(8 * q, 8 * q + 8))
        swap = mesh_copy(BANDS, BANDR, t_send.at[n, 0], t_recv.at[n, 0], {"spec": other})
        swap.start()
        swap.wait_recv()
        full = [tuple(sums[q][h] + BANDR[8 * q : 8 * q + 8, halves[h]] for h in range(2)) for q in range(5)]
        breaking = tuple(1.0 / (1.0 + stiff[h] * full[0][h]) for h in range(2))
        final = tuple(wet[h] * breaking[h] for h in range(2))
        bands = []
        for q in range(1, 5):
            scale = breaking if q < 3 else final
            bands.append(circular(barrel(tuple(scale[h] * full[q][h] for h in range(2)), shift), 1))
        bands = [tuple(pltpu.roll(x, 32 * f, 1) if f else x for x in field) for f, field in enumerate(bands)]
        for u in range(TILES):
            MSG2[pl.ds(8 * u, 8), :] = windows(bands, u)

        def send_bands(u, carry):
            to_ocean(MSG2, BR, f_send, f_recv, u).start()
            return carry

        lax.fori_loop(0, TILES, send_bands, 0)

        def store(c):
            rows = pl.ds(pl.multiple_of(c * RCH * 8, 8), RCH * 8)
            return [
                pltpu.make_async_copy(B.at[h, rows, :], out_w.at[rows, hs], load_sem.at[c, h])
                for h, hs in enumerate(halves)
            ]

        def finish(c, carry):
            def scale_f(i, carry):
                for d in range(DLOC):
                    rows = pl.ds(pl.multiple_of((c * RCH + i * DLOC + d) * 8, 8), 8)
                    for h in range(2):
                        B[h, rows, :] = B[h, rows, :] * final[h]
                return carry

            lax.fori_loop(0, FCH, scale_f, 0)
            for copy in store(c):
                copy.start()
            return carry

        lax.fori_loop(0, CHUNKS, finish, 0)
        def drain(c, carry):
            for copy in store(c):
                copy.wait()

            @pl.when(has_hi)
            def _():
                for n in range(WSTEPS):
                    halo(n, 0, c).wait_send()

            @pl.when(has_lo)
            def _():
                for n in range(WSTEPS):
                    halo(n, 1, c).wait_send()

            return carry

        lax.fori_loop(0, CHUNKS, drain, 0)
        for m in range(WSTEPS - 1):
            for condition, copy in total_copies(m):
                gated(condition, copy.wait_send)
        swap.wait_send()
        gated(has_hi, neighbour(0).wait_send)
        gated(has_lo, neighbour(1).wait_send)
        settle(MMSG, m_send)
        settle(MSG2, f_send)

    @pl.when(grp == 1)
    def circulation():
        top = (1 - sp).astype(F32)
        deep = sp.astype(F32)
        down = jnp.where(sp == 0, 1.0, math.exp(-1.0)).astype(F32)
        loads = [
            pltpu.make_async_copy(ocean_h.at[:, halves[0]], Q.at[0], small_sem.at[0]),
            pltpu.make_async_copy(ocean_h.at[:, halves[1]], Q.at[1], small_sem.at[1]),
            pltpu.make_async_copy(sea_h, sea, small_sem.at[2]),
        ]
        for copy in loads:
            copy.start()
        for copy in loads:
            copy.wait()
        for c in range(2):
            for h, hs in enumerate(halves):
                acc = jnp.zeros((8, 128), F32)
                for k in range(KLOC):
                    acc += Q[h, pl.ds((c * KLOC + k) * 8, 8), :] * float(_wgt[k])
                CS[pl.ds(8 * c, 8), hs] = acc * down
        everyone_in()
        part = mesh_copy(CS, CR, c_send, c_recv, {"spec": other})
        part.start()

        def edge(n, side):
            return mesh_copy(
                ES.at[n, side], EH.at[n, side], e_send.at[n, side], e_recv.at[n, side],
                {"tile": hi_t if side == 0 else lo_t},
            )

        def level(n):
            return mesh_copy(LS.at[n], LH.at[n], l_send.at[n], l_recv.at[n], {"spec": other})

        def rims_out(n, src):
            for c in range(3):
                for h, hs in enumerate(halves):
                    ES[n, 0, pl.ds(8 * c, 8), hs] = src[h, pl.ds(c * 64 + 7, 8, stride=8), :]
                    ES[n, 1, pl.ds(8 * c, 8), hs] = src[h, pl.ds(c * 64, 8, stride=8), :]
                    LS[n, pl.ds(8 * c, 8), hs] = jnp.where(
                        sp == 0, src[h, pl.ds(c * 64 + 56, 8), :], src[h, pl.ds(c * 64, 8), :]
                    )
            pl.when(has_hi)(edge(n, 0).start)
            pl.when(has_lo)(edge(n, 1).start)
            level(n).start()

        SX[...] = jnp.zeros((128, 256), F32)
        put(SX, pair(sea), slice(16, 24))
        part.wait_recv()
        for c in range(2):
            rows = pl.ds(8 * c, 8)
            SX[rows, :] = CS[rows, :] + CR[rows, :]
        ahead_rows = (lane & 7) < 4
        for c in range(2):
            src = tuple(SX[pl.ds(8 + 8 * c, 8), hs] for hs in halves)
            ahead, behind = circular(src, 120), circular(src, 8)
            ahead = (ahead[1], ahead[0])
            put(SX, tuple(jnp.where(ahead_rows, ahead[h], behind[h]) for h in range(2)), slice(24 + 8 * c, 32 + 8 * c))
        for h, hs in enumerate(halves):
            MSG[pl.ds(128 * h, 128), :] = pltpu.roll(SX[:, hs].T, tile * 8 % 128, 1)

        def to_wave(u):
            return mesh_copy(
                MSG.at[pl.ds(pl.multiple_of(u * 8, 8), 8), :],
                QR.at[pl.ds(pl.multiple_of(tile * 8, 8), 8), :],
                q_send, q_recv, {"grp": 0, "tile": u},
            )

        def send_q(u, carry):
            to_wave(u).start()
            return carry

        lax.fori_loop(0, TILES, send_q, 0)
        rims_out(0, Q)

        @pl.when(jnp.logical_not(has_lo))
        def _():
            EH[:, 0] = jnp.zeros((2, 24, 256), F32)

        @pl.when(jnp.logical_not(has_hi))
        def _():
            EH[:, 1] = jnp.zeros((2, 24, 256), F32)

        settle(MR, m_recv)
        flags = pltpu.make_async_copy(MR, out_m, small_sem.at[0])
        flags.start()
        (mask3,) = arrived(MR, BTS, tile, 1)
        mask = tuple(x[1] for x in mask3)

        def substep(n, src, dst):
            for c in range(3):
                for k in range(KLOC):
                    at = (c * KLOC + k) * 8
                    x = tuple(src[h, pl.ds(at, 8), :] for h in range(2))
                    row_at = 8 * c + k
                    lower = tuple(
                        jnp.where(first_row, EH[n, 0, row_at : row_at + 1, hs], pltpu.roll(x[h], 1, 0))
                        for h, hs in enumerate(halves)
                    )
                    upper = tuple(
                        jnp.where(last_row, EH[n, 1, row_at : row_at + 1, hs], pltpu.roll(x[h], 7, 0))
                        for h, hs in enumerate(halves)
                    )
                    side = lateral(x, lower, upper)
                    for h, hs in enumerate(halves):
                        if k > 0:
                            above = src[h, pl.ds(at - 8, 8), :]
                        else:
                            above = LH[n, pl.ds(8 * c, 8), hs] * deep
                        if k < KLOC - 1:
                            below = src[h, pl.ds(at + 8, 8), :]
                        else:
                            below = LH[n, pl.ds(8 * c, 8), hs] * top
                        value = x[h] + 0.1 * side[h] + 0.2 * (above + below - 2.0 * x[h])
                        if c == 0:
                            value = value + 0.1 * src[h, pl.ds(at + 64, 8), :]
                        if c == 1:
                            value = value - 0.1 * src[h, pl.ds(at - 64, 8), :]
                        dst[h, pl.ds(at, 8), :] = value * mask[h]

        def rims_in(n):
            pl.when(has_lo)(edge(n, 0).wait_recv)
            pl.when(has_hi)(edge(n, 1).wait_recv)
            level(n).wait_recv()

        rims_in(0)
        substep(0, Q, A1)
        rims_out(1, A1)
        rims_in(1)
        substep(1, A1, A2)

        results = [pltpu.make_async_copy(A2.at[h], out_o.at[:, hs], out_sem.at[h]) for h, hs in enumerate(halves)]
        for copy in results:
            copy.start()
        part.wait_send()
        for n in range(2):
            pl.when(has_hi)(edge(n, 0).wait_send)
            pl.when(has_lo)(edge(n, 1).wait_send)
            level(n).wait_send()
        settle(MSG, q_send)
        flags.wait()
        for copy in results:
            copy.wait()
        settle(BR, f_recv)


def tail(wave_h, unforced_h, bands_h, flags_h, out_w, out_o, zeros, A2, BR, MR, BTS, in_sem, w_sem, o_sem):
    grp = lax.axis_index("grp")
    tile = lax.axis_index("tile")
    sp = lax.axis_index("spec")

    @pl.when(grp == 0)
    def wave():
        copies = []
        for c in range(CHUNKS):
            rows = pl.ds(c * RCH * 8, RCH * 8)
            copies.append(pltpu.make_async_copy(wave_h.at[rows, :], out_w.at[rows, :], w_sem.at[c]))
            copies[-1].start()
        zeros[0:192, :] = jnp.zeros((192, 256), F32)
        copies.append(pltpu.make_async_copy(zeros.at[0:192, :], out_o, o_sem.at[0]))
        copies[-1].start()
        for copy in copies:
            copy.wait()

    @pl.when(grp == 1)
    def circulation():
        loads = [
            pltpu.make_async_copy(flags_h, MR, in_sem.at[0]),
            pltpu.make_async_copy(bands_h, BR, in_sem.at[1]),
        ] + [pltpu.make_async_copy(unforced_h.at[:, hs], A2.at[h], in_sem.at[2 + h]) for h, hs in enumerate(HALVES)]
        for copy in loads:
            copy.start()
        zeros[...] = jnp.zeros(zeros.shape, F32)
        blanks = []
        for c in range(CHUNKS):
            rows = pl.ds(c * RCH * 8, RCH * 8)
            blanks.append(pltpu.make_async_copy(zeros, out_w.at[rows, :], w_sem.at[c]))
            blanks[-1].start()
        row = lax.broadcasted_iota(jnp.int32, (8, 128), 0)
        top = (1 - sp).astype(F32)
        deep = sp.astype(F32)
        down = jnp.where(sp == 0, 1.0, math.exp(-1.0)).astype(F32)
        at_lo = jnp.where(tile > 0, 1.0, 0.0).astype(F32)
        at_hi = jnp.where(tile < TILES - 1, 1.0, 0.0).astype(F32)
        loads[0].wait()
        (mask3,) = arrived(MR, BTS, tile, 1)
        mask = tuple(x[1] for x in mask3)
        mask_lo = tuple(jnp.where(row == 0, x[0] * at_lo, x[0]) for x in mask3)
        mask_hi = tuple(jnp.where(row == 7, x[2] * at_hi, x[2]) for x in mask3)
        for copy in loads[1:]:
            copy.wait()
        forced, spread = [], []
        for f, three in enumerate(arrived(BR, BTS, tile, 4)):
            lower = tuple(three[h][0] * mask_lo[h] for h in range(2))
            own = tuple(three[h][1] * mask[h] for h in range(2))
            upper = tuple(three[h][2] * mask_hi[h] for h in range(2))
            forced.append(own)
            spread.append(lateral(own, lower, upper))
        for k in range(KLOC):
            near, far = math.exp(0.125), math.exp(-0.125)
            prof = float(_prof[k]) * down
            above = near if k > 0 else near * deep
            below = far if k < KLOC - 1 else far * top
            stay = prof * (1.0 + 0.2 * (above + below - 2.0))
            for h, hs in enumerate(HALVES):
                east = (0.1 * prof) * forced[3][h]
                north = (-0.1 * prof) * forced[2][h]
                d_east = (0.1 * stay) * forced[3][h] + (0.01 * prof) * spread[3][h]
                d_north = (-0.1 * stay) * forced[2][h] - (0.01 * prof) * spread[2][h]
                if k == 0:
                    east = east + top * forced[0][h]
                    north = north + top * forced[1][h]
                    d_east = d_east + top * (0.6 * forced[0][h] + 0.1 * spread[0][h])
                    d_north = d_north + top * (0.6 * forced[1][h] + 0.1 * spread[1][h])
                if k == 1:
                    d_east = d_east + (0.2 * top) * forced[0][h]
                    d_north = d_north + (0.2 * top) * forced[1][h]
                A2[h, pl.ds(8 * k, 8), :] += mask[h] * (d_east + 0.1 * north) + east
                A2[h, pl.ds(64 + 8 * k, 8), :] += mask[h] * (d_north - 0.1 * east) + north
        results = [pltpu.make_async_copy(A2.at[h], out_o.at[:, hs], o_sem.at[h]) for h, hs in enumerate(HALVES)]
        for copy in results:
            copy.start()

        for copy in results + blanks:
            copy.wait()


def body(spectrum, wind, land_mask, intersection, ocean_state, sea_level):
    v = lambda *shape, dtype=F32: pltpu.VMEM(shape, dtype)
    dma = lambda *shape: pltpu.SemaphoreType.DMA(shape) if shape else pltpu.SemaphoreType.DMA
    anywhere = pl.BlockSpec(memory_space=pltpu.HBM)
    scratch = [
        pltpu.SMEM(TABLE.shape, F32),
        v(2, FD * 8, 128), v(2, FD * 8, 128), v(5, 2, PCH * RCH * 8, 128), v(DLOC, 8, 256), v(FD, 128),
        v(WSTEPS, 2, 2, FD, 128), v(WSTEPS, 2, 2, FD, 128),
        v(2, 8, 256), v(8, 256, dtype=jnp.int32), v(8, 256, dtype=jnp.int32),
        v(16, 256, dtype=jnp.int32), v(2, 16, 256, dtype=jnp.int32),
        v(256, 128), v(WSTEPS, 8, 256), v(WSTEPS, 5, 8, 256), v(40, 256), v(40, 256), v(256, 128), v(256, 128),
        v(2, 192, 128), v(2, 192, 128), v(2, 192, 128), v(8, 256), v(16, 256), v(16, 256), v(128, 256),
        v(256, 128), v(256, 128), v(256, 256),
        v(2, 2, 24, 256), v(2, 2, 24, 256), v(2, 24, 256), v(2, 24, 256),
        dma(CHUNKS, 2), dma(3), dma(WSTEPS, 2, CHUNKS), dma(WSTEPS, 2, CHUNKS), dma(WSTEPS, 5), dma(WSTEPS, 5),
        dma(2), dma(2), dma(), dma(), dma(), dma(), dma(), dma(), dma(), dma(),
        dma(2, 2), dma(2, 2), dma(2), dma(2), dma(2),
    ]
    landed = pl.pallas_call(
        kernel,
        out_shape=(
            jax.ShapeDtypeStruct((FD * 8, 256), F32),
            jax.ShapeDtypeStruct((192, 256), F32),
            jax.ShapeDtypeStruct((256, 128), F32),
            jax.ShapeDtypeStruct((256, 128), F32),
        ),
        in_specs=[anywhere] * 6,
        out_specs=(pl.BlockSpec(memory_space=pl.ANY),) * 4,
        scratch_shapes=scratch,
        compiler_params=pltpu.CompilerParams(collective_id=0, has_side_effects=True, vmem_limit_bytes=48 << 20),
    )(
        *(
            pltpu.with_memory_space_constraint(x, pltpu.HBM)
            for x in (
                spectrum.reshape(FD * 8, 256),
                wind,
                land_mask,
                intersection,
                ocean_state.reshape(192, 256),
                sea_level.reshape(8, 256),
            )
        )
    )
    waves, ocean = pl.pallas_call(
        tail,
        out_shape=(jax.ShapeDtypeStruct((FD * 8, 256), F32), jax.ShapeDtypeStruct((192, 256), F32)),
        in_specs=[pl.BlockSpec(memory_space=pl.ANY)] * 4,
        out_specs=(pl.BlockSpec(memory_space=pl.ANY),) * 2,
        scratch_shapes=[
            v(RCH * 8, 256), v(2, 192, 128), v(256, 128), v(256, 128), v(256, 256), dma(4), dma(CHUNKS), dma(2)
        ],
        compiler_params=pltpu.CompilerParams(vmem_limit_bytes=6 << 20),
    )(*landed)
    return waves.reshape(spectrum.shape), ocean.reshape(ocean_state.shape)


def solution(mesh):
    return jax.shard_map(
        body,
        mesh=mesh,
        in_specs=(
            P("grp", None, "spec", "tile", None),
            P(None, "tile", None),
            P("tile", None),
            P("tile", None),
            P("grp", None, "spec", "tile", None),
            P("grp", "tile", None),
        ),
        out_specs=(P("grp", None, "spec", "tile", None), P("grp", None, "spec", "tile", None)),
        check_vma=False,
    )
```

```python
import math

import jax
import jax.numpy as jnp
import numpy as np
from jax import lax
from jax.experimental import pallas as pl
from jax.experimental.pallas import tpu as pltpu
from jax.sharding import PartitionSpec as P

FREQS = 32
DIRS = 36
LEVELS = 16
WSTEPS = 4
TILES = 32
DLOC = 18
KLOC = 8
FD = FREQS * DLOC
CHUNKS = 8
FCH = FREQS // CHUNKS
RCH = FCH * DLOC
PCH = 5
HELD = 3
F32 = jnp.float32

_freq = 0.04 * 1.1 ** np.arange(FREQS)
_cel = 1.56 / _freq
_gs = 0.4 * 1.1 ** (-np.arange(FREQS, dtype=np.float64))
_bw = 0.1 * _freq * (2.0 * math.pi / DIRS)
TABLE = np.stack([_gs, 0.05 / _cel, _bw, 5.0 * _bw / _cel, 20.0 * _bw * _freq**3]).astype(np.float32)
_ang = 2.0 * math.pi * (np.arange(DIRS) + 0.5) / DIRS
COS = [float(np.float32(x)) for x in np.cos(_ang)[:DLOC]]
SIN = [float(np.float32(x)) for x in np.sin(_ang)[:DLOC]]
DIR_ORDER = [d for k in range(DLOC // 2) for d in (k, DLOC - 1 - k)]
_prof = np.exp(-2.0 * (np.arange(LEVELS) + 0.5) / LEVELS)
_wgt = _prof / _prof.sum()


def mesh_copy(src, dst, send, recv, where):
    return pltpu.make_async_remote_copy(
        src_ref=src,
        dst_ref=dst,
        send_sem=send,
        recv_sem=recv,
        device_id=where,
        device_id_type=pl.DeviceIdType.MESH,
    )


def settle(buf, sem):
    pltpu.make_async_copy(buf, buf, sem).wait()


HALVES = (slice(0, 128), slice(128, 256))


def at_lane(k):
    return lax.broadcasted_iota(jnp.int32, (8, 128), 1) == k


def from_left(x):
    a, b = pltpu.roll(x[0], 1, 1), pltpu.roll(x[1], 1, 1)
    return jnp.where(at_lane(0), 0.0, a), jnp.where(at_lane(0), a, b)


def from_right(x):
    a, b = pltpu.roll(x[0], 127, 1), pltpu.roll(x[1], 127, 1)
    return jnp.where(at_lane(127), b, a), jnp.where(at_lane(127), 0.0, b)


def lateral(x, lower, upper):
    left, right = from_left(x), from_right(x)
    return tuple(lower[h] + upper[h] + left[h] + right[h] - 4.0 * x[h] for h in range(2))


def arrived(buf, BTS, tile, slots):
    for h in range(2):
        turned = buf[pl.ds(128 * h, 128), :].T
        BTS[pl.ds(0, 128), HALVES[h]] = turned
        BTS[pl.ds(128, 128), HALVES[h]] = turned
    out = []
    for f in range(slots):
        start = pl.multiple_of((8 * tile + 32 * f) % 128, 8)
        wide = BTS[pl.ds(start, 16), :]
        out.append(tuple((wide[0:8, hs], wide[1:9, hs], wide[2:10, hs]) for hs in HALVES))
    return out


def kernel(
    spec_h, wind_h, land_h, inter_h, ocean_h, sea_h, out_w, out_o, BR, out_m,
    tab, B, G, PT, WD, CNT, H, S, wind, land, inter, NBS, NBR, QR, TS, TR, BANDS, BANDR, MSG2, MMSG,
    Q, A1, A2, sea, CS, SX, MSG, MR, BTS, ES, EH, LS, LH,
    load_sem, small_sem, h_send, h_recv, t_send, t_recv, nb_send, nb_recv,
    q_send, q_recv, m_send, m_recv, f_send, f_recv, e_send, e_recv, l_send, l_recv, out_sem,
):
    grp = lax.axis_index("grp")
    tile = lax.axis_index("tile")
    sp = lax.axis_index("spec")
    other = 1 - sp
    sgn = (1 - 2 * sp).astype(F32)
    has_lo = tile > 0
    has_hi = tile < TILES - 1
    lo_t = jnp.maximum(tile - 1, 0)
    hi_t = jnp.minimum(tile + 1, TILES - 1)
    lane = lax.broadcasted_iota(jnp.int32, (8, 128), 1)
    row = lax.broadcasted_iota(jnp.int32, (8, 128), 0)
    first_lane, last_lane = lane == 0, lane == 127
    first_row, last_row = row == 0, row == 7
    low_rows = row < 4
    halves = HALVES

    def circular(x, shift):
        a, b = pltpu.roll(x[0], shift, 1), pltpu.roll(x[1], shift, 1)
        m = lane < shift
        return jnp.where(m, b, a), jnp.where(m, a, b)

    def barrel(x, amount):
        for bit in range(8):
            moved = circular(x, 1 << bit) if bit < 7 else (x[1], x[0])
            x = tuple(jnp.where((amount[h] & (1 << bit)) != 0, moved[h], x[h]) for h in range(2))
        return x

    def pair(ref, *lead):
        return tuple(ref[(*lead, slice(None), hs)] for hs in halves)

    def put(ref, value, rows):
        for h in range(2):
            ref[rows, halves[h]] = value[h]

    barrier = pltpu.get_barrier_semaphore()

    def greet(where):
        pl.semaphore_signal(barrier, 1, device_id=where, device_id_type=pl.DeviceIdType.MESH)

    greet({"spec": other})

    @pl.when(has_lo)
    def _():
        greet({"tile": lo_t})
        greet({"tile": lo_t, "spec": other})

    @pl.when(has_hi)
    def _():
        greet({"tile": hi_t})
        greet({"tile": hi_t, "spec": other})

    def greet_across(u, carry):
        greet({"grp": 1 - grp, "tile": u})
        greet({"grp": 1 - grp, "tile": u, "spec": other})
        return carry

    lax.fori_loop(0, TILES, greet_across, 0)
    beside = jnp.where(has_lo, 2, 0) + jnp.where(has_hi, 2, 0)

    def everyone_in():
        pl.semaphore_wait(barrier, 2 * TILES + 1 + beside)

    @pl.when(grp == 0)
    def wave():
        def load(c):
            rows = pl.ds(pl.multiple_of(c * RCH * 8, 8), RCH * 8)
            return [
                pltpu.make_async_copy(spec_h.at[rows, hs], B.at[h, rows, :], load_sem.at[c, h])
                for h, hs in enumerate(halves)
            ]

        smalls = [
            pltpu.make_async_copy(wind_h, wind, small_sem.at[0]),
            pltpu.make_async_copy(land_h, land, small_sem.at[1]),
            pltpu.make_async_copy(inter_h, inter, small_sem.at[2]),
        ]
        for copy in smalls:
            copy.start()
        for q in range(TABLE.shape[0]):
            for f in range(FREQS):
                tab[q, f] = float(TABLE[q, f])

        def begin(c, carry):
            for copy in load(c):
                copy.start()
            return carry

        lax.fori_loop(0, CHUNKS, begin, 0)

        def halo(n, side, c):
            rows = pl.ds(pl.multiple_of(c * RCH, 8), RCH)
            return mesh_copy(
                S.at[n, side, :, rows, :], H.at[n, side, :, rows, :], h_send.at[n, side, c], h_recv.at[n, side, c],
                {"tile": hi_t if side == 0 else lo_t},
            )

        def edges_out(n, c):
            for k in range(RCH // 8):
                at = c * RCH + 8 * k
                rows = pl.ds(pl.multiple_of(at, 8), 8)
                for h in range(2):
                    S[n, 0, h, rows, :] = B[h, pl.ds(at * 8 + 7, 8, stride=8), :]
                    S[n, 1, h, rows, :] = B[h, pl.ds(at * 8, 8, stride=8), :]

            @pl.when(has_hi)
            def _():
                halo(n, 0, c).start()

            @pl.when(has_lo)
            def _():
                halo(n, 1, c).start()

        for copy in smalls:
            copy.wait()
        wet_i = pair(land)
        wet = tuple(x.astype(F32) for x in wet_i)
        shift = tuple((x - lane - 128 * h) & 255 for h, x in enumerate(pair(inter)))
        put(NBS, wet_i, slice(0, 8))
        put(NBS, shift, slice(8, 16))

        def neighbour(side):
            return mesh_copy(
                NBS, NBR.at[side], nb_send.at[side], nb_recv.at[side],
                {"tile": hi_t if side == 0 else lo_t},
            )

        everyone_in()

        @pl.when(has_hi)
        def _():
            neighbour(0).start()

        @pl.when(has_lo)
        def _():
            neighbour(1).start()

        wet_back = circular(barrel(wet, shift), 1)

        def windows(fields, u):
            acc = jnp.zeros((8, 128), F32)
            for f, field in enumerate(fields):
                start = (8 * u + 32 * f) % 128
                offset = (lane - start) & 127
                inside = offset < 10
                base = (8 * u) // 128
                p = 8 * u + offset
                value = field[base]
                if 8 * u % 128 + 10 > 128:
                    turned = (lane - 32 * f) & 127
                    value = jnp.where(turned < 16, field[1 - base], value)
                acc = jnp.where(inside, value, acc)
            return acc

        for u in range(TILES):
            MMSG[pl.ds(8 * u, 8), :] = windows([wet_back], u)

        def to_ocean(src, dst, send, recv, u):
            return mesh_copy(
                src.at[pl.ds(pl.multiple_of(u * 8, 8), 8), :],
                dst.at[pl.ds(pl.multiple_of(tile * 8, 8), 8), :],
                send, recv, {"grp": 1, "tile": u},
            )

        def send_mask(u, carry):
            to_ocean(MMSG, MR, m_send, m_recv, u).start()
            return carry

        lax.fori_loop(0, TILES, send_mask, 0)

        @pl.when(jnp.logical_not(has_lo))
        def _():
            H[:, 0] = jnp.zeros((WSTEPS, 2, FD, 128), F32)
            NBR[0] = jnp.zeros((16, 256), jnp.int32)
            TR[:, 1:3] = jnp.zeros((WSTEPS, 2, 8, 256), F32)

        @pl.when(jnp.logical_not(has_hi))
        def _():
            H[:, 1] = jnp.zeros((WSTEPS, 2, FD, 128), F32)
            NBR[1] = jnp.zeros((16, 256), jnp.int32)
            TR[:, 3:5] = jnp.zeros((WSTEPS, 2, 8, 256), F32)

        def first_edges(c, carry):
            for copy in load(c):
                copy.wait()
            edges_out(0, c)
            return carry

        lax.fori_loop(0, CHUNKS, first_edges, 0)

        for d in range(DLOC):
            for h, hs in enumerate(halves):
                WD[d, :, hs] = wind[0, :, hs] * (sgn * COS[d]) + wind[1, :, hs] * (sgn * SIN[d])

        def growth(f, carry):
            slope = tab[1, f]
            sgs = tab[0, f] * sgn
            for d in range(DLOC):
                i = f * DLOC + d
                rows = pl.ds(pl.multiple_of(i * 8, 8), 8)
                for h, hs in enumerate(halves):
                    G[h, rows, :] = 1.0 + jnp.maximum(WD[d, :, hs] * slope - 0.05, 0.0)
                CNT[pl.ds(i, 1), :] = jnp.full((1, 128), sgs * SIN[d], F32)
            return carry

        lax.fori_loop(0, FREQS, growth, 0)

        @pl.when(has_lo)
        def _():
            neighbour(0).wait_recv()

        @pl.when(has_hi)
        def _():
            neighbour(1).wait_recv()

        edge_i = tuple(
            jnp.where(low_rows, NBR[1, 0:8, hs], NBR[0, 0:8, hs]) for hs in halves
        )
        edge_wet = tuple(x.astype(F32) for x in edge_i)
        edge_shift = tuple(
            jnp.where(low_rows, NBR[1, 8:16, hs], NBR[0, 8:16, hs]) for hs in halves
        )

        settle(QR, q_recv)
        group = lax.broadcasted_iota(jnp.int32, (4, 128), 1) >> 3
        parts = [[], [], [], [], []]
        for h in range(2):
            upper = [jnp.zeros((4, 128), F32)] * 5
            lower = [jnp.zeros((4, 128), F32)] * 5
            for k in range(16):
                m = QR[0, 16 * h + k] + QR[1, 16 * h + k]
                turned = pltpu.roll(m, 64, 1)
                for c in range(5):
                    at = (k + c) % 16
                    near, far = (m, turned) if at < 8 else (turned, m)
                    upper[c] = jnp.where(group == at, near, upper[c])
                    lower[c] = jnp.where(group == at, far, lower[c])
            for c in range(5):
                acc = jnp.concatenate([upper[c], lower[c]], axis=0)
                parts[c].append(pltpu.roll(acc, 128 - 8 * c, 1) if c else acc)
        fields = [tuple(x) for x in parts]
        left = tuple((256 - x) & 255 for x in shift)
        edge_left = tuple((256 - x) & 255 for x in edge_shift)
        u01 = tuple(0.1 * x for x in barrel(fields[0], left))
        v01 = tuple(0.1 * x for x in barrel(fields[1], left))

        def stiffness(level):
            depth = tuple(10.0 + 4.0 * x for x in level)
            return tuple(25.0 / (x * x) for x in depth)

        stiff = stiffness(barrel(fields[2], left))
        edge_v = tuple(0.1 * x for x in barrel(fields[3], edge_left))
        edge_stiff = stiffness(barrel(fields[4], edge_left))
        v_lo = tuple(jnp.broadcast_to(x[7:8], (8, 128)) for x in edge_v)
        v_hi = tuple(jnp.broadcast_to(x[0:1], (8, 128)) for x in edge_v)

        def halo_in(n, c, scale=None):
            @pl.when(has_lo)
            def _():
                halo(n, 0, c).wait_recv()

            @pl.when(has_hi)
            def _():
                halo(n, 1, c).wait_recv()

            for k in range(RCH // 8):
                rows = pl.ds(pl.multiple_of(c * RCH + 8 * k, 8), 8)
                cn = CNT[rows, :]
                for h in range(2):
                    lower, upper = H[n, 0, h, rows, :], H[n, 1, h, rows, :]
                    if scale is not None:
                        lower, upper = scale[0][h] * lower, scale[1][h] * upper
                    H[n, 0, h, rows, :] = jnp.maximum((cn + v_lo[h]) * lower, 0.0)
                    H[n, 1, h, rows, :] = jnp.minimum((cn + v_hi[h]) * upper, 0.0)

        def terms(n, i, rows, ce, cn, r=None):
            b = [B[h, rows, :] for h in range(2)]
            if r is not None:
                b = [r[h] * b[h] for h in range(2)]
            X = [(u01[h] + ce) * b[h] for h in range(2)]
            Y = [(v01[h] + cn) * b[h] for h in range(2)]
            own = [(b[h] - jnp.abs(X[h])) - jnp.abs(Y[h]) for h in range(2)]
            west, east = [jnp.maximum(x, 0.0) for x in X], [jnp.minimum(x, 0.0) for x in X]
            if r is not None:
                west, east = from_left(west), from_right(east)
            else:
                a = [pltpu.roll(x, 1, 1) for x in west]
                west = [a[0], jnp.where(first_lane, a[0], a[1])]
                a = [pltpu.roll(x, 127, 1) for x in east]
                east = [jnp.where(last_lane, a[1], a[0]), a[1]]
            south = [
                jnp.where(
                    first_row, H[n, 0, h, pl.ds(i, 8, stride=0), :], pltpu.roll(jnp.maximum(Y[h], 0.0), 1, 0)
                )
                for h in range(2)
            ]
            north = [
                jnp.where(
                    last_row, H[n, 1, h, pl.ds(i, 8, stride=0), :], pltpu.roll(jnp.minimum(Y[h], 0.0), 7, 0)
                )
                for h in range(2)
            ]
            return own, west, east, south, north

        def ahead(n):
            def chunk(c, carry):
                halo_in(n, c)

                def band(fc, carry):
                    f = c * FCH + fc
                    sgs = tab[0, f] * sgn
                    for d in range(DLOC):
                        i = f * DLOC + d
                        rows = pl.ds(pl.multiple_of(i * 8, 8), 8)
                        for q, term in enumerate(terms(n, i, rows, sgs * COS[d], sgs * SIN[d])):
                            for h in range(2):
                                PT[q, h, rows, :] = term[h]
                    return carry

                return lax.fori_loop(0, FCH, band, carry, unroll=2)

            lax.fori_loop(0, PCH, chunk, 0)

        def factors(r, edge_r):
            a, b = [pltpu.roll(x, 1, 1) for x in r], [pltpu.roll(x, 127, 1) for x in r]
            r_w = (jnp.where(first_lane, 0.0, a[0]), jnp.where(first_lane, a[0], a[1]))
            r_e = (jnp.where(last_lane, b[1], b[0]), jnp.where(last_lane, 0.0, b[1]))
            r_s = tuple(jnp.where(first_row, pltpu.roll(edge_r[h], 1, 0), pltpu.roll(r[h], 1, 0)) for h in range(2))
            r_n = tuple(jnp.where(last_row, pltpu.roll(edge_r[h], 7, 0), pltpu.roll(r[h], 7, 0)) for h in range(2))
            return tuple(r), r_w, r_e, r_s, r_n

        def sweep(n, r, edge_r, last):
            r_all = factors(r, edge_r)
            scale = (
                tuple(jnp.broadcast_to(x[7:8], (8, 128)) for x in edge_r),
                tuple(jnp.broadcast_to(x[0:1], (8, 128)) for x in edge_r),
            )

            def chunk(c, sums, prepared):
                if not prepared:
                    halo_in(n, c, scale)

                def band(fc, sums):
                    f = c * FCH + fc
                    sgs = tab[0, f] * sgn
                    zero = jnp.zeros((8, 128), F32)
                    acc = [[zero, zero] for _ in range(5 if last else 1)]
                    half_way = {}
                    for d in (DIR_ORDER if last else range(DLOC)):
                        i = f * DLOC + d
                        rows = pl.ds(pl.multiple_of(i * 8, 8), 8)
                        if prepared:
                            five = [[r_all[q][h] * PT[q, h, rows, :] for h in range(2)] for q in range(5)]
                        else:
                            five = terms(n, i, rows, sgs * COS[d], sgs * SIN[d], r)
                        for h in range(2):
                            own, west, east, south, north = (five[q][h] for q in range(5))
                            adv = own + ((west - east) + (south - north))
                            new = adv * G[h, rows, :]
                            B[h, rows, :] = new
                            acc[0][h] += adv
                            if last:
                                mine = (new - adv, new)
                                if h not in half_way:
                                    half_way[h] = mine
                                    continue
                                for q, (a, b) in enumerate(zip(half_way.pop(h), mine)):
                                    acc[1 + 2 * q][h] += (a - b) * COS[DLOC - 1 - d]
                                    acc[2 + 2 * q][h] += (a + b) * SIN[d]
                    weights = [tab[2, f], tab[3, f], tab[3, f], tab[4, f], tab[4, f]]
                    if last:
                        weights = weights[:1] + [w * sgn for w in weights[1:]]
                    return tuple(
                        tuple(total[h] + acc[q][h] * weights[q] for h in range(2)) for q, total in enumerate(sums)
                    )

                sums = lax.fori_loop(0, FCH, band, sums, unroll=2)
                if not last:

                    @pl.when(c < CHUNKS - HELD)
                    def _():
                        edges_out(n + 1, c)

                return sums

            zero = jnp.zeros((8, 128), F32)
            sums = tuple((zero, zero) for _ in range(5 if last else 1))
            begun = PCH if last else jnp.where(n > 0, PCH, 0)
            sums = lax.fori_loop(0, begun, lambda c, x: chunk(c, x, True), sums)
            return lax.fori_loop(begun, CHUNKS, lambda c, x: chunk(c, x, False), sums)

        def total_copies(n):
            return [
                (None, mesh_copy(TS.at[n], TR.at[n, 0], t_send.at[n, 0], t_recv.at[n, 0], {"spec": other})),
                (has_hi, mesh_copy(TS.at[n], TR.at[n, 1], t_send.at[n, 1], t_recv.at[n, 1], {"tile": hi_t})),
                (has_hi, mesh_copy(TS.at[n], TR.at[n, 2], t_send.at[n, 2], t_recv.at[n, 2], {"tile": hi_t, "spec": other})),
                (has_lo, mesh_copy(TS.at[n], TR.at[n, 3], t_send.at[n, 3], t_recv.at[n, 3], {"tile": lo_t})),
                (has_lo, mesh_copy(TS.at[n], TR.at[n, 4], t_send.at[n, 4], t_recv.at[n, 4], {"tile": lo_t, "spec": other})),
            ]

        def gated(condition, action):
            if condition is None:
                action()
            else:
                pl.when(condition)(action)

        def one_step(n, carry):
            r, edge_r = carry
            (total,) = sweep(n, r, edge_r, False)
            for h, hs in enumerate(halves):
                TS[n, :, hs] = total[h]
            copies = total_copies(n)
            for condition, copy in copies:
                gated(condition, copy.start)

            def late(c, carry):
                edges_out(n + 1, c)
                return carry

            lax.fori_loop(CHUNKS - HELD, CHUNKS, late, 0)
            ahead(n + 1)
            for (_, copy), condition in zip(copies, [None, has_lo, has_lo, has_hi, has_hi]):
                gated(condition, copy.wait_recv)
            new_r, new_edge = [], []
            for h, hs in enumerate(halves):
                full = total[h] + TR[n, 0, :, hs]
                new_r.append(wet[h] / (1.0 + stiff[h] * full))
                lower = TR[n, 1, :, hs] + TR[n, 2, :, hs]
                upper = TR[n, 3, :, hs] + TR[n, 4, :, hs]
                edge = jnp.where(low_rows, upper, lower)
                new_edge.append(edge_wet[h] / (1.0 + edge_stiff[h] * edge))
            return tuple(new_r), tuple(new_edge)

        r, edge_r = lax.fori_loop(0, WSTEPS - 1, one_step, (wet, edge_wet))
        n = WSTEPS - 1
        sums = sweep(n, r, edge_r, True)
        for q in range(5):
            put(BANDS, sums[q], slice(8 * q, 8 * q + 8))
        swap = mesh_copy(BANDS, BANDR, t_send.at[n, 0], t_recv.at[n, 0], {"spec": other})
        swap.start()
        swap.wait_recv()
        full = [tuple(sums[q][h] + BANDR[8 * q : 8 * q + 8, halves[h]] for h in range(2)) for q in range(5)]
        breaking = tuple(1.0 / (1.0 + stiff[h] * full[0][h]) for h in range(2))
        final = tuple(wet[h] * breaking[h] for h in range(2))
        bands = []
        for q in range(1, 5):
            scale = breaking if q < 3 else final
            bands.append(circular(barrel(tuple(scale[h] * full[q][h] for h in range(2)), shift), 1))
        bands = [tuple(pltpu.roll(x, 32 * f, 1) if f else x for x in field) for f, field in enumerate(bands)]
        for u in range(TILES):
            MSG2[pl.ds(8 * u, 8), :] = windows(bands, u)

        def send_bands(u, carry):
            to_ocean(MSG2, BR, f_send, f_recv, u).start()
            return carry

        lax.fori_loop(0, TILES, send_bands, 0)

        def store(c):
            rows = pl.ds(pl.multiple_of(c * RCH * 8, 8), RCH * 8)
            return [
                pltpu.make_async_copy(B.at[h, rows, :], out_w.at[rows, hs], load_sem.at[c, h])
                for h, hs in enumerate(halves)
            ]

        def finish(c, carry):
            def scale_f(i, carry):
                for d in range(DLOC):
                    rows = pl.ds(pl.multiple_of((c * RCH + i * DLOC + d) * 8, 8), 8)
                    for h in range(2):
                        B[h, rows, :] = B[h, rows, :] * final[h]
                return carry

            lax.fori_loop(0, FCH, scale_f, 0)
            for copy in store(c):
                copy.start()
            return carry

        lax.fori_loop(0, CHUNKS, finish, 0)
        def drain(c, carry):
            for copy in store(c):
                copy.wait()

            @pl.when(has_hi)
            def _():
                for n in range(WSTEPS):
                    halo(n, 0, c).wait_send()

            @pl.when(has_lo)
            def _():
                for n in range(WSTEPS):
                    halo(n, 1, c).wait_send()

            return carry

        lax.fori_loop(0, CHUNKS, drain, 0)
        for m in range(WSTEPS - 1):
            for condition, copy in total_copies(m):
                gated(condition, copy.wait_send)
        swap.wait_send()
        gated(has_hi, neighbour(0).wait_send)
        gated(has_lo, neighbour(1).wait_send)
        settle(MMSG, m_send)
        settle(MSG2, f_send)

    @pl.when(grp == 1)
    def circulation():
        top = (1 - sp).astype(F32)
        deep = sp.astype(F32)
        down = jnp.where(sp == 0, 1.0, math.exp(-1.0)).astype(F32)
        loads = [
            pltpu.make_async_copy(ocean_h.at[:, halves[0]], Q.at[0], small_sem.at[0]),
            pltpu.make_async_copy(ocean_h.at[:, halves[1]], Q.at[1], small_sem.at[1]),
            pltpu.make_async_copy(sea_h, sea, small_sem.at[2]),
        ]
        for copy in loads:
            copy.start()
        for copy in loads:
            copy.wait()
        for c in range(2):
            for h, hs in enumerate(halves):
                acc = jnp.zeros((8, 128), F32)
                for k in range(KLOC):
                    acc += Q[h, pl.ds((c * KLOC + k) * 8, 8), :] * float(_wgt[k])
                CS[pl.ds(8 * c, 8), hs] = acc * down

        def edge(n, side):
            return mesh_copy(
                ES.at[n, side], EH.at[n, side], e_send.at[n, side], e_recv.at[n, side],
                {"tile": hi_t if side == 0 else lo_t},
            )

        def level(n):
            return mesh_copy(LS.at[n], LH.at[n], l_send.at[n], l_recv.at[n], {"spec": other})

        def rims_out(n, src):
            for c in range(3):
                for h, hs in enumerate(halves):
                    ES[n, 0, pl.ds(8 * c, 8), hs] = src[h, pl.ds(c * 64 + 7, 8, stride=8), :]
                    ES[n, 1, pl.ds(8 * c, 8), hs] = src[h, pl.ds(c * 64, 8, stride=8), :]
                    LS[n, pl.ds(8 * c, 8), hs] = jnp.where(
                        sp == 0, src[h, pl.ds(c * 64 + 56, 8), :], src[h, pl.ds(c * 64, 8), :]
                    )
            pl.when(has_hi)(edge(n, 0).start)
            pl.when(has_lo)(edge(n, 1).start)
            level(n).start()

        SX[...] = jnp.zeros((128, 256), F32)
        put(SX, tuple(0.5 * x for x in pair(sea)), slice(16, 24))
        SX[0:16, :] = CS[...]
        ahead_rows = (lane & 7) < 4
        for c in range(2):
            src = tuple(SX[pl.ds(8 + 8 * c, 8), hs] for hs in halves)
            ahead, behind = circular(src, 120), circular(src, 8)
            ahead = (ahead[1], ahead[0])
            put(SX, tuple(jnp.where(ahead_rows, ahead[h], behind[h]) for h in range(2)), slice(24 + 8 * c, 32 + 8 * c))
        slot = lax.broadcasted_iota(jnp.int32, (4, 128), 1) < 64
        for h, hs in enumerate(halves):
            turned = pltpu.roll(SX[:, hs].T, tile % 8 * 8, 1)
            turned = turned + pltpu.roll(turned, 64, 1)
            for k in range(16):
                MSG[16 * h + k] = jnp.where(slot, turned[8 * k : 8 * k + 4], turned[8 * k + 4 : 8 * k + 8])
        everyone_in()

        def to_wave(u, half):
            return mesh_copy(
                MSG.at[u], QR.at[sp, tile], q_send, q_recv, {"grp": 0, "tile": u, "spec": half},
            )

        def send_q(u, carry):
            to_wave(u, sp).start()
            to_wave(u, other).start()
            return carry

        lax.fori_loop(0, TILES, send_q, 0)
        rims_out(0, Q)

        @pl.when(jnp.logical_not(has_lo))
        def _():
            EH[:, 0] = jnp.zeros((2, 24, 256), F32)

        @pl.when(jnp.logical_not(has_hi))
        def _():
            EH[:, 1] = jnp.zeros((2, 24, 256), F32)

        settle(MR, m_recv)
        flags = pltpu.make_async_copy(MR, out_m, small_sem.at[0])
        flags.start()
        (mask3,) = arrived(MR, BTS, tile, 1)
        mask = tuple(x[1] for x in mask3)

        def substep(n, src, dst):
            for c in range(3):
                for k in range(KLOC):
                    at = (c * KLOC + k) * 8
                    x = tuple(src[h, pl.ds(at, 8), :] for h in range(2))
                    row_at = 8 * c + k
                    lower = tuple(
                        jnp.where(first_row, EH[n, 0, row_at : row_at + 1, hs], pltpu.roll(x[h], 1, 0))
                        for h, hs in enumerate(halves)
                    )
                    upper = tuple(
                        jnp.where(last_row, EH[n, 1, row_at : row_at + 1, hs], pltpu.roll(x[h], 7, 0))
                        for h, hs in enumerate(halves)
                    )
                    side = lateral(x, lower, upper)
                    for h, hs in enumerate(halves):
                        if k > 0:
                            above = src[h, pl.ds(at - 8, 8), :]
                        else:
                            above = LH[n, pl.ds(8 * c, 8), hs] * deep
                        if k < KLOC - 1:
                            below = src[h, pl.ds(at + 8, 8), :]
                        else:
                            below = LH[n, pl.ds(8 * c, 8), hs] * top
                        value = x[h] + 0.1 * side[h] + 0.2 * (above + below - 2.0 * x[h])
                        if c == 0:
                            value = value + 0.1 * src[h, pl.ds(at + 64, 8), :]
                        if c == 1:
                            value = value - 0.1 * src[h, pl.ds(at - 64, 8), :]
                        dst[h, pl.ds(at, 8), :] = value * mask[h]

        def rims_in(n):
            pl.when(has_lo)(edge(n, 0).wait_recv)
            pl.when(has_hi)(edge(n, 1).wait_recv)
            level(n).wait_recv()

        rims_in(0)
        substep(0, Q, A1)
        rims_out(1, A1)
        rims_in(1)
        substep(1, A1, A2)

        results = [pltpu.make_async_copy(A2.at[h], out_o.at[:, hs], out_sem.at[h]) for h, hs in enumerate(halves)]
        for copy in results:
            copy.start()
        for n in range(2):
            pl.when(has_hi)(edge(n, 0).wait_send)
            pl.when(has_lo)(edge(n, 1).wait_send)
            level(n).wait_send()
        settle(QR, q_send)
        flags.wait()
        for copy in results:
            copy.wait()
        settle(BR, f_recv)


def tail(wave_h, unforced_h, bands_h, flags_h, out_w, out_o, zeros, A2, BR, MR, BTS, in_sem, w_sem, o_sem):
    grp = lax.axis_index("grp")
    tile = lax.axis_index("tile")
    sp = lax.axis_index("spec")

    @pl.when(grp == 0)
    def wave():
        copies = []
        for c in range(CHUNKS):
            rows = pl.ds(c * RCH * 8, RCH * 8)
            copies.append(pltpu.make_async_copy(wave_h.at[rows, :], out_w.at[rows, :], w_sem.at[c]))
            copies[-1].start()
        zeros[0:192, :] = jnp.zeros((192, 256), F32)
        copies.append(pltpu.make_async_copy(zeros.at[0:192, :], out_o, o_sem.at[0]))
        copies[-1].start()
        for copy in copies:
            copy.wait()

    @pl.when(grp == 1)
    def circulation():
        loads = [
            pltpu.make_async_copy(flags_h, MR, in_sem.at[0]),
            pltpu.make_async_copy(bands_h, BR, in_sem.at[1]),
        ] + [pltpu.make_async_copy(unforced_h.at[:, hs], A2.at[h], in_sem.at[2 + h]) for h, hs in enumerate(HALVES)]
        for copy in loads:
            copy.start()
        zeros[...] = jnp.zeros(zeros.shape, F32)
        blanks = []
        for c in range(CHUNKS):
            rows = pl.ds(c * RCH * 8, RCH * 8)
            blanks.append(pltpu.make_async_copy(zeros, out_w.at[rows, :], w_sem.at[c]))
            blanks[-1].start()
        row = lax.broadcasted_iota(jnp.int32, (8, 128), 0)
        top = (1 - sp).astype(F32)
        deep = sp.astype(F32)
        down = jnp.where(sp == 0, 1.0, math.exp(-1.0)).astype(F32)
        at_lo = jnp.where(tile > 0, 1.0, 0.0).astype(F32)
        at_hi = jnp.where(tile < TILES - 1, 1.0, 0.0).astype(F32)
        loads[0].wait()
        (mask3,) = arrived(MR, BTS, tile, 1)
        mask = tuple(x[1] for x in mask3)
        mask_lo = tuple(jnp.where(row == 0, x[0] * at_lo, x[0]) for x in mask3)
        mask_hi = tuple(jnp.where(row == 7, x[2] * at_hi, x[2]) for x in mask3)
        for copy in loads[1:]:
            copy.wait()
        forced, spread = [], []
        for f, three in enumerate(arrived(BR, BTS, tile, 4)):
            lower = tuple(three[h][0] * mask_lo[h] for h in range(2))
            own = tuple(three[h][1] * mask[h] for h in range(2))
            upper = tuple(three[h][2] * mask_hi[h] for h in range(2))
            forced.append(own)
            spread.append(lateral(own, lower, upper))
        for k in range(KLOC):
            near, far = math.exp(0.125), math.exp(-0.125)
            prof = float(_prof[k]) * down
            above = near if k > 0 else near * deep
            below = far if k < KLOC - 1 else far * top
            stay = prof * (1.0 + 0.2 * (above + below - 2.0))
            for h, hs in enumerate(HALVES):
                east = (0.1 * prof) * forced[3][h]
                north = (-0.1 * prof) * forced[2][h]
                d_east = (0.1 * stay) * forced[3][h] + (0.01 * prof) * spread[3][h]
                d_north = (-0.1 * stay) * forced[2][h] - (0.01 * prof) * spread[2][h]
                if k == 0:
                    east = east + top * forced[0][h]
                    north = north + top * forced[1][h]
                    d_east = d_east + top * (0.6 * forced[0][h] + 0.1 * spread[0][h])
                    d_north = d_north + top * (0.6 * forced[1][h] + 0.1 * spread[1][h])
                if k == 1:
                    d_east = d_east + (0.2 * top) * forced[0][h]
                    d_north = d_north + (0.2 * top) * forced[1][h]
                A2[h, pl.ds(8 * k, 8), :] += mask[h] * (d_east + 0.1 * north) + east
                A2[h, pl.ds(64 + 8 * k, 8), :] += mask[h] * (d_north - 0.1 * east) + north
        results = [pltpu.make_async_copy(A2.at[h], out_o.at[:, hs], o_sem.at[h]) for h, hs in enumerate(HALVES)]
        for copy in results:
            copy.start()

        for copy in results + blanks:
            copy.wait()


def body(spectrum, wind, land_mask, intersection, ocean_state, sea_level):
    v = lambda *shape, dtype=F32: pltpu.VMEM(shape, dtype)
    dma = lambda *shape: pltpu.SemaphoreType.DMA(shape) if shape else pltpu.SemaphoreType.DMA
    anywhere = pl.BlockSpec(memory_space=pltpu.HBM)
    scratch = [
        pltpu.SMEM(TABLE.shape, F32),
        v(2, FD * 8, 128), v(2, FD * 8, 128), v(5, 2, PCH * RCH * 8, 128), v(DLOC, 8, 256), v(FD, 128),
        v(WSTEPS, 2, 2, FD, 128), v(WSTEPS, 2, 2, FD, 128),
        v(2, 8, 256), v(8, 256, dtype=jnp.int32), v(8, 256, dtype=jnp.int32),
        v(16, 256, dtype=jnp.int32), v(2, 16, 256, dtype=jnp.int32),
        v(2, TILES, 4, 128), v(WSTEPS, 8, 256), v(WSTEPS, 5, 8, 256), v(40, 256), v(40, 256), v(256, 128), v(256, 128),
        v(2, 192, 128), v(2, 192, 128), v(2, 192, 128), v(8, 256), v(16, 256), v(128, 256),
        v(TILES, 4, 128), v(256, 128), v(256, 256),
        v(2, 2, 24, 256), v(2, 2, 24, 256), v(2, 24, 256), v(2, 24, 256),
        dma(CHUNKS, 2), dma(3), dma(WSTEPS, 2, CHUNKS), dma(WSTEPS, 2, CHUNKS), dma(WSTEPS, 5), dma(WSTEPS, 5),
        dma(2), dma(2), dma(), dma(), dma(), dma(), dma(), dma(),
        dma(2, 2), dma(2, 2), dma(2), dma(2), dma(2),
    ]
    landed = pl.pallas_call(
        kernel,
        out_shape=(
            jax.ShapeDtypeStruct((FD * 8, 256), F32),
            jax.ShapeDtypeStruct((192, 256), F32),
            jax.ShapeDtypeStruct((256, 128), F32),
            jax.ShapeDtypeStruct((256, 128), F32),
        ),
        in_specs=[anywhere] * 6,
        out_specs=(pl.BlockSpec(memory_space=pl.ANY),) * 4,
        scratch_shapes=scratch,
        compiler_params=pltpu.CompilerParams(collective_id=0, has_side_effects=True, vmem_limit_bytes=48 << 20),
    )(
        *(
            pltpu.with_memory_space_constraint(x, pltpu.HBM)
            for x in (
                spectrum.reshape(FD * 8, 256),
                wind,
                land_mask,
                intersection,
                ocean_state.reshape(192, 256),
                sea_level.reshape(8, 256),
            )
        )
    )
    waves, ocean = pl.pallas_call(
        tail,
        out_shape=(jax.ShapeDtypeStruct((FD * 8, 256), F32), jax.ShapeDtypeStruct((192, 256), F32)),
        in_specs=[pl.BlockSpec(memory_space=pl.ANY)] * 4,
        out_specs=(pl.BlockSpec(memory_space=pl.ANY),) * 2,
        scratch_shapes=[
            v(RCH * 8, 256), v(2, 192, 128), v(256, 128), v(256, 128), v(256, 256), dma(4), dma(CHUNKS), dma(2)
        ],
        compiler_params=pltpu.CompilerParams(vmem_limit_bytes=6 << 20),
    )(*landed)
    return waves.reshape(spectrum.shape), ocean.reshape(ocean_state.shape)


def solution(mesh):
    return jax.shard_map(
        body,
        mesh=mesh,
        in_specs=(
            P("grp", None, "spec", "tile", None),
            P(None, "tile", None),
            P("tile", None),
            P("tile", None),
            P("grp", None, "spec", "tile", None),
            P("grp", "tile", None),
        ),
        out_specs=(P("grp", None, "spec", "tile", None), P("grp", None, "spec", "tile", None)),
        check_vma=False,
    )
```

```python
import math

import jax
import jax.numpy as jnp
import numpy as np
from jax import lax
from jax.experimental import pallas as pl
from jax.experimental.pallas import tpu as pltpu
from jax.sharding import PartitionSpec as P

FREQS = 32
DIRS = 36
LEVELS = 16
WSTEPS = 4
TILES = 32
DLOC = 18
KLOC = 8
FD = FREQS * DLOC
CHUNKS = 8
FCH = FREQS // CHUNKS
RCH = FCH * DLOC
PCH = 5
HELD = 3
F32 = jnp.float32

_freq = 0.04 * 1.1 ** np.arange(FREQS)
_cel = 1.56 / _freq
_gs = 0.4 * 1.1 ** (-np.arange(FREQS, dtype=np.float64))
_bw = 0.1 * _freq * (2.0 * math.pi / DIRS)
TABLE = np.stack([_gs, 0.05 / _cel, _bw, 5.0 * _bw / _cel, 20.0 * _bw * _freq**3]).astype(np.float32)
_ang = 2.0 * math.pi * (np.arange(DIRS) + 0.5) / DIRS
COS = [float(np.float32(x)) for x in np.cos(_ang)[:DLOC]]
SIN = [float(np.float32(x)) for x in np.sin(_ang)[:DLOC]]
DIR_ORDER = [d for k in range(DLOC // 2) for d in (k, DLOC - 1 - k)]
_prof = np.exp(-2.0 * (np.arange(LEVELS) + 0.5) / LEVELS)
_wgt = _prof / _prof.sum()


def mesh_copy(src, dst, send, recv, where):
    return pltpu.make_async_remote_copy(
        src_ref=src,
        dst_ref=dst,
        send_sem=send,
        recv_sem=recv,
        device_id=where,
        device_id_type=pl.DeviceIdType.MESH,
    )


def settle(buf, sem):
    pltpu.make_async_copy(buf, buf, sem).wait()


HALVES = (slice(0, 128), slice(128, 256))


def at_lane(k):
    return lax.broadcasted_iota(jnp.int32, (8, 128), 1) == k


def from_left(x):
    a, b = pltpu.roll(x[0], 1, 1), pltpu.roll(x[1], 1, 1)
    return jnp.where(at_lane(0), 0.0, a), jnp.where(at_lane(0), a, b)


def from_right(x):
    a, b = pltpu.roll(x[0], 127, 1), pltpu.roll(x[1], 127, 1)
    return jnp.where(at_lane(127), b, a), jnp.where(at_lane(127), 0.0, b)


def lateral(x, lower, upper):
    left, right = from_left(x), from_right(x)
    return tuple(lower[h] + upper[h] + left[h] + right[h] - 4.0 * x[h] for h in range(2))


def arrived(buf, BTS, tile, slots):
    for h in range(2):
        turned = buf[pl.ds(128 * h, 128), :].T
        BTS[pl.ds(0, 128), HALVES[h]] = turned
        BTS[pl.ds(128, 128), HALVES[h]] = turned
    out = []
    for f in range(slots):
        start = pl.multiple_of((8 * tile + 32 * f) % 128, 8)
        wide = BTS[pl.ds(start, 16), :]
        out.append(tuple((wide[0:8, hs], wide[1:9, hs], wide[2:10, hs]) for hs in HALVES))
    return out


def kernel(
    spec_h, wind_h, land_h, inter_h, ocean_h, sea_h, out_w, out_o, BR, BT, out_m, out_s,
    tab, B, G, PT, WD, CNT, H, S, wind, land, inter, NBS, NBR, QR, TS, TR, MSG2, MSG3, MMSG,
    Q, A1, A2, sea, CS, SX, MSG, MR, BTS, ES, EH, SEA3, LS, LH,
    load_sem, small_sem, h_send, h_recv, t_send, t_recv, nb_send, nb_recv,
    q_send, q_recv, m_send, m_recv, f_send, f_recv, g_send, g_recv, e_send, e_recv, l_send, l_recv, out_sem,
):
    grp = lax.axis_index("grp")
    tile = lax.axis_index("tile")
    sp = lax.axis_index("spec")
    other = 1 - sp
    sgn = (1 - 2 * sp).astype(F32)
    has_lo = tile > 0
    has_hi = tile < TILES - 1
    lo_t = jnp.maximum(tile - 1, 0)
    hi_t = jnp.minimum(tile + 1, TILES - 1)
    lane = lax.broadcasted_iota(jnp.int32, (8, 128), 1)
    row = lax.broadcasted_iota(jnp.int32, (8, 128), 0)
    first_lane, last_lane = lane == 0, lane == 127
    first_row, last_row = row == 0, row == 7
    low_rows = row < 4
    halves = HALVES

    def circular(x, shift):
        a, b = pltpu.roll(x[0], shift, 1), pltpu.roll(x[1], shift, 1)
        m = lane < shift
        return jnp.where(m, b, a), jnp.where(m, a, b)

    def barrel(x, amount):
        for bit in range(0, 8, 2):
            options = [x]
            for digit in range(1, 4):
                by = digit << bit
                y = circular(x, by % 128) if by % 128 else x
                options.append((y[1], y[0]) if by >= 128 else y)
            low = [(amount[h] & (1 << bit)) != 0 for h in range(2)]
            high = [(amount[h] & (2 << bit)) != 0 for h in range(2)]
            x = tuple(
                jnp.where(
                    high[h],
                    jnp.where(low[h], options[3][h], options[2][h]),
                    jnp.where(low[h], options[1][h], options[0][h]),
                )
                for h in range(2)
            )
        return x

    def pair(ref, *lead):
        return tuple(ref[(*lead, slice(None), hs)] for hs in halves)

    def put(ref, value, rows):
        for h in range(2):
            ref[rows, halves[h]] = value[h]

    barrier = pltpu.get_barrier_semaphore()

    def greet(where):
        pl.semaphore_signal(barrier, 1, device_id=where, device_id_type=pl.DeviceIdType.MESH)

    greet({"spec": other})

    @pl.when(has_lo)
    def _():
        greet({"tile": lo_t})
        greet({"tile": lo_t, "spec": other})

    @pl.when(has_hi)
    def _():
        greet({"tile": hi_t})
        greet({"tile": hi_t, "spec": other})

    def greet_across(u, carry):
        greet({"grp": 1 - grp, "tile": u})
        greet({"grp": 1 - grp, "tile": u, "spec": other})
        return carry

    lax.fori_loop(0, TILES, greet_across, 0)
    beside = jnp.where(has_lo, 2, 0) + jnp.where(has_hi, 2, 0)

    def everyone_in():
        pl.semaphore_wait(barrier, 2 * TILES + 1 + beside)

    @pl.when(grp == 0)
    def wave():
        def load(c):
            rows = pl.ds(pl.multiple_of(c * RCH * 8, 8), RCH * 8)
            return [
                pltpu.make_async_copy(spec_h.at[rows, hs], B.at[h, rows, :], load_sem.at[c, h])
                for h, hs in enumerate(halves)
            ]

        smalls = [
            pltpu.make_async_copy(wind_h, wind, small_sem.at[0]),
            pltpu.make_async_copy(land_h, land, small_sem.at[1]),
            pltpu.make_async_copy(inter_h, inter, small_sem.at[2]),
        ]
        for copy in smalls:
            copy.start()
        for q in range(TABLE.shape[0]):
            for f in range(FREQS):
                tab[q, f] = float(TABLE[q, f])

        def begin(c, carry):
            for copy in load(c):
                copy.start()
            return carry

        lax.fori_loop(0, CHUNKS, begin, 0)

        def halo(n, side, c):
            rows = pl.ds(pl.multiple_of(c * RCH, 8), RCH)
            return mesh_copy(
                S.at[n, side, :, rows, :], H.at[n, side, :, rows, :], h_send.at[n, side, c], h_recv.at[n, side, c],
                {"tile": hi_t if side == 0 else lo_t},
            )

        def edges_out(n, c):
            for k in range(RCH // 8):
                at = c * RCH + 8 * k
                rows = pl.ds(pl.multiple_of(at, 8), 8)
                for h in range(2):
                    S[n, 0, h, rows, :] = B[h, pl.ds(at * 8 + 7, 8, stride=8), :]
                    S[n, 1, h, rows, :] = B[h, pl.ds(at * 8, 8, stride=8), :]

            @pl.when(has_hi)
            def _():
                halo(n, 0, c).start()

            @pl.when(has_lo)
            def _():
                halo(n, 1, c).start()

        for copy in smalls:
            copy.wait()
        wet_i = pair(land)
        wet = tuple(x.astype(F32) for x in wet_i)
        shift = tuple((x - lane - 128 * h) & 255 for h, x in enumerate(pair(inter)))
        put(NBS, wet_i, slice(0, 8))
        put(NBS, shift, slice(8, 16))

        def neighbour(side):
            return mesh_copy(
                NBS, NBR.at[side], nb_send.at[side], nb_recv.at[side],
                {"tile": hi_t if side == 0 else lo_t},
            )

        everyone_in()

        @pl.when(has_hi)
        def _():
            neighbour(0).start()

        @pl.when(has_lo)
        def _():
            neighbour(1).start()

        wet_back = circular(barrel(wet, shift), 1)

        def windows(fields, u, pitch):
            acc = jnp.zeros((8, 128), F32)
            for f, field in enumerate(fields):
                start = (8 * u + pitch * f) % 128
                offset = (lane - start) & 127
                inside = offset < 10
                base = (8 * u) // 128
                p = 8 * u + offset
                value = field[base]
                if 8 * u % 128 + 10 > 128:
                    turned = (lane - pitch * f) & 127
                    value = jnp.where(turned < 16, field[1 - base], value)
                acc = jnp.where(inside, value, acc)
            return acc

        for u in range(TILES):
            MMSG[pl.ds(8 * u, 8), :] = windows([wet_back], u, 32)

        def to_ocean(src, dst, send, recv, u):
            return mesh_copy(
                src.at[pl.ds(pl.multiple_of(u * 8, 8), 8), :],
                dst.at[pl.ds(pl.multiple_of(tile * 8, 8), 8), :],
                send, recv, {"grp": 1, "tile": u},
            )

        def send_mask(u, carry):
            to_ocean(MMSG, MR, m_send, m_recv, u).start()
            return carry

        lax.fori_loop(0, TILES, send_mask, 0)

        @pl.when(jnp.logical_not(has_lo))
        def _():
            H[:, 0] = jnp.zeros((WSTEPS, 2, FD, 128), F32)
            NBR[0] = jnp.zeros((16, 256), jnp.int32)
            TR[:, 1:3] = jnp.zeros((WSTEPS, 2, 8, 256), F32)

        @pl.when(jnp.logical_not(has_hi))
        def _():
            H[:, 1] = jnp.zeros((WSTEPS, 2, FD, 128), F32)
            NBR[1] = jnp.zeros((16, 256), jnp.int32)
            TR[:, 3:5] = jnp.zeros((WSTEPS, 2, 8, 256), F32)

        def first_edges(c, carry):
            for copy in load(c):
                copy.wait()
            edges_out(0, c)
            return carry

        lax.fori_loop(0, CHUNKS, first_edges, 0)

        for d in range(DLOC):
            for h, hs in enumerate(halves):
                WD[d, :, hs] = wind[0, :, hs] * (sgn * COS[d]) + wind[1, :, hs] * (sgn * SIN[d])

        def growth(f, carry):
            slope = tab[1, f]
            sgs = tab[0, f] * sgn
            for d in range(DLOC):
                i = f * DLOC + d
                rows = pl.ds(pl.multiple_of(i * 8, 8), 8)
                for h, hs in enumerate(halves):
                    G[h, rows, :] = 1.0 + jnp.maximum(WD[d, :, hs] * slope - 0.05, 0.0)
                CNT[pl.ds(i, 1), :] = jnp.full((1, 128), sgs * SIN[d], F32)
            return carry

        lax.fori_loop(0, FREQS, growth, 0)

        @pl.when(has_lo)
        def _():
            neighbour(0).wait_recv()

        @pl.when(has_hi)
        def _():
            neighbour(1).wait_recv()

        edge_i = tuple(
            jnp.where(low_rows, NBR[1, 0:8, hs], NBR[0, 0:8, hs]) for hs in halves
        )
        edge_wet = tuple(x.astype(F32) for x in edge_i)
        edge_shift = tuple(
            jnp.where(low_rows, NBR[1, 8:16, hs], NBR[0, 8:16, hs]) for hs in halves
        )

        settle(QR, q_recv)
        group = lax.broadcasted_iota(jnp.int32, (4, 128), 1) >> 3
        parts = [[], [], [], [], []]
        for h in range(2):
            upper = [jnp.zeros((4, 128), F32)] * 5
            lower = [jnp.zeros((4, 128), F32)] * 5
            for k in range(16):
                m = QR[0, 16 * h + k] + QR[1, 16 * h + k]
                turned = pltpu.roll(m, 64, 1)
                for c in range(5):
                    at = (k + c) % 16
                    near, far = (m, turned) if at < 8 else (turned, m)
                    upper[c] = jnp.where(group == at, near, upper[c])
                    lower[c] = jnp.where(group == at, far, lower[c])
            for c in range(5):
                acc = jnp.concatenate([upper[c], lower[c]], axis=0)
                parts[c].append(pltpu.roll(acc, 128 - 8 * c, 1) if c else acc)
        fields = [tuple(x) for x in parts]
        left = tuple((256 - x) & 255 for x in shift)
        edge_left = tuple((256 - x) & 255 for x in edge_shift)
        u01 = tuple(0.1 * x for x in barrel(fields[0], left))
        v01 = tuple(0.1 * x for x in barrel(fields[1], left))

        def stiffness(level):
            depth = tuple(10.0 + 4.0 * x for x in level)
            return tuple(25.0 / (x * x) for x in depth)

        stiff = stiffness(barrel(fields[2], left))
        edge_v = tuple(0.1 * x for x in barrel(fields[3], edge_left))
        edge_stiff = stiffness(barrel(fields[4], edge_left))
        v_lo = tuple(jnp.broadcast_to(x[7:8], (8, 128)) for x in edge_v)
        v_hi = tuple(jnp.broadcast_to(x[0:1], (8, 128)) for x in edge_v)

        def halo_in(n, c, scale=None):
            @pl.when(has_lo)
            def _():
                halo(n, 0, c).wait_recv()

            @pl.when(has_hi)
            def _():
                halo(n, 1, c).wait_recv()

            for k in range(RCH // 8):
                rows = pl.ds(pl.multiple_of(c * RCH + 8 * k, 8), 8)
                cn = CNT[rows, :]
                for h in range(2):
                    lower, upper = H[n, 0, h, rows, :], H[n, 1, h, rows, :]
                    if scale is not None:
                        lower, upper = scale[0][h] * lower, scale[1][h] * upper
                    H[n, 0, h, rows, :] = jnp.maximum((cn + v_lo[h]) * lower, 0.0)
                    H[n, 1, h, rows, :] = jnp.minimum((cn + v_hi[h]) * upper, 0.0)

        def terms(n, i, rows, ce, cn, r=None):
            b = [B[h, rows, :] for h in range(2)]
            if r is not None:
                b = [r[h] * b[h] for h in range(2)]
            X = [(u01[h] + ce) * b[h] for h in range(2)]
            Y = [(v01[h] + cn) * b[h] for h in range(2)]
            own = [(b[h] - jnp.abs(X[h])) - jnp.abs(Y[h]) for h in range(2)]
            west, east = [jnp.maximum(x, 0.0) for x in X], [jnp.minimum(x, 0.0) for x in X]
            if r is not None:
                west, east = from_left(west), from_right(east)
            else:
                a = [pltpu.roll(x, 1, 1) for x in west]
                west = [a[0], jnp.where(first_lane, a[0], a[1])]
                a = [pltpu.roll(x, 127, 1) for x in east]
                east = [jnp.where(last_lane, a[1], a[0]), a[1]]
            south = [
                jnp.where(
                    first_row, H[n, 0, h, pl.ds(i, 8, stride=0), :], pltpu.roll(jnp.maximum(Y[h], 0.0), 1, 0)
                )
                for h in range(2)
            ]
            north = [
                jnp.where(
                    last_row, H[n, 1, h, pl.ds(i, 8, stride=0), :], pltpu.roll(jnp.minimum(Y[h], 0.0), 7, 0)
                )
                for h in range(2)
            ]
            return own, west, east, south, north

        def ahead(n):
            def chunk(c, carry):
                halo_in(n, c)

                def band(fc, carry):
                    f = c * FCH + fc
                    sgs = tab[0, f] * sgn
                    for d in range(DLOC):
                        i = f * DLOC + d
                        rows = pl.ds(pl.multiple_of(i * 8, 8), 8)
                        for q, term in enumerate(terms(n, i, rows, sgs * COS[d], sgs * SIN[d])):
                            for h in range(2):
                                PT[q, h, rows, :] = term[h]
                    return carry

                return lax.fori_loop(0, FCH, band, carry, unroll=2)

            lax.fori_loop(0, PCH, chunk, 0)

        def factors(r, edge_r):
            a, b = [pltpu.roll(x, 1, 1) for x in r], [pltpu.roll(x, 127, 1) for x in r]
            r_w = (jnp.where(first_lane, 0.0, a[0]), jnp.where(first_lane, a[0], a[1]))
            r_e = (jnp.where(last_lane, b[1], b[0]), jnp.where(last_lane, 0.0, b[1]))
            r_s = tuple(jnp.where(first_row, pltpu.roll(edge_r[h], 1, 0), pltpu.roll(r[h], 1, 0)) for h in range(2))
            r_n = tuple(jnp.where(last_row, pltpu.roll(edge_r[h], 7, 0), pltpu.roll(r[h], 7, 0)) for h in range(2))
            return tuple(r), r_w, r_e, r_s, r_n

        def sweep(n, r, edge_r, last):
            r_all = factors(r, edge_r)
            scale = (
                tuple(jnp.broadcast_to(x[7:8], (8, 128)) for x in edge_r),
                tuple(jnp.broadcast_to(x[0:1], (8, 128)) for x in edge_r),
            )

            def chunk(c, sums, prepared):
                if not prepared:
                    halo_in(n, c, scale)

                def band(fc, sums):
                    f = c * FCH + fc
                    sgs = tab[0, f] * sgn
                    zero = jnp.zeros((8, 128), F32)
                    acc = [[zero, zero] for _ in range(5 if last else 1)]
                    half_way = {}
                    for d in (DIR_ORDER if last else range(DLOC)):
                        i = f * DLOC + d
                        rows = pl.ds(pl.multiple_of(i * 8, 8), 8)
                        if prepared:
                            five = [[r_all[q][h] * PT[q, h, rows, :] for h in range(2)] for q in range(5)]
                        else:
                            five = terms(n, i, rows, sgs * COS[d], sgs * SIN[d], r)
                        for h in range(2):
                            own, west, east, south, north = (five[q][h] for q in range(5))
                            adv = own + ((west - east) + (south - north))
                            new = adv * G[h, rows, :]
                            B[h, rows, :] = new
                            acc[0][h] += adv
                            if last:
                                mine = (new - adv, new)
                                if h not in half_way:
                                    half_way[h] = mine
                                    continue
                                for q, (a, b) in enumerate(zip(half_way.pop(h), mine)):
                                    acc[1 + 2 * q][h] += (a - b) * COS[DLOC - 1 - d]
                                    acc[2 + 2 * q][h] += (a + b) * SIN[d]
                    weights = [tab[2, f], tab[3, f], tab[3, f], tab[4, f], tab[4, f]]
                    if last:
                        weights = weights[:1] + [w * sgn for w in weights[1:]]
                    return tuple(
                        tuple(total[h] + acc[q][h] * weights[q] for h in range(2)) for q, total in enumerate(sums)
                    )

                sums = lax.fori_loop(0, FCH, band, sums, unroll=2)
                if not last:

                    @pl.when(c < CHUNKS - HELD)
                    def _():
                        edges_out(n + 1, c)

                return sums

            zero = jnp.zeros((8, 128), F32)
            sums = tuple((zero, zero) for _ in range(5 if last else 1))
            begun = PCH if last else jnp.where(n > 0, PCH, 0)
            sums = lax.fori_loop(0, begun, lambda c, x: chunk(c, x, True), sums)
            return lax.fori_loop(begun, CHUNKS, lambda c, x: chunk(c, x, False), sums)

        def total_copies(n):
            return [
                (None, mesh_copy(TS.at[n], TR.at[n, 0], t_send.at[n, 0], t_recv.at[n, 0], {"spec": other})),
                (has_hi, mesh_copy(TS.at[n], TR.at[n, 1], t_send.at[n, 1], t_recv.at[n, 1], {"tile": hi_t})),
                (has_hi, mesh_copy(TS.at[n], TR.at[n, 2], t_send.at[n, 2], t_recv.at[n, 2], {"tile": hi_t, "spec": other})),
                (has_lo, mesh_copy(TS.at[n], TR.at[n, 3], t_send.at[n, 3], t_recv.at[n, 3], {"tile": lo_t})),
                (has_lo, mesh_copy(TS.at[n], TR.at[n, 4], t_send.at[n, 4], t_recv.at[n, 4], {"tile": lo_t, "spec": other})),
            ]

        def gated(condition, action):
            if condition is None:
                action()
            else:
                pl.when(condition)(action)

        def one_step(n, carry):
            r, edge_r = carry
            (total,) = sweep(n, r, edge_r, False)
            for h, hs in enumerate(halves):
                TS[n, :, hs] = total[h]
            copies = total_copies(n)
            for condition, copy in copies:
                gated(condition, copy.start)

            def late(c, carry):
                edges_out(n + 1, c)
                return carry

            lax.fori_loop(CHUNKS - HELD, CHUNKS, late, 0)
            ahead(n + 1)
            for (_, copy), condition in zip(copies, [None, has_lo, has_lo, has_hi, has_hi]):
                gated(condition, copy.wait_recv)
            new_r, new_edge = [], []
            for h, hs in enumerate(halves):
                full = total[h] + TR[n, 0, :, hs]
                new_r.append(wet[h] / (1.0 + stiff[h] * full))
                lower = TR[n, 1, :, hs] + TR[n, 2, :, hs]
                upper = TR[n, 3, :, hs] + TR[n, 4, :, hs]
                edge = jnp.where(low_rows, upper, lower)
                new_edge.append(edge_wet[h] / (1.0 + edge_stiff[h] * edge))
            return tuple(new_r), tuple(new_edge)

        r, edge_r = lax.fori_loop(0, WSTEPS - 1, one_step, (wet, edge_wet))
        n = WSTEPS - 1
        sums = sweep(n, r, edge_r, True)
        for h, hs in enumerate(halves):
            TS[n, :, hs] = sums[0][h]
        swap = mesh_copy(TS.at[n], TR.at[n, 0], t_send.at[n, 0], t_recv.at[n, 0], {"spec": other})
        swap.start()
        turned = [circular(barrel(sums[q], shift), 1) for q in (0, 3, 4, 1, 2)]
        slots = [tuple(pltpu.roll(x, 16 * f, 1) if f else x for x in field) for f, field in enumerate(turned[:4])]
        slot = lax.broadcasted_iota(jnp.int32, (4, 128), 1) < 64
        for fields, out in ((slots, MSG2), (turned[4:], MSG3)):
            for u in range(TILES):
                wide = windows(fields, u, 16)
                wide = wide + pltpu.roll(wide, 64, 1)
                out[u] = jnp.where(slot, wide[0:4], wide[4:8])

        def bands_to(src, dst, send, recv, u, half):
            return mesh_copy(src.at[u], dst.at[sp, tile], send, recv, {"grp": 1, "tile": u, "spec": half})

        def send_bands(u, carry):
            bands_to(MSG2, BR, f_send, f_recv, u, sp).start()
            bands_to(MSG2, BR, f_send, f_recv, u, other).start()
            bands_to(MSG3, BT, g_send, g_recv, u, 0).start()
            return carry

        lax.fori_loop(0, TILES, send_bands, 0)
        swap.wait_recv()
        final = tuple(
            wet[h] / (1.0 + stiff[h] * (sums[0][h] + TR[n, 0, :, halves[h]])) for h in range(2)
        )

        def store(c):
            rows = pl.ds(pl.multiple_of(c * RCH * 8, 8), RCH * 8)
            return [
                pltpu.make_async_copy(B.at[h, rows, :], out_w.at[rows, hs], load_sem.at[c, h])
                for h, hs in enumerate(halves)
            ]

        def finish(c, carry):
            def scale_f(i, carry):
                for d in range(DLOC):
                    rows = pl.ds(pl.multiple_of((c * RCH + i * DLOC + d) * 8, 8), 8)
                    for h in range(2):
                        B[h, rows, :] = B[h, rows, :] * final[h]
                return carry

            lax.fori_loop(0, FCH, scale_f, 0)
            for copy in store(c):
                copy.start()
            return carry

        lax.fori_loop(0, CHUNKS, finish, 0)
        def drain(c, carry):
            for copy in store(c):
                copy.wait()

            @pl.when(has_hi)
            def _():
                for n in range(WSTEPS):
                    halo(n, 0, c).wait_send()

            @pl.when(has_lo)
            def _():
                for n in range(WSTEPS):
                    halo(n, 1, c).wait_send()

            return carry

        lax.fori_loop(0, CHUNKS, drain, 0)
        for m in range(WSTEPS - 1):
            for condition, copy in total_copies(m):
                gated(condition, copy.wait_send)
        swap.wait_send()
        gated(has_hi, neighbour(0).wait_send)
        gated(has_lo, neighbour(1).wait_send)
        settle(MMSG, m_send)
        settle(BR, f_send)
        settle(MSG3, g_send)

    @pl.when(grp == 1)
    def circulation():
        top = (1 - sp).astype(F32)
        deep = sp.astype(F32)
        down = jnp.where(sp == 0, 1.0, math.exp(-1.0)).astype(F32)
        loads = [
            pltpu.make_async_copy(ocean_h.at[:, halves[0]], Q.at[0], small_sem.at[0]),
            pltpu.make_async_copy(ocean_h.at[:, halves[1]], Q.at[1], small_sem.at[1]),
            pltpu.make_async_copy(sea_h, sea, small_sem.at[2]),
        ]
        for copy in loads:
            copy.start()
        for copy in loads:
            copy.wait()
        for c in range(2):
            for h, hs in enumerate(halves):
                acc = jnp.zeros((8, 128), F32)
                for k in range(KLOC):
                    acc += Q[h, pl.ds((c * KLOC + k) * 8, 8), :] * float(_wgt[k])
                CS[pl.ds(8 * c, 8), hs] = acc * down

        def edge(n, side):
            return mesh_copy(
                ES.at[n, side], EH.at[n, side], e_send.at[n, side], e_recv.at[n, side],
                {"tile": hi_t if side == 0 else lo_t},
            )

        def level(n):
            return mesh_copy(LS.at[n], LH.at[n], l_send.at[n], l_recv.at[n], {"spec": other})

        def rims_out(n, src):
            for c in range(3):
                for h, hs in enumerate(halves):
                    ES[n, 0, pl.ds(8 * c, 8), hs] = src[h, pl.ds(c * 64 + 7, 8, stride=8), :]
                    ES[n, 1, pl.ds(8 * c, 8), hs] = src[h, pl.ds(c * 64, 8, stride=8), :]
                    LS[n, pl.ds(8 * c, 8), hs] = jnp.where(
                        sp == 0, src[h, pl.ds(c * 64 + 56, 8), :], src[h, pl.ds(c * 64, 8), :]
                    )
            for side in range(2):
                ES[n, side, 24:32, :] = sea[...]
            pl.when(has_hi)(edge(n, 0).start)
            pl.when(has_lo)(edge(n, 1).start)
            level(n).start()

        SX[...] = jnp.zeros((128, 256), F32)
        put(SX, tuple(0.5 * x for x in pair(sea)), slice(16, 24))
        SX[0:16, :] = CS[...]
        ahead_rows = (lane & 7) < 4
        for c in range(2):
            src = tuple(SX[pl.ds(8 + 8 * c, 8), hs] for hs in halves)
            ahead, behind = circular(src, 120), circular(src, 8)
            ahead = (ahead[1], ahead[0])
            put(SX, tuple(jnp.where(ahead_rows, ahead[h], behind[h]) for h in range(2)), slice(24 + 8 * c, 32 + 8 * c))
        slot = lax.broadcasted_iota(jnp.int32, (4, 128), 1) < 64
        for h, hs in enumerate(halves):
            turned = pltpu.roll(SX[:, hs].T, tile % 8 * 8, 1)
            turned = turned + pltpu.roll(turned, 64, 1)
            for k in range(16):
                MSG[16 * h + k] = jnp.where(slot, turned[8 * k : 8 * k + 4], turned[8 * k + 4 : 8 * k + 8])
        everyone_in()

        def to_wave(u, half):
            return mesh_copy(
                MSG.at[u], QR.at[sp, tile], q_send, q_recv, {"grp": 0, "tile": u, "spec": half},
            )

        def send_q(u, carry):
            to_wave(u, sp).start()
            to_wave(u, other).start()
            return carry

        lax.fori_loop(0, TILES, send_q, 0)
        rims_out(0, Q)

        @pl.when(jnp.logical_not(has_lo))
        def _():
            EH[:, 0] = jnp.zeros((2, 32, 256), F32)

        @pl.when(jnp.logical_not(has_hi))
        def _():
            EH[:, 1] = jnp.zeros((2, 32, 256), F32)

        settle(MR, m_recv)
        flags = pltpu.make_async_copy(MR, out_m, small_sem.at[0])
        flags.start()
        (mask3,) = arrived(MR, BTS, tile, 1)
        mask = tuple(x[1] for x in mask3)

        def substep(n, src, dst):
            for c in range(3):
                for k in range(KLOC):
                    at = (c * KLOC + k) * 8
                    x = tuple(src[h, pl.ds(at, 8), :] for h in range(2))
                    row_at = 8 * c + k
                    lower = tuple(
                        jnp.where(first_row, EH[n, 0, row_at : row_at + 1, hs], pltpu.roll(x[h], 1, 0))
                        for h, hs in enumerate(halves)
                    )
                    upper = tuple(
                        jnp.where(last_row, EH[n, 1, row_at : row_at + 1, hs], pltpu.roll(x[h], 7, 0))
                        for h, hs in enumerate(halves)
                    )
                    side = lateral(x, lower, upper)
                    for h, hs in enumerate(halves):
                        if k > 0:
                            above = src[h, pl.ds(at - 8, 8), :]
                        else:
                            above = LH[n, pl.ds(8 * c, 8), hs] * deep
                        if k < KLOC - 1:
                            below = src[h, pl.ds(at + 8, 8), :]
                        else:
                            below = LH[n, pl.ds(8 * c, 8), hs] * top
                        value = x[h] + 0.1 * side[h] + 0.2 * (above + below - 2.0 * x[h])
                        if c == 0:
                            value = value + 0.1 * src[h, pl.ds(at + 64, 8), :]
                        if c == 1:
                            value = value - 0.1 * src[h, pl.ds(at - 64, 8), :]
                        dst[h, pl.ds(at, 8), :] = value * mask[h]

        def rims_in(n):
            pl.when(has_lo)(edge(n, 0).wait_recv)
            pl.when(has_hi)(edge(n, 1).wait_recv)
            level(n).wait_recv()

        rims_in(0)
        for h, hs in enumerate(halves):
            level_here = sea[:, hs]
            SEA3[0:8, hs] = jnp.where(first_row, EH[0, 0, 31:32, hs], pltpu.roll(level_here, 1, 0))
            SEA3[8:16, hs] = level_here
            SEA3[16:24, hs] = jnp.where(last_row, EH[0, 1, 24:25, hs], pltpu.roll(level_here, 7, 0))
        seas = pltpu.make_async_copy(SEA3, out_s, small_sem.at[1])
        seas.start()
        substep(0, Q, A1)
        rims_out(1, A1)
        rims_in(1)
        substep(1, A1, A2)

        results = [pltpu.make_async_copy(A2.at[h], out_o.at[:, hs], out_sem.at[h]) for h, hs in enumerate(halves)]
        for copy in results:
            copy.start()
        for n in range(2):
            pl.when(has_hi)(edge(n, 0).wait_send)
            pl.when(has_lo)(edge(n, 1).wait_send)
            level(n).wait_send()
        settle(QR, q_send)
        flags.wait()
        seas.wait()
        for copy in results:
            copy.wait()
        settle(BR, f_recv)
        pl.when(sp == 0)(lambda: settle(BT, g_recv))


def tail(wave_h, unforced_h, bands_h, north_h, flags_h, sea_h, out_w, out_o, zeros, A2, BR, BT, MR, U, sea, BTS, in_sem, w_sem, o_sem):
    grp = lax.axis_index("grp")
    tile = lax.axis_index("tile")
    sp = lax.axis_index("spec")

    @pl.when(grp == 0)
    def wave():
        copies = []
        for c in range(CHUNKS):
            rows = pl.ds(c * RCH * 8, RCH * 8)
            copies.append(pltpu.make_async_copy(wave_h.at[rows, :], out_w.at[rows, :], w_sem.at[c]))
            copies[-1].start()
        zeros[0:192, :] = jnp.zeros((192, 256), F32)
        copies.append(pltpu.make_async_copy(zeros.at[0:192, :], out_o, o_sem.at[0]))
        copies[-1].start()
        for copy in copies:
            copy.wait()

    @pl.when(grp == 1)
    def circulation():
        loads = [
            pltpu.make_async_copy(flags_h, MR, in_sem.at[0]),
            pltpu.make_async_copy(bands_h, BR, in_sem.at[1]),
            pltpu.make_async_copy(sea_h, sea, in_sem.at[4]),
        ] + [pltpu.make_async_copy(unforced_h.at[:, hs], A2.at[h], in_sem.at[2 + h]) for h, hs in enumerate(HALVES)]
        for copy in loads:
            copy.start()
        norths = pltpu.make_async_copy(north_h, BT, in_sem.at[5])

        @pl.when(sp == 0)
        def _():
            norths.start()

        zeros[...] = jnp.zeros(zeros.shape, F32)
        blanks = []
        for c in range(CHUNKS):
            rows = pl.ds(c * RCH * 8, RCH * 8)
            blanks.append(pltpu.make_async_copy(zeros, out_w.at[rows, :], w_sem.at[c]))
            blanks[-1].start()
        row = lax.broadcasted_iota(jnp.int32, (8, 128), 0)
        top = (1 - sp).astype(F32)
        deep = sp.astype(F32)
        down = jnp.where(sp == 0, 1.0, math.exp(-1.0)).astype(F32)
        at_lo = jnp.where(tile > 0, 1.0, 0.0).astype(F32)
        at_hi = jnp.where(tile < TILES - 1, 1.0, 0.0).astype(F32)
        loads[0].wait()
        (mask3,) = arrived(MR, BTS, tile, 1)
        mask = tuple(x[1] for x in mask3)
        mask_lo = tuple(jnp.where(row == 0, x[0] * at_lo, x[0]) for x in mask3)
        mask_hi = tuple(jnp.where(row == 7, x[2] * at_hi, x[2]) for x in mask3)
        for copy in loads[1:]:
            copy.wait()

        @pl.when(sp == 0)
        def _():
            norths.wait()

        @pl.when(sp == 1)
        def _():
            BT[...] = jnp.zeros(BT.shape, F32)

        def unpacked(buf, slots):
            for t in range(TILES):
                both = buf[0, t] + buf[1, t]
                U[8 * t : 8 * t + 8, :] = jnp.concatenate([both, pltpu.roll(both, 64, 1)], axis=0)
            for h in range(2):
                turned = U[pl.ds(128 * h, 128), :].T
                BTS[pl.ds(0, 64), HALVES[h]] = turned[0:64]
                BTS[pl.ds(64, 64), HALVES[h]] = turned[0:64]
            out = []
            for f in range(slots):
                start = pl.multiple_of((8 * tile + 16 * f) % 64, 8)
                wide = BTS[pl.ds(start, 16), :]
                out.append(tuple((wide[0:8, hs], wide[1:9, hs], wide[2:10, hs]) for hs in HALVES))
            return out

        total, drift_e, drift_n, stress_e = unpacked(BR, 4)
        (stress_n,) = unpacked(BT, 1)
        factor = []
        for h, hs in enumerate(HALVES):
            row_of = []
            for q, masked in enumerate((mask_lo, mask, mask_hi)):
                depth = 10.0 + 4.0 * sea[8 * q : 8 * q + 8, hs]
                row_of.append(masked[h] / (1.0 + 25.0 * total[h][q] / (depth * depth)))
            factor.append(row_of)
        forced, spread = [], []
        for three in (stress_e, stress_n, drift_e, drift_n):
            lower, own, upper = (tuple(three[h][q] * factor[h][q] for h in range(2)) for q in range(3))
            forced.append(own)
            spread.append(lateral(own, lower, upper))
        for k in range(KLOC):
            near, far = math.exp(0.125), math.exp(-0.125)
            prof = float(_prof[k]) * down
            above = near if k > 0 else near * deep
            below = far if k < KLOC - 1 else far * top
            stay = prof * (1.0 + 0.2 * (above + below - 2.0))
            for h, hs in enumerate(HALVES):
                east = (0.1 * prof) * forced[3][h]
                north = (-0.1 * prof) * forced[2][h]
                d_east = (0.1 * stay) * forced[3][h] + (0.01 * prof) * spread[3][h]
                d_north = (-0.1 * stay) * forced[2][h] - (0.01 * prof) * spread[2][h]
                if k == 0:
                    east = east + top * forced[0][h]
                    north = north + top * forced[1][h]
                    d_east = d_east + top * (0.6 * forced[0][h] + 0.1 * spread[0][h])
                    d_north = d_north + top * (0.6 * forced[1][h] + 0.1 * spread[1][h])
                if k == 1:
                    d_east = d_east + (0.2 * top) * forced[0][h]
                    d_north = d_north + (0.2 * top) * forced[1][h]
                A2[h, pl.ds(8 * k, 8), :] += mask[h] * (d_east + 0.1 * north) + east
                A2[h, pl.ds(64 + 8 * k, 8), :] += mask[h] * (d_north - 0.1 * east) + north
        results = [pltpu.make_async_copy(A2.at[h], out_o.at[:, hs], o_sem.at[h]) for h, hs in enumerate(HALVES)]
        for copy in results:
            copy.start()

        for copy in results + blanks:
            copy.wait()


def body(spectrum, wind, land_mask, intersection, ocean_state, sea_level):
    v = lambda *shape, dtype=F32: pltpu.VMEM(shape, dtype)
    dma = lambda *shape: pltpu.SemaphoreType.DMA(shape) if shape else pltpu.SemaphoreType.DMA
    anywhere = pl.BlockSpec(memory_space=pltpu.HBM)
    scratch = [
        pltpu.SMEM(TABLE.shape, F32),
        v(2, FD * 8, 128), v(2, FD * 8, 128), v(5, 2, PCH * RCH * 8, 128), v(DLOC, 8, 256), v(FD, 128),
        v(WSTEPS, 2, 2, FD, 128), v(WSTEPS, 2, 2, FD, 128),
        v(2, 8, 256), v(8, 256, dtype=jnp.int32), v(8, 256, dtype=jnp.int32),
        v(16, 256, dtype=jnp.int32), v(2, 16, 256, dtype=jnp.int32),
        v(2, TILES, 4, 128), v(WSTEPS, 8, 256), v(WSTEPS, 5, 8, 256), v(TILES, 4, 128), v(TILES, 4, 128), v(256, 128),
        v(2, 192, 128), v(2, 192, 128), v(2, 192, 128), v(8, 256), v(16, 256), v(128, 256),
        v(TILES, 4, 128), v(256, 128), v(256, 256),
        v(2, 2, 32, 256), v(2, 2, 32, 256), v(24, 256), v(2, 24, 256), v(2, 24, 256),
        dma(CHUNKS, 2), dma(3), dma(WSTEPS, 2, CHUNKS), dma(WSTEPS, 2, CHUNKS), dma(WSTEPS, 5), dma(WSTEPS, 5),
        dma(2), dma(2), dma(), dma(), dma(), dma(), dma(), dma(), dma(), dma(),
        dma(2, 2), dma(2, 2), dma(2), dma(2), dma(2),
    ]
    landed = pl.pallas_call(
        kernel,
        out_shape=(
            jax.ShapeDtypeStruct((FD * 8, 256), F32),
            jax.ShapeDtypeStruct((192, 256), F32),
            jax.ShapeDtypeStruct((2, TILES, 4, 128), F32),
            jax.ShapeDtypeStruct((2, TILES, 4, 128), F32),
            jax.ShapeDtypeStruct((256, 128), F32),
            jax.ShapeDtypeStruct((24, 256), F32),
        ),
        in_specs=[anywhere] * 6,
        out_specs=(pl.BlockSpec(memory_space=pl.ANY),) * 6,
        scratch_shapes=scratch,
        compiler_params=pltpu.CompilerParams(collective_id=0, has_side_effects=True, vmem_limit_bytes=48 << 20),
    )(
        *(
            pltpu.with_memory_space_constraint(x, pltpu.HBM)
            for x in (
                spectrum.reshape(FD * 8, 256),
                wind,
                land_mask,
                intersection,
                ocean_state.reshape(192, 256),
                sea_level.reshape(8, 256),
            )
        )
    )
    waves, ocean = pl.pallas_call(
        tail,
        out_shape=(jax.ShapeDtypeStruct((FD * 8, 256), F32), jax.ShapeDtypeStruct((192, 256), F32)),
        in_specs=[pl.BlockSpec(memory_space=pl.ANY)] * 6,
        out_specs=(pl.BlockSpec(memory_space=pl.ANY),) * 2,
        scratch_shapes=[
            v(RCH * 8, 256), v(2, 192, 128), v(2, TILES, 4, 128), v(2, TILES, 4, 128), v(256, 128), v(256, 128),
            v(24, 256), v(256, 256), dma(6), dma(CHUNKS), dma(2),
        ],
        compiler_params=pltpu.CompilerParams(vmem_limit_bytes=6 << 20),
    )(*landed)
    return waves.reshape(spectrum.shape), ocean.reshape(ocean_state.shape)


def solution(mesh):
    return jax.shard_map(
        body,
        mesh=mesh,
        in_specs=(
            P("grp", None, "spec", "tile", None),
            P(None, "tile", None),
            P("tile", None),
            P("tile", None),
            P("grp", None, "spec", "tile", None),
            P("grp", "tile", None),
        ),
        out_specs=(P("grp", None, "spec", "tile", None), P("grp", None, "spec", "tile", None)),
        check_vma=False,
    )
```

```python
import math

import jax
import jax.numpy as jnp
import numpy as np
from jax import lax
from jax.experimental import pallas as pl
from jax.experimental.pallas import tpu as pltpu
from jax.sharding import PartitionSpec as P

FREQS = 32
DIRS = 36
LEVELS = 16
WSTEPS = 4
TILES = 32
DLOC = 18
KLOC = 8
FD = FREQS * DLOC
CHUNKS = 8
FCH = FREQS // CHUNKS
RCH = FCH * DLOC
PCH = 4
HELD = 4
F32 = jnp.float32

_freq = 0.04 * 1.1 ** np.arange(FREQS)
_cel = 1.56 / _freq
_gs = 0.4 * 1.1 ** (-np.arange(FREQS, dtype=np.float64))
_bw = 0.1 * _freq * (2.0 * math.pi / DIRS)
TABLE = np.stack([_gs, 0.05 / _cel, _bw, 5.0 * _bw / _cel, 20.0 * _bw * _freq**3]).astype(np.float32)
_ang = 2.0 * math.pi * (np.arange(DIRS) + 0.5) / DIRS
COS = [float(np.float32(x)) for x in np.cos(_ang)[:DLOC]]
SIN = [float(np.float32(x)) for x in np.sin(_ang)[:DLOC]]
DIR_ORDER = [d for k in range(DLOC // 2) for d in (k, DLOC - 1 - k)]
_prof = np.exp(-2.0 * (np.arange(LEVELS) + 0.5) / LEVELS)
_wgt = _prof / _prof.sum()


def mesh_copy(src, dst, send, recv, where):
    return pltpu.make_async_remote_copy(
        src_ref=src,
        dst_ref=dst,
        send_sem=send,
        recv_sem=recv,
        device_id=where,
        device_id_type=pl.DeviceIdType.MESH,
    )


def settle(buf, sem):
    pltpu.make_async_copy(buf, buf, sem).wait()


HALVES = (slice(0, 128), slice(128, 256))


def at_lane(k):
    return lax.broadcasted_iota(jnp.int32, (8, 128), 1) == k


def from_left(x):
    a, b = pltpu.roll(x[0], 1, 1), pltpu.roll(x[1], 1, 1)
    return jnp.where(at_lane(0), 0.0, a), jnp.where(at_lane(0), a, b)


def from_right(x):
    a, b = pltpu.roll(x[0], 127, 1), pltpu.roll(x[1], 127, 1)
    return jnp.where(at_lane(127), b, a), jnp.where(at_lane(127), 0.0, b)


def lateral(x, lower, upper):
    left, right = from_left(x), from_right(x)
    return tuple(lower[h] + upper[h] + left[h] + right[h] - 4.0 * x[h] for h in range(2))


def arrived(buf, BTS, tile, slots):
    for h in range(2):
        turned = buf[pl.ds(128 * h, 128), :].T
        BTS[pl.ds(0, 128), HALVES[h]] = turned
        BTS[pl.ds(128, 128), HALVES[h]] = turned
    out = []
    for f in range(slots):
        start = pl.multiple_of((8 * tile + 32 * f) % 128, 8)
        wide = BTS[pl.ds(start, 16), :]
        out.append(tuple((wide[0:8, hs], wide[1:9, hs], wide[2:10, hs]) for hs in HALVES))
    return out


def kernel(
    spec_h, wind_h, land_h, inter_h, ocean_h, sea_h, out_w, out_o, BR, BT, out_m, out_s,
    tab, B, G, PT, WD, CNT, H, S, wind, land, inter, NBS, NBR, QR, TS, TR, MSG2, MSG3, MMSG,
    Q, A1, A2, sea, CS, SX, MSG, MR, BTS, ES, EH, SEA3, LS, LH,
    load_sem, small_sem, h_send, h_recv, t_send, t_recv, nb_send, nb_recv,
    q_send, q_recv, m_send, m_recv, f_send, f_recv, g_send, g_recv, e_send, e_recv, l_send, l_recv, out_sem,
):
    grp = lax.axis_index("grp")
    tile = lax.axis_index("tile")
    sp = lax.axis_index("spec")
    other = 1 - sp
    sgn = (1 - 2 * sp).astype(F32)
    has_lo = tile > 0
    has_hi = tile < TILES - 1
    lo_t = jnp.maximum(tile - 1, 0)
    hi_t = jnp.minimum(tile + 1, TILES - 1)
    lane = lax.broadcasted_iota(jnp.int32, (8, 128), 1)
    row = lax.broadcasted_iota(jnp.int32, (8, 128), 0)
    first_lane, last_lane = lane == 0, lane == 127
    first_row, last_row = row == 0, row == 7
    low_rows = row < 4
    halves = HALVES

    def circular(x, shift):
        a, b = pltpu.roll(x[0], shift, 1), pltpu.roll(x[1], shift, 1)
        m = lane < shift
        return jnp.where(m, b, a), jnp.where(m, a, b)

    def barrel(x, amount):
        for bit in range(0, 8, 2):
            options = [x]
            for digit in range(1, 4):
                by = digit << bit
                y = circular(x, by % 128) if by % 128 else x
                options.append((y[1], y[0]) if by >= 128 else y)
            low = [(amount[h] & (1 << bit)) != 0 for h in range(2)]
            high = [(amount[h] & (2 << bit)) != 0 for h in range(2)]
            x = tuple(
                jnp.where(
                    high[h],
                    jnp.where(low[h], options[3][h], options[2][h]),
                    jnp.where(low[h], options[1][h], options[0][h]),
                )
                for h in range(2)
            )
        return x

    def pair(ref, *lead):
        return tuple(ref[(*lead, slice(None), hs)] for hs in halves)

    def put(ref, value, rows):
        for h in range(2):
            ref[rows, halves[h]] = value[h]

    barrier = pltpu.get_barrier_semaphore()

    def greet(where):
        pl.semaphore_signal(barrier, 1, device_id=where, device_id_type=pl.DeviceIdType.MESH)

    greet({"spec": other})

    @pl.when(has_lo)
    def _():
        greet({"tile": lo_t})
        greet({"tile": lo_t, "spec": other})

    @pl.when(has_hi)
    def _():
        greet({"tile": hi_t})
        greet({"tile": hi_t, "spec": other})

    def greet_across(u, carry):
        greet({"grp": 1 - grp, "tile": u})
        greet({"grp": 1 - grp, "tile": u, "spec": other})
        return carry

    lax.fori_loop(0, TILES, greet_across, 0)
    beside = jnp.where(has_lo, 2, 0) + jnp.where(has_hi, 2, 0)

    def everyone_in():
        pl.semaphore_wait(barrier, 2 * TILES + 1 + beside)

    @pl.when(grp == 0)
    def wave():
        def load(c):
            rows = pl.ds(pl.multiple_of(c * RCH * 8, 8), RCH * 8)
            return [
                pltpu.make_async_copy(spec_h.at[rows, hs], B.at[h, rows, :], load_sem.at[c, h])
                for h, hs in enumerate(halves)
            ]

        smalls = [
            pltpu.make_async_copy(wind_h, wind, small_sem.at[0]),
            pltpu.make_async_copy(land_h, land, small_sem.at[1]),
            pltpu.make_async_copy(inter_h, inter, small_sem.at[2]),
        ]
        for copy in smalls:
            copy.start()
        for q in range(TABLE.shape[0]):
            for f in range(FREQS):
                tab[q, f] = float(TABLE[q, f])

        def begin(c, carry):
            for copy in load(c):
                copy.start()
            return carry

        lax.fori_loop(0, CHUNKS, begin, 0)

        def halo(n, side, c):
            rows = pl.ds(pl.multiple_of(c * RCH, 8), RCH)
            return mesh_copy(
                S.at[n, side, :, rows, :], H.at[n, side, :, rows, :], h_send.at[n, side, c], h_recv.at[n, side, c],
                {"tile": hi_t if side == 0 else lo_t},
            )

        def edges_out(n, c):
            for k in range(RCH // 8):
                at = c * RCH + 8 * k
                rows = pl.ds(pl.multiple_of(at, 8), 8)
                for h in range(2):
                    S[n, 0, h, rows, :] = B[h, pl.ds(at * 8 + 7, 8, stride=8), :]
                    S[n, 1, h, rows, :] = B[h, pl.ds(at * 8, 8, stride=8), :]

            @pl.when(has_hi)
            def _():
                halo(n, 0, c).start()

            @pl.when(has_lo)
            def _():
                halo(n, 1, c).start()

        for copy in smalls:
            copy.wait()
        wet_i = pair(land)
        wet = tuple(x.astype(F32) for x in wet_i)
        shift = tuple((x - lane - 128 * h) & 255 for h, x in enumerate(pair(inter)))
        put(NBS, wet_i, slice(0, 8))
        put(NBS, shift, slice(8, 16))

        def neighbour(side):
            return mesh_copy(
                NBS, NBR.at[side], nb_send.at[side], nb_recv.at[side],
                {"tile": hi_t if side == 0 else lo_t},
            )

        everyone_in()

        @pl.when(has_hi)
        def _():
            neighbour(0).start()

        @pl.when(has_lo)
        def _():
            neighbour(1).start()

        wet_back = circular(barrel(wet, shift), 1)

        def windows(fields, u, pitch):
            acc = jnp.zeros((8, 128), F32)
            for f, field in enumerate(fields):
                start = (8 * u + pitch * f) % 128
                offset = (lane - start) & 127
                inside = offset < 10
                base = (8 * u) // 128
                p = 8 * u + offset
                value = field[base]
                if 8 * u % 128 + 10 > 128:
                    turned = (lane - pitch * f) & 127
                    value = jnp.where(turned < 16, field[1 - base], value)
                acc = jnp.where(inside, value, acc)
            return acc

        for u in range(TILES):
            MMSG[pl.ds(8 * u, 8), :] = windows([wet_back], u, 32)

        def to_ocean(src, dst, send, recv, u):
            return mesh_copy(
                src.at[pl.ds(pl.multiple_of(u * 8, 8), 8), :],
                dst.at[pl.ds(pl.multiple_of(tile * 8, 8), 8), :],
                send, recv, {"grp": 1, "tile": u},
            )

        def send_mask(u, carry):
            to_ocean(MMSG, MR, m_send, m_recv, u).start()
            return carry

        lax.fori_loop(0, TILES, send_mask, 0)

        @pl.when(jnp.logical_not(has_lo))
        def _():
            H[:, 0] = jnp.zeros((WSTEPS, 2, FD, 128), F32)
            NBR[0] = jnp.zeros((16, 256), jnp.int32)
            TR[:, 1:3] = jnp.zeros((WSTEPS, 2, 8, 256), F32)

        @pl.when(jnp.logical_not(has_hi))
        def _():
            H[:, 1] = jnp.zeros((WSTEPS, 2, FD, 128), F32)
            NBR[1] = jnp.zeros((16, 256), jnp.int32)
            TR[:, 3:5] = jnp.zeros((WSTEPS, 2, 8, 256), F32)

        def first_edges(c, carry):
            for copy in load(c):
                copy.wait()
            edges_out(0, c)
            return carry

        lax.fori_loop(0, CHUNKS, first_edges, 0)

        for d in range(DLOC):
            for h, hs in enumerate(halves):
                WD[d, :, hs] = wind[0, :, hs] * (sgn * COS[d]) + wind[1, :, hs] * (sgn * SIN[d])

        def growth(f, carry):
            slope = tab[1, f]
            sgs = tab[0, f] * sgn
            for d in range(DLOC):
                i = f * DLOC + d
                rows = pl.ds(pl.multiple_of(i * 8, 8), 8)
                for h, hs in enumerate(halves):
                    G[h, rows, :] = 1.0 + jnp.maximum(WD[d, :, hs] * slope - 0.05, 0.0)
                CNT[pl.ds(i, 1), :] = jnp.full((1, 128), sgs * SIN[d], F32)
            return carry

        lax.fori_loop(0, FREQS, growth, 0)

        @pl.when(has_lo)
        def _():
            neighbour(0).wait_recv()

        @pl.when(has_hi)
        def _():
            neighbour(1).wait_recv()

        edge_i = tuple(
            jnp.where(low_rows, NBR[1, 0:8, hs], NBR[0, 0:8, hs]) for hs in halves
        )
        edge_wet = tuple(x.astype(F32) for x in edge_i)
        edge_shift = tuple(
            jnp.where(low_rows, NBR[1, 8:16, hs], NBR[0, 8:16, hs]) for hs in halves
        )

        settle(QR, q_recv)
        group = lax.broadcasted_iota(jnp.int32, (4, 128), 1) >> 3
        parts = [[], [], [], [], []]
        for h in range(2):
            upper = [jnp.zeros((4, 128), F32)] * 5
            lower = [jnp.zeros((4, 128), F32)] * 5
            for k in range(16):
                m = QR[0, 16 * h + k] + QR[1, 16 * h + k]
                turned = pltpu.roll(m, 64, 1)
                for c in range(5):
                    at = (k + c) % 16
                    near, far = (m, turned) if at < 8 else (turned, m)
                    upper[c] = jnp.where(group == at, near, upper[c])
                    lower[c] = jnp.where(group == at, far, lower[c])
            for c in range(5):
                acc = jnp.concatenate([upper[c], lower[c]], axis=0)
                parts[c].append(pltpu.roll(acc, 128 - 8 * c, 1) if c else acc)
        fields = [tuple(x) for x in parts]
        left = tuple((256 - x) & 255 for x in shift)
        edge_left = tuple((256 - x) & 255 for x in edge_shift)
        u01 = tuple(0.1 * x for x in barrel(fields[0], left))
        v01 = tuple(0.1 * x for x in barrel(fields[1], left))

        def stiffness(level):
            depth = tuple(10.0 + 4.0 * x for x in level)
            return tuple(25.0 / (x * x) for x in depth)

        stiff = stiffness(barrel(fields[2], left))
        edge_v = tuple(0.1 * x for x in barrel(fields[3], edge_left))
        edge_stiff = stiffness(barrel(fields[4], edge_left))
        v_lo = tuple(jnp.broadcast_to(x[7:8], (8, 128)) for x in edge_v)
        v_hi = tuple(jnp.broadcast_to(x[0:1], (8, 128)) for x in edge_v)

        def halo_in(n, c, scale=None):
            @pl.when(has_lo)
            def _():
                halo(n, 0, c).wait_recv()

            @pl.when(has_hi)
            def _():
                halo(n, 1, c).wait_recv()

            for k in range(RCH // 8):
                rows = pl.ds(pl.multiple_of(c * RCH + 8 * k, 8), 8)
                cn = CNT[rows, :]
                for h in range(2):
                    lower, upper = H[n, 0, h, rows, :], H[n, 1, h, rows, :]
                    if scale is not None:
                        lower, upper = scale[0][h] * lower, scale[1][h] * upper
                    H[n, 0, h, rows, :] = jnp.maximum((cn + v_lo[h]) * lower, 0.0)
                    H[n, 1, h, rows, :] = jnp.minimum((cn + v_hi[h]) * upper, 0.0)

        def terms(n, i, rows, ce, cn, r=None):
            b = [B[h, rows, :] for h in range(2)]
            if r is not None:
                b = [r[h] * b[h] for h in range(2)]
            X = [(u01[h] + ce) * b[h] for h in range(2)]
            Y = [(v01[h] + cn) * b[h] for h in range(2)]
            own = [(b[h] - jnp.abs(X[h])) - jnp.abs(Y[h]) for h in range(2)]
            west, east = [jnp.maximum(x, 0.0) for x in X], [jnp.minimum(x, 0.0) for x in X]
            if r is not None:
                west, east = from_left(west), from_right(east)
            else:
                a = [pltpu.roll(x, 1, 1) for x in west]
                west = [a[0], jnp.where(first_lane, a[0], a[1])]
                a = [pltpu.roll(x, 127, 1) for x in east]
                east = [jnp.where(last_lane, a[1], a[0]), a[1]]
            south = [
                jnp.where(
                    first_row, H[n, 0, h, pl.ds(i, 8, stride=0), :], pltpu.roll(jnp.maximum(Y[h], 0.0), 1, 0)
                )
                for h in range(2)
            ]
            north = [
                jnp.where(
                    last_row, H[n, 1, h, pl.ds(i, 8, stride=0), :], pltpu.roll(jnp.minimum(Y[h], 0.0), 7, 0)
                )
                for h in range(2)
            ]
            return own, west, east, south, north

        def ahead(n):
            def chunk(c, carry):
                halo_in(n, c)

                def band(fc, carry):
                    f = c * FCH + fc
                    sgs = tab[0, f] * sgn
                    for d in range(DLOC):
                        i = f * DLOC + d
                        rows = pl.ds(pl.multiple_of(i * 8, 8), 8)
                        for q, term in enumerate(terms(n, i, rows, sgs * COS[d], sgs * SIN[d])):
                            for h in range(2):
                                PT[q, h, rows, :] = term[h]
                    return carry

                return lax.fori_loop(0, FCH, band, carry, unroll=2)

            lax.fori_loop(0, PCH, chunk, 0)

        def factors(r, edge_r):
            a, b = [pltpu.roll(x, 1, 1) for x in r], [pltpu.roll(x, 127, 1) for x in r]
            r_w = (jnp.where(first_lane, 0.0, a[0]), jnp.where(first_lane, a[0], a[1]))
            r_e = (jnp.where(last_lane, b[1], b[0]), jnp.where(last_lane, 0.0, b[1]))
            r_s = tuple(jnp.where(first_row, pltpu.roll(edge_r[h], 1, 0), pltpu.roll(r[h], 1, 0)) for h in range(2))
            r_n = tuple(jnp.where(last_row, pltpu.roll(edge_r[h], 7, 0), pltpu.roll(r[h], 7, 0)) for h in range(2))
            return tuple(r), r_w, r_e, r_s, r_n

        def sweep(n, r, edge_r, last):
            r_all = factors(r, edge_r)
            scale = (
                tuple(jnp.broadcast_to(x[7:8], (8, 128)) for x in edge_r),
                tuple(jnp.broadcast_to(x[0:1], (8, 128)) for x in edge_r),
            )

            def chunk(c, sums, prepared):
                if not prepared:
                    halo_in(n, c, scale)

                def band(fc, sums):
                    f = c * FCH + fc
                    sgs = tab[0, f] * sgn
                    zero = jnp.zeros((8, 128), F32)
                    acc = [[zero, zero] for _ in range(5 if last else 1)]
                    half_way = {}
                    for d in (DIR_ORDER if last else range(DLOC)):
                        i = f * DLOC + d
                        rows = pl.ds(pl.multiple_of(i * 8, 8), 8)
                        if prepared:
                            five = [[r_all[q][h] * PT[q, h, rows, :] for h in range(2)] for q in range(5)]
                        else:
                            five = terms(n, i, rows, sgs * COS[d], sgs * SIN[d], r)
                        for h in range(2):
                            own, west, east, south, north = (five[q][h] for q in range(5))
                            adv = own + ((west - east) + (south - north))
                            new = adv * G[h, rows, :]
                            B[h, rows, :] = new
                            acc[0][h] += adv
                            if last:
                                mine = (new - adv, new)
                                if h not in half_way:
                                    half_way[h] = mine
                                    continue
                                for q, (a, b) in enumerate(zip(half_way.pop(h), mine)):
                                    acc[1 + 2 * q][h] += (a - b) * COS[DLOC - 1 - d]
                                    acc[2 + 2 * q][h] += (a + b) * SIN[d]
                    weights = [tab[2, f], tab[3, f], tab[3, f], tab[4, f], tab[4, f]]
                    if last:
                        weights = weights[:1] + [w * sgn for w in weights[1:]]
                    return tuple(
                        tuple(total[h] + acc[q][h] * weights[q] for h in range(2)) for q, total in enumerate(sums)
                    )

                sums = lax.fori_loop(0, FCH, band, sums, unroll=2)
                if not last:

                    @pl.when(c < CHUNKS - HELD)
                    def _():
                        edges_out(n + 1, c)

                return sums

            zero = jnp.zeros((8, 128), F32)
            sums = tuple((zero, zero) for _ in range(5 if last else 1))
            begun = PCH if last else jnp.where(n > 0, PCH, 0)
            sums = lax.fori_loop(0, begun, lambda c, x: chunk(c, x, True), sums)
            return lax.fori_loop(begun, CHUNKS, lambda c, x: chunk(c, x, False), sums)

        def total_copies(n):
            return [
                (None, mesh_copy(TS.at[n], TR.at[n, 0], t_send.at[n, 0], t_recv.at[n, 0], {"spec": other})),
                (has_hi, mesh_copy(TS.at[n], TR.at[n, 1], t_send.at[n, 1], t_recv.at[n, 1], {"tile": hi_t})),
                (has_hi, mesh_copy(TS.at[n], TR.at[n, 2], t_send.at[n, 2], t_recv.at[n, 2], {"tile": hi_t, "spec": other})),
                (has_lo, mesh_copy(TS.at[n], TR.at[n, 3], t_send.at[n, 3], t_recv.at[n, 3], {"tile": lo_t})),
                (has_lo, mesh_copy(TS.at[n], TR.at[n, 4], t_send.at[n, 4], t_recv.at[n, 4], {"tile": lo_t, "spec": other})),
            ]

        def gated(condition, action):
            if condition is None:
                action()
            else:
                pl.when(condition)(action)

        def one_step(n, carry):
            r, edge_r = carry
            (total,) = sweep(n, r, edge_r, False)
            for h, hs in enumerate(halves):
                TS[n, :, hs] = total[h]
            copies = total_copies(n)
            for condition, copy in copies:
                gated(condition, copy.start)

            def late(c, carry):
                edges_out(n + 1, c)
                return carry

            lax.fori_loop(CHUNKS - HELD, CHUNKS, late, 0)
            ahead(n + 1)
            for (_, copy), condition in zip(copies, [None, has_lo, has_lo, has_hi, has_hi]):
                gated(condition, copy.wait_recv)
            new_r, new_edge = [], []
            for h, hs in enumerate(halves):
                full = total[h] + TR[n, 0, :, hs]
                new_r.append(wet[h] / (1.0 + stiff[h] * full))
                lower = TR[n, 1, :, hs] + TR[n, 2, :, hs]
                upper = TR[n, 3, :, hs] + TR[n, 4, :, hs]
                edge = jnp.where(low_rows, upper, lower)
                new_edge.append(edge_wet[h] / (1.0 + edge_stiff[h] * edge))
            return tuple(new_r), tuple(new_edge)

        r, edge_r = lax.fori_loop(0, WSTEPS - 1, one_step, (wet, edge_wet))
        n = WSTEPS - 1
        sums = sweep(n, r, edge_r, True)
        for h, hs in enumerate(halves):
            TS[n, :, hs] = sums[0][h]
        swap = mesh_copy(TS.at[n], TR.at[n, 0], t_send.at[n, 0], t_recv.at[n, 0], {"spec": other})
        swap.start()
        turned = [circular(barrel(sums[q], shift), 1) for q in (0, 3, 4, 1, 2)]
        slots = [tuple(pltpu.roll(x, 16 * f, 1) if f else x for x in field) for f, field in enumerate(turned[:4])]
        slot = lax.broadcasted_iota(jnp.int32, (4, 128), 1) < 64
        for fields, out in ((slots, MSG2), (turned[4:], MSG3)):
            for u in range(TILES):
                wide = windows(fields, u, 16)
                wide = wide + pltpu.roll(wide, 64, 1)
                out[u] = jnp.where(slot, wide[0:4], wide[4:8])

        def bands_to(src, dst, send, recv, u, half):
            return mesh_copy(src.at[u], dst.at[sp, tile], send, recv, {"grp": 1, "tile": u, "spec": half})

        def send_bands(u, carry):
            bands_to(MSG2, BR, f_send, f_recv, u, sp).start()
            bands_to(MSG2, BR, f_send, f_recv, u, other).start()
            bands_to(MSG3, BT, g_send, g_recv, u, 0).start()
            return carry

        lax.fori_loop(0, TILES, send_bands, 0)
        swap.wait_recv()
        final = tuple(
            wet[h] / (1.0 + stiff[h] * (sums[0][h] + TR[n, 0, :, halves[h]])) for h in range(2)
        )

        def store(c):
            rows = pl.ds(pl.multiple_of(c * RCH * 8, 8), RCH * 8)
            return [
                pltpu.make_async_copy(B.at[h, rows, :], out_w.at[rows, hs], load_sem.at[c, h])
                for h, hs in enumerate(halves)
            ]

        def finish(c, carry):
            def scale_f(i, carry):
                for d in range(DLOC):
                    rows = pl.ds(pl.multiple_of((c * RCH + i * DLOC + d) * 8, 8), 8)
                    for h in range(2):
                        B[h, rows, :] = B[h, rows, :] * final[h]
                return carry

            lax.fori_loop(0, FCH, scale_f, 0)
            for copy in store(c):
                copy.start()
            return carry

        lax.fori_loop(0, CHUNKS, finish, 0)
        def drain(c, carry):
            for copy in store(c):
                copy.wait()

            @pl.when(has_hi)
            def _():
                for n in range(WSTEPS):
                    halo(n, 0, c).wait_send()

            @pl.when(has_lo)
            def _():
                for n in range(WSTEPS):
                    halo(n, 1, c).wait_send()

            return carry

        lax.fori_loop(0, CHUNKS, drain, 0)
        for m in range(WSTEPS - 1):
            for condition, copy in total_copies(m):
                gated(condition, copy.wait_send)
        swap.wait_send()
        gated(has_hi, neighbour(0).wait_send)
        gated(has_lo, neighbour(1).wait_send)
        settle(MMSG, m_send)
        settle(BR, f_send)
        settle(MSG3, g_send)

    @pl.when(grp == 1)
    def circulation():
        top = (1 - sp).astype(F32)
        deep = sp.astype(F32)
        down = jnp.where(sp == 0, 1.0, math.exp(-1.0)).astype(F32)
        loads = [
            pltpu.make_async_copy(ocean_h.at[:, halves[0]], Q.at[0], small_sem.at[0]),
            pltpu.make_async_copy(ocean_h.at[:, halves[1]], Q.at[1], small_sem.at[1]),
            pltpu.make_async_copy(sea_h, sea, small_sem.at[2]),
        ]
        for copy in loads:
            copy.start()
        for copy in loads:
            copy.wait()
        for c in range(2):
            for h, hs in enumerate(halves):
                acc = jnp.zeros((8, 128), F32)
                for k in range(KLOC):
                    acc += Q[h, pl.ds((c * KLOC + k) * 8, 8), :] * float(_wgt[k])
                CS[pl.ds(8 * c, 8), hs] = acc * down

        def edge(n, side):
            return mesh_copy(
                ES.at[n, side], EH.at[n, side], e_send.at[n, side], e_recv.at[n, side],
                {"tile": hi_t if side == 0 else lo_t},
            )

        def level(n):
            return mesh_copy(LS.at[n], LH.at[n], l_send.at[n], l_recv.at[n], {"spec": other})

        def rims_out(n, src):
            for c in range(3):
                for h, hs in enumerate(halves):
                    ES[n, 0, pl.ds(8 * c, 8), hs] = src[h, pl.ds(c * 64 + 7, 8, stride=8), :]
                    ES[n, 1, pl.ds(8 * c, 8), hs] = src[h, pl.ds(c * 64, 8, stride=8), :]
                    LS[n, pl.ds(8 * c, 8), hs] = jnp.where(
                        sp == 0, src[h, pl.ds(c * 64 + 56, 8), :], src[h, pl.ds(c * 64, 8), :]
                    )
            for side in range(2):
                ES[n, side, 24:32, :] = sea[...]
            pl.when(has_hi)(edge(n, 0).start)
            pl.when(has_lo)(edge(n, 1).start)
            level(n).start()

        SX[...] = jnp.zeros((128, 256), F32)
        put(SX, tuple(0.5 * x for x in pair(sea)), slice(16, 24))
        SX[0:16, :] = CS[...]
        ahead_rows = (lane & 7) < 4
        for c in range(2):
            src = tuple(SX[pl.ds(8 + 8 * c, 8), hs] for hs in halves)
            ahead, behind = circular(src, 120), circular(src, 8)
            ahead = (ahead[1], ahead[0])
            put(SX, tuple(jnp.where(ahead_rows, ahead[h], behind[h]) for h in range(2)), slice(24 + 8 * c, 32 + 8 * c))
        slot = lax.broadcasted_iota(jnp.int32, (4, 128), 1) < 64
        for h, hs in enumerate(halves):
            turned = pltpu.roll(SX[:, hs].T, tile % 8 * 8, 1)
            turned = turned + pltpu.roll(turned, 64, 1)
            for k in range(16):
                MSG[16 * h + k] = jnp.where(slot, turned[8 * k : 8 * k + 4], turned[8 * k + 4 : 8 * k + 8])
        everyone_in()

        def to_wave(u, half):
            return mesh_copy(
                MSG.at[u], QR.at[sp, tile], q_send, q_recv, {"grp": 0, "tile": u, "spec": half},
            )

        def send_q(u, carry):
            to_wave(u, sp).start()
            to_wave(u, other).start()
            return carry

        lax.fori_loop(0, TILES, send_q, 0)
        rims_out(0, Q)

        @pl.when(jnp.logical_not(has_lo))
        def _():
            EH[:, 0] = jnp.zeros((2, 32, 256), F32)

        @pl.when(jnp.logical_not(has_hi))
        def _():
            EH[:, 1] = jnp.zeros((2, 32, 256), F32)

        settle(MR, m_recv)
        flags = pltpu.make_async_copy(MR, out_m, small_sem.at[0])
        flags.start()
        (mask3,) = arrived(MR, BTS, tile, 1)
        mask = tuple(x[1] for x in mask3)

        def substep(n, src, dst):
            for c in range(3):
                for k in range(KLOC):
                    at = (c * KLOC + k) * 8
                    x = tuple(src[h, pl.ds(at, 8), :] for h in range(2))
                    row_at = 8 * c + k
                    lower = tuple(
                        jnp.where(first_row, EH[n, 0, row_at : row_at + 1, hs], pltpu.roll(x[h], 1, 0))
                        for h, hs in enumerate(halves)
                    )
                    upper = tuple(
                        jnp.where(last_row, EH[n, 1, row_at : row_at + 1, hs], pltpu.roll(x[h], 7, 0))
                        for h, hs in enumerate(halves)
                    )
                    side = lateral(x, lower, upper)
                    for h, hs in enumerate(halves):
                        if k > 0:
                            above = src[h, pl.ds(at - 8, 8), :]
                        else:
                            above = LH[n, pl.ds(8 * c, 8), hs] * deep
                        if k < KLOC - 1:
                            below = src[h, pl.ds(at + 8, 8), :]
                        else:
                            below = LH[n, pl.ds(8 * c, 8), hs] * top
                        value = x[h] + 0.1 * side[h] + 0.2 * (above + below - 2.0 * x[h])
                        if c == 0:
                            value = value + 0.1 * src[h, pl.ds(at + 64, 8), :]
                        if c == 1:
                            value = value - 0.1 * src[h, pl.ds(at - 64, 8), :]
                        dst[h, pl.ds(at, 8), :] = value * mask[h]

        def rims_in(n):
            pl.when(has_lo)(edge(n, 0).wait_recv)
            pl.when(has_hi)(edge(n, 1).wait_recv)
            level(n).wait_recv()

        rims_in(0)
        for h, hs in enumerate(halves):
            level_here = sea[:, hs]
            SEA3[0:8, hs] = jnp.where(first_row, EH[0, 0, 31:32, hs], pltpu.roll(level_here, 1, 0))
            SEA3[8:16, hs] = level_here
            SEA3[16:24, hs] = jnp.where(last_row, EH[0, 1, 24:25, hs], pltpu.roll(level_here, 7, 0))
        seas = pltpu.make_async_copy(SEA3, out_s, small_sem.at[1])
        seas.start()
        substep(0, Q, A1)
        rims_out(1, A1)
        rims_in(1)
        substep(1, A1, A2)

        results = [pltpu.make_async_copy(A2.at[h], out_o.at[:, hs], out_sem.at[h]) for h, hs in enumerate(halves)]
        for copy in results:
            copy.start()
        for n in range(2):
            pl.when(has_hi)(edge(n, 0).wait_send)
            pl.when(has_lo)(edge(n, 1).wait_send)
            level(n).wait_send()
        settle(QR, q_send)
        flags.wait()
        seas.wait()
        for copy in results:
            copy.wait()
        settle(BR, f_recv)
        pl.when(sp == 0)(lambda: settle(BT, g_recv))


def tail(wave_h, unforced_h, bands_h, north_h, flags_h, sea_h, out_w, out_o, zeros, A2, BR, BT, MR, U, sea, BTS, in_sem, w_sem, o_sem):
    grp = lax.axis_index("grp")
    tile = lax.axis_index("tile")
    sp = lax.axis_index("spec")

    @pl.when(grp == 0)
    def wave():
        copies = []
        for c in range(CHUNKS):
            rows = pl.ds(c * RCH * 8, RCH * 8)
            copies.append(pltpu.make_async_copy(wave_h.at[rows, :], out_w.at[rows, :], w_sem.at[c]))
            copies[-1].start()
        zeros[0:192, :] = jnp.zeros((192, 256), F32)
        copies.append(pltpu.make_async_copy(zeros.at[0:192, :], out_o, o_sem.at[0]))
        copies[-1].start()
        for copy in copies:
            copy.wait()

    @pl.when(grp == 1)
    def circulation():
        loads = [
            pltpu.make_async_copy(flags_h, MR, in_sem.at[0]),
            pltpu.make_async_copy(bands_h, BR, in_sem.at[1]),
            pltpu.make_async_copy(sea_h, sea, in_sem.at[4]),
        ] + [pltpu.make_async_copy(unforced_h.at[:, hs], A2.at[h], in_sem.at[2 + h]) for h, hs in enumerate(HALVES)]
        for copy in loads:
            copy.start()
        norths = pltpu.make_async_copy(north_h, BT, in_sem.at[5])

        @pl.when(sp == 0)
        def _():
            norths.start()

        zeros[...] = jnp.zeros(zeros.shape, F32)
        blanks = []
        for c in range(CHUNKS):
            rows = pl.ds(c * RCH * 8, RCH * 8)
            blanks.append(pltpu.make_async_copy(zeros, out_w.at[rows, :], w_sem.at[c]))
            blanks[-1].start()
        row = lax.broadcasted_iota(jnp.int32, (8, 128), 0)
        top = (1 - sp).astype(F32)
        deep = sp.astype(F32)
        down = jnp.where(sp == 0, 1.0, math.exp(-1.0)).astype(F32)
        at_lo = jnp.where(tile > 0, 1.0, 0.0).astype(F32)
        at_hi = jnp.where(tile < TILES - 1, 1.0, 0.0).astype(F32)
        loads[0].wait()
        (mask3,) = arrived(MR, BTS, tile, 1)
        mask = tuple(x[1] for x in mask3)
        mask_lo = tuple(jnp.where(row == 0, x[0] * at_lo, x[0]) for x in mask3)
        mask_hi = tuple(jnp.where(row == 7, x[2] * at_hi, x[2]) for x in mask3)
        for copy in loads[1:]:
            copy.wait()

        @pl.when(sp == 0)
        def _():
            norths.wait()

        @pl.when(sp == 1)
        def _():
            BT[...] = jnp.zeros(BT.shape, F32)

        def unpacked(buf, slots):
            for t in range(TILES):
                both = buf[0, t] + buf[1, t]
                U[8 * t : 8 * t + 8, :] = jnp.concatenate([both, pltpu.roll(both, 64, 1)], axis=0)
            for h in range(2):
                turned = U[pl.ds(128 * h, 128), :].T
                BTS[pl.ds(0, 64), HALVES[h]] = turned[0:64]
                BTS[pl.ds(64, 64), HALVES[h]] = turned[0:64]
            out = []
            for f in range(slots):
                start = pl.multiple_of((8 * tile + 16 * f) % 64, 8)
                wide = BTS[pl.ds(start, 16), :]
                out.append(tuple((wide[0:8, hs], wide[1:9, hs], wide[2:10, hs]) for hs in HALVES))
            return out

        total, drift_e, drift_n, stress_e = unpacked(BR, 4)
        (stress_n,) = unpacked(BT, 1)
        factor = []
        for h, hs in enumerate(HALVES):
            row_of = []
            for q, masked in enumerate((mask_lo, mask, mask_hi)):
                depth = 10.0 + 4.0 * sea[8 * q : 8 * q + 8, hs]
                row_of.append(masked[h] / (1.0 + 25.0 * total[h][q] / (depth * depth)))
            factor.append(row_of)
        forced, spread = [], []
        for three in (stress_e, stress_n, drift_e, drift_n):
            lower, own, upper = (tuple(three[h][q] * factor[h][q] for h in range(2)) for q in range(3))
            forced.append(own)
            spread.append(lateral(own, lower, upper))
        for k in range(KLOC):
            near, far = math.exp(0.125), math.exp(-0.125)
            prof = float(_prof[k]) * down
            above = near if k > 0 else near * deep
            below = far if k < KLOC - 1 else far * top
            stay = prof * (1.0 + 0.2 * (above + below - 2.0))
            for h, hs in enumerate(HALVES):
                east = (0.1 * prof) * forced[3][h]
                north = (-0.1 * prof) * forced[2][h]
                d_east = (0.1 * stay) * forced[3][h] + (0.01 * prof) * spread[3][h]
                d_north = (-0.1 * stay) * forced[2][h] - (0.01 * prof) * spread[2][h]
                if k == 0:
                    east = east + top * forced[0][h]
                    north = north + top * forced[1][h]
                    d_east = d_east + top * (0.6 * forced[0][h] + 0.1 * spread[0][h])
                    d_north = d_north + top * (0.6 * forced[1][h] + 0.1 * spread[1][h])
                if k == 1:
                    d_east = d_east + (0.2 * top) * forced[0][h]
                    d_north = d_north + (0.2 * top) * forced[1][h]
                A2[h, pl.ds(8 * k, 8), :] += mask[h] * (d_east + 0.1 * north) + east
                A2[h, pl.ds(64 + 8 * k, 8), :] += mask[h] * (d_north - 0.1 * east) + north
        results = [pltpu.make_async_copy(A2.at[h], out_o.at[:, hs], o_sem.at[h]) for h, hs in enumerate(HALVES)]
        for copy in results:
            copy.start()

        for copy in results + blanks:
            copy.wait()


def body(spectrum, wind, land_mask, intersection, ocean_state, sea_level):
    v = lambda *shape, dtype=F32: pltpu.VMEM(shape, dtype)
    dma = lambda *shape: pltpu.SemaphoreType.DMA(shape) if shape else pltpu.SemaphoreType.DMA
    anywhere = pl.BlockSpec(memory_space=pltpu.HBM)
    scratch = [
        pltpu.SMEM(TABLE.shape, F32),
        v(2, FD * 8, 128), v(2, FD * 8, 128), v(5, 2, PCH * RCH * 8, 128), v(DLOC, 8, 256), v(FD, 128),
        v(WSTEPS, 2, 2, FD, 128), v(WSTEPS, 2, 2, FD, 128),
        v(2, 8, 256), v(8, 256, dtype=jnp.int32), v(8, 256, dtype=jnp.int32),
        v(16, 256, dtype=jnp.int32), v(2, 16, 256, dtype=jnp.int32),
        v(2, TILES, 4, 128), v(WSTEPS, 8, 256), v(WSTEPS, 5, 8, 256), v(TILES, 4, 128), v(TILES, 4, 128), v(256, 128),
        v(2, 192, 128), v(2, 192, 128), v(2, 192, 128), v(8, 256), v(16, 256), v(128, 256),
        v(TILES, 4, 128), v(256, 128), v(256, 256),
        v(2, 2, 32, 256), v(2, 2, 32, 256), v(24, 256), v(2, 24, 256), v(2, 24, 256),
        dma(CHUNKS, 2), dma(3), dma(WSTEPS, 2, CHUNKS), dma(WSTEPS, 2, CHUNKS), dma(WSTEPS, 5), dma(WSTEPS, 5),
        dma(2), dma(2), dma(), dma(), dma(), dma(), dma(), dma(), dma(), dma(),
        dma(2, 2), dma(2, 2), dma(2), dma(2), dma(2),
    ]
    landed = pl.pallas_call(
        kernel,
        out_shape=(
            jax.ShapeDtypeStruct((FD * 8, 256), F32),
            jax.ShapeDtypeStruct((192, 256), F32),
            jax.ShapeDtypeStruct((2, TILES, 4, 128), F32),
            jax.ShapeDtypeStruct((2, TILES, 4, 128), F32),
            jax.ShapeDtypeStruct((256, 128), F32),
            jax.ShapeDtypeStruct((24, 256), F32),
        ),
        in_specs=[anywhere] * 6,
        out_specs=(pl.BlockSpec(memory_space=pl.ANY),) * 6,
        scratch_shapes=scratch,
        compiler_params=pltpu.CompilerParams(collective_id=0, has_side_effects=True, vmem_limit_bytes=48 << 20),
    )(
        *(
            pltpu.with_memory_space_constraint(x, pltpu.HBM)
            for x in (
                spectrum.reshape(FD * 8, 256),
                wind,
                land_mask,
                intersection,
                ocean_state.reshape(192, 256),
                sea_level.reshape(8, 256),
            )
        )
    )
    waves, ocean = pl.pallas_call(
        tail,
        out_shape=(jax.ShapeDtypeStruct((FD * 8, 256), F32), jax.ShapeDtypeStruct((192, 256), F32)),
        in_specs=[pl.BlockSpec(memory_space=pl.ANY)] * 6,
        out_specs=(pl.BlockSpec(memory_space=pl.ANY),) * 2,
        scratch_shapes=[
            v(RCH * 8, 256), v(2, 192, 128), v(2, TILES, 4, 128), v(2, TILES, 4, 128), v(256, 128), v(256, 128),
            v(24, 256), v(256, 256), dma(6), dma(CHUNKS), dma(2),
        ],
        compiler_params=pltpu.CompilerParams(vmem_limit_bytes=6 << 20),
    )(*landed)
    return waves.reshape(spectrum.shape), ocean.reshape(ocean_state.shape)


def solution(mesh):
    return jax.shard_map(
        body,
        mesh=mesh,
        in_specs=(
            P("grp", None, "spec", "tile", None),
            P(None, "tile", None),
            P("tile", None),
            P("tile", None),
            P("grp", None, "spec", "tile", None),
            P("grp", "tile", None),
        ),
        out_specs=(P("grp", None, "spec", "tile", None), P("grp", None, "spec", "tile", None)),
        check_vma=False,
    )
```

```python
import math

import jax
import jax.numpy as jnp
import numpy as np
from jax import lax
from jax.experimental import pallas as pl
from jax.experimental.pallas import tpu as pltpu
from jax.sharding import PartitionSpec as P

FREQS = 32
DIRS = 36
LEVELS = 16
WSTEPS = 4
TILES = 32
DLOC = 18
KLOC = 8
FD = FREQS * DLOC
CHUNKS = 8
FCH = FREQS // CHUNKS
RCH = FCH * DLOC
PCH = 4
HELD = 4
F32 = jnp.float32

_freq = 0.04 * 1.1 ** np.arange(FREQS)
_cel = 1.56 / _freq
_gs = 0.4 * 1.1 ** (-np.arange(FREQS, dtype=np.float64))
_bw = 0.1 * _freq * (2.0 * math.pi / DIRS)
TABLE = np.stack([_gs, 0.05 / _cel, _bw, 5.0 * _bw / _cel, 20.0 * _bw * _freq**3]).astype(np.float32)
_ang = 2.0 * math.pi * (np.arange(DIRS) + 0.5) / DIRS
COS = [float(np.float32(x)) for x in np.cos(_ang)[:DLOC]]
SIN = [float(np.float32(x)) for x in np.sin(_ang)[:DLOC]]
DIR_ORDER = [d for k in range(DLOC // 2) for d in (k, DLOC - 1 - k)]
_prof = np.exp(-2.0 * (np.arange(LEVELS) + 0.5) / LEVELS)
_wgt = _prof / _prof.sum()


def mesh_copy(src, dst, send, recv, where):
    return pltpu.make_async_remote_copy(
        src_ref=src,
        dst_ref=dst,
        send_sem=send,
        recv_sem=recv,
        device_id=where,
        device_id_type=pl.DeviceIdType.MESH,
    )


def settle(buf, sem):
    pltpu.make_async_copy(buf, buf, sem).wait()


HALVES = (slice(0, 128), slice(128, 256))


def at_lane(k):
    return lax.broadcasted_iota(jnp.int32, (8, 128), 1) == k


def from_left(x):
    a, b = pltpu.roll(x[0], 1, 1), pltpu.roll(x[1], 1, 1)
    return jnp.where(at_lane(0), 0.0, a), jnp.where(at_lane(0), a, b)


def from_right(x):
    a, b = pltpu.roll(x[0], 127, 1), pltpu.roll(x[1], 127, 1)
    return jnp.where(at_lane(127), b, a), jnp.where(at_lane(127), 0.0, b)


def lateral(x, lower, upper):
    left, right = from_left(x), from_right(x)
    return tuple(lower[h] + upper[h] + left[h] + right[h] - 4.0 * x[h] for h in range(2))


def arrived(buf, BTS, tile, slots):
    for h in range(2):
        turned = buf[pl.ds(128 * h, 128), :].T
        BTS[pl.ds(0, 128), HALVES[h]] = turned
        BTS[pl.ds(128, 128), HALVES[h]] = turned
    out = []
    for f in range(slots):
        start = pl.multiple_of((8 * tile + 32 * f) % 128, 8)
        wide = BTS[pl.ds(start, 16), :]
        out.append(tuple((wide[0:8, hs], wide[1:9, hs], wide[2:10, hs]) for hs in HALVES))
    return out


def kernel(
    spec_h, wind_h, land_h, inter_h, ocean_h, sea_h, out_w, out_o, BR, BT, out_m, out_s,
    tab, B, G, PT, WD, CNT, H, S, wind, land, inter, NBS, NBR, QR, TS, TR, MSG2, MSG3, MMSG,
    Q, A1, A2, sea, CS, SX, MSG, MR, BTS, ES, EH, SEA3, LS, LH,
    load_sem, small_sem, h_send, h_recv, t_send, t_recv, nb_send, nb_recv,
    q_send, q_recv, m_send, m_recv, f_send, f_recv, g_send, g_recv, e_send, e_recv, l_send, l_recv, out_sem,
):
    grp = lax.axis_index("grp")
    tile = lax.axis_index("tile")
    sp = lax.axis_index("spec")
    other = 1 - sp
    sgn = (1 - 2 * sp).astype(F32)
    has_lo = tile > 0
    has_hi = tile < TILES - 1
    lo_t = jnp.maximum(tile - 1, 0)
    hi_t = jnp.minimum(tile + 1, TILES - 1)
    lane = lax.broadcasted_iota(jnp.int32, (8, 128), 1)
    row = lax.broadcasted_iota(jnp.int32, (8, 128), 0)
    first_lane, last_lane = lane == 0, lane == 127
    first_row, last_row = row == 0, row == 7
    low_rows = row < 4
    halves = HALVES

    def circular(x, shift):
        a, b = pltpu.roll(x[0], shift, 1), pltpu.roll(x[1], shift, 1)
        m = lane < shift
        return jnp.where(m, b, a), jnp.where(m, a, b)

    def barrel(x, amount):
        for bit in range(0, 8, 2):
            options = [x]
            for digit in range(1, 4):
                by = digit << bit
                y = circular(x, by % 128) if by % 128 else x
                options.append((y[1], y[0]) if by >= 128 else y)
            low = [(amount[h] & (1 << bit)) != 0 for h in range(2)]
            high = [(amount[h] & (2 << bit)) != 0 for h in range(2)]
            x = tuple(
                jnp.where(
                    high[h],
                    jnp.where(low[h], options[3][h], options[2][h]),
                    jnp.where(low[h], options[1][h], options[0][h]),
                )
                for h in range(2)
            )
        return x

    def pair(ref, *lead):
        return tuple(ref[(*lead, slice(None), hs)] for hs in halves)

    def put(ref, value, rows):
        for h in range(2):
            ref[rows, halves[h]] = value[h]

    barrier = pltpu.get_barrier_semaphore()

    def greet(where):
        pl.semaphore_signal(barrier, 1, device_id=where, device_id_type=pl.DeviceIdType.MESH)

    greet({"spec": other})

    @pl.when(has_lo)
    def _():
        greet({"tile": lo_t})
        greet({"tile": lo_t, "spec": other})

    @pl.when(has_hi)
    def _():
        greet({"tile": hi_t})
        greet({"tile": hi_t, "spec": other})

    def greet_across(u, carry):
        greet({"grp": 1 - grp, "tile": u})
        greet({"grp": 1 - grp, "tile": u, "spec": other})
        return carry

    lax.fori_loop(0, TILES, greet_across, 0)
    beside = jnp.where(has_lo, 2, 0) + jnp.where(has_hi, 2, 0)

    def everyone_in():
        pl.semaphore_wait(barrier, 2 * TILES + 1 + beside)

    @pl.when(grp == 0)
    def wave():
        def load(c):
            rows = pl.ds(pl.multiple_of(c * RCH * 8, 8), RCH * 8)
            return [
                pltpu.make_async_copy(spec_h.at[rows, hs], B.at[h, rows, :], load_sem.at[c, h])
                for h, hs in enumerate(halves)
            ]

        smalls = [
            pltpu.make_async_copy(wind_h, wind, small_sem.at[0]),
            pltpu.make_async_copy(land_h, land, small_sem.at[1]),
            pltpu.make_async_copy(inter_h, inter, small_sem.at[2]),
        ]
        for copy in smalls:
            copy.start()
        for q in range(TABLE.shape[0]):
            for f in range(FREQS):
                tab[q, f] = float(TABLE[q, f])

        def begin(c, carry):
            for copy in load(c):
                copy.start()
            return carry

        lax.fori_loop(0, CHUNKS, begin, 0)

        def halo(n, side, c):
            rows = pl.ds(pl.multiple_of(c * RCH, 8), RCH)
            return mesh_copy(
                S.at[n, side, :, rows, :], H.at[n, side, :, rows, :], h_send.at[n, side, c], h_recv.at[n, side, c],
                {"tile": hi_t if side == 0 else lo_t},
            )

        def edges_out(n, c):
            for k in range(RCH // 8):
                at = c * RCH + 8 * k
                rows = pl.ds(pl.multiple_of(at, 8), 8)
                for h in range(2):
                    S[n, 0, h, rows, :] = B[h, pl.ds(at * 8 + 7, 8, stride=8), :]
                    S[n, 1, h, rows, :] = B[h, pl.ds(at * 8, 8, stride=8), :]

            @pl.when(has_hi)
            def _():
                halo(n, 0, c).start()

            @pl.when(has_lo)
            def _():
                halo(n, 1, c).start()

        for copy in smalls:
            copy.wait()
        wet_i = pair(land)
        wet = tuple(x.astype(F32) for x in wet_i)
        shift = tuple((x - lane - 128 * h) & 255 for h, x in enumerate(pair(inter)))
        put(NBS, wet_i, slice(0, 8))
        put(NBS, shift, slice(8, 16))

        def neighbour(side):
            return mesh_copy(
                NBS, NBR.at[side], nb_send.at[side], nb_recv.at[side],
                {"tile": hi_t if side == 0 else lo_t},
            )

        everyone_in()

        @pl.when(has_hi)
        def _():
            neighbour(0).start()

        @pl.when(has_lo)
        def _():
            neighbour(1).start()

        wet_back = circular(barrel(wet, shift), 1)

        def windows(fields, u, pitch):
            acc = jnp.zeros((8, 128), F32)
            for f, field in enumerate(fields):
                start = (8 * u + pitch * f) % 128
                offset = (lane - start) & 127
                inside = offset < 10
                base = (8 * u) // 128
                p = 8 * u + offset
                value = field[base]
                if 8 * u % 128 + 10 > 128:
                    turned = (lane - pitch * f) & 127
                    value = jnp.where(turned < 16, field[1 - base], value)
                acc = jnp.where(inside, value, acc)
            return acc

        for u in range(TILES):
            MMSG[pl.ds(8 * u, 8), :] = windows([wet_back], u, 32)

        def to_ocean(src, dst, send, recv, u):
            return mesh_copy(
                src.at[pl.ds(pl.multiple_of(u * 8, 8), 8), :],
                dst.at[pl.ds(pl.multiple_of(tile * 8, 8), 8), :],
                send, recv, {"grp": 1, "tile": u},
            )

        def send_mask(u, carry):
            to_ocean(MMSG, MR, m_send, m_recv, u).start()
            return carry

        lax.fori_loop(0, TILES, send_mask, 0)

        @pl.when(jnp.logical_not(has_lo))
        def _():
            H[:, 0] = jnp.zeros((WSTEPS, 2, FD, 128), F32)
            NBR[0] = jnp.zeros((16, 256), jnp.int32)
            TR[:, 1:3] = jnp.zeros((WSTEPS, 2, 8, 256), F32)

        @pl.when(jnp.logical_not(has_hi))
        def _():
            H[:, 1] = jnp.zeros((WSTEPS, 2, FD, 128), F32)
            NBR[1] = jnp.zeros((16, 256), jnp.int32)
            TR[:, 3:5] = jnp.zeros((WSTEPS, 2, 8, 256), F32)

        def first_edges(c, carry):
            for copy in load(c):
                copy.wait()
            edges_out(0, c)
            return carry

        lax.fori_loop(0, CHUNKS, first_edges, 0)

        for d in range(DLOC):
            for h, hs in enumerate(halves):
                WD[d, :, hs] = wind[0, :, hs] * (sgn * COS[d]) + wind[1, :, hs] * (sgn * SIN[d])

        def growth(f, carry):
            slope = tab[1, f]
            sgs = tab[0, f] * sgn
            for d in range(DLOC):
                i = f * DLOC + d
                rows = pl.ds(pl.multiple_of(i * 8, 8), 8)
                for h, hs in enumerate(halves):
                    G[h, rows, :] = 1.0 + jnp.maximum(WD[d, :, hs] * slope - 0.05, 0.0)
                CNT[pl.ds(i, 1), :] = jnp.full((1, 128), sgs * SIN[d], F32)
            return carry

        lax.fori_loop(0, FREQS, growth, 0)

        @pl.when(has_lo)
        def _():
            neighbour(0).wait_recv()

        @pl.when(has_hi)
        def _():
            neighbour(1).wait_recv()

        edge_i = tuple(
            jnp.where(low_rows, NBR[1, 0:8, hs], NBR[0, 0:8, hs]) for hs in halves
        )
        edge_wet = tuple(x.astype(F32) for x in edge_i)
        edge_shift = tuple(
            jnp.where(low_rows, NBR[1, 8:16, hs], NBR[0, 8:16, hs]) for hs in halves
        )

        settle(QR, q_recv)
        group = lax.broadcasted_iota(jnp.int32, (4, 128), 1) >> 3
        parts = [[], [], [], [], []]
        for h in range(2):
            upper = [jnp.zeros((4, 128), F32)] * 5
            lower = [jnp.zeros((4, 128), F32)] * 5
            for k in range(16):
                m = QR[0, 16 * h + k] + QR[1, 16 * h + k]
                turned = pltpu.roll(m, 64, 1)
                for c in range(5):
                    at = (k + c) % 16
                    near, far = (m, turned) if at < 8 else (turned, m)
                    upper[c] = jnp.where(group == at, near, upper[c])
                    lower[c] = jnp.where(group == at, far, lower[c])
            for c in range(5):
                acc = jnp.concatenate([upper[c], lower[c]], axis=0)
                parts[c].append(pltpu.roll(acc, 128 - 8 * c, 1) if c else acc)
        fields = [tuple(x) for x in parts]
        left = tuple((256 - x) & 255 for x in shift)
        edge_left = tuple((256 - x) & 255 for x in edge_shift)
        u01 = tuple(0.1 * x for x in barrel(fields[0], left))
        v01 = tuple(0.1 * x for x in barrel(fields[1], left))

        def stiffness(level):
            depth = tuple(10.0 + 4.0 * x for x in level)
            return tuple(25.0 / (x * x) for x in depth)

        stiff = stiffness(barrel(fields[2], left))
        edge_v = tuple(0.1 * x for x in barrel(fields[3], edge_left))
        edge_stiff = stiffness(barrel(fields[4], edge_left))
        v_lo = tuple(jnp.broadcast_to(x[7:8], (8, 128)) for x in edge_v)
        v_hi = tuple(jnp.broadcast_to(x[0:1], (8, 128)) for x in edge_v)

        def halo_in(n, c, scale=None):
            @pl.when(has_lo)
            def _():
                halo(n, 0, c).wait_recv()

            @pl.when(has_hi)
            def _():
                halo(n, 1, c).wait_recv()

            for k in range(RCH // 8):
                rows = pl.ds(pl.multiple_of(c * RCH + 8 * k, 8), 8)
                cn = CNT[rows, :]
                for h in range(2):
                    lower, upper = H[n, 0, h, rows, :], H[n, 1, h, rows, :]
                    if scale is not None:
                        lower, upper = scale[0][h] * lower, scale[1][h] * upper
                    H[n, 0, h, rows, :] = jnp.maximum((cn + v_lo[h]) * lower, 0.0)
                    H[n, 1, h, rows, :] = jnp.minimum((cn + v_hi[h]) * upper, 0.0)

        def terms(n, i, rows, ce, cn, r=None):
            b = [B[h, rows, :] for h in range(2)]
            if r is not None:
                b = [r[h] * b[h] for h in range(2)]
            X = [(u01[h] + ce) * b[h] for h in range(2)]
            Y = [(v01[h] + cn) * b[h] for h in range(2)]
            own = [(b[h] - jnp.abs(X[h])) - jnp.abs(Y[h]) for h in range(2)]
            west, east = [jnp.maximum(x, 0.0) for x in X], [jnp.minimum(x, 0.0) for x in X]
            if r is not None:
                west, east = from_left(west), from_right(east)
            else:
                a = [pltpu.roll(x, 1, 1) for x in west]
                west = [a[0], jnp.where(first_lane, a[0], a[1])]
                a = [pltpu.roll(x, 127, 1) for x in east]
                east = [jnp.where(last_lane, a[1], a[0]), a[1]]
            south = [
                jnp.where(
                    first_row, H[n, 0, h, pl.ds(i, 8, stride=0), :], pltpu.roll(jnp.maximum(Y[h], 0.0), 1, 0)
                )
                for h in range(2)
            ]
            north = [
                jnp.where(
                    last_row, H[n, 1, h, pl.ds(i, 8, stride=0), :], pltpu.roll(jnp.minimum(Y[h], 0.0), 7, 0)
                )
                for h in range(2)
            ]
            return own, west, east, south, north

        def ahead(n):
            def chunk(c, carry):
                halo_in(n, c)

                def band(fc, carry):
                    f = c * FCH + fc
                    sgs = tab[0, f] * sgn
                    for d in range(DLOC):
                        i = f * DLOC + d
                        rows = pl.ds(pl.multiple_of(i * 8, 8), 8)
                        for q, term in enumerate(terms(n, i, rows, sgs * COS[d], sgs * SIN[d])):
                            for h in range(2):
                                PT[q, h, rows, :] = term[h]
                    return carry

                return lax.fori_loop(0, FCH, band, carry, unroll=2)

            lax.fori_loop(0, PCH, chunk, 0)

        def factors(r, edge_r):
            a, b = [pltpu.roll(x, 1, 1) for x in r], [pltpu.roll(x, 127, 1) for x in r]
            r_w = (jnp.where(first_lane, 0.0, a[0]), jnp.where(first_lane, a[0], a[1]))
            r_e = (jnp.where(last_lane, b[1], b[0]), jnp.where(last_lane, 0.0, b[1]))
            r_s = tuple(jnp.where(first_row, pltpu.roll(edge_r[h], 1, 0), pltpu.roll(r[h], 1, 0)) for h in range(2))
            r_n = tuple(jnp.where(last_row, pltpu.roll(edge_r[h], 7, 0), pltpu.roll(r[h], 7, 0)) for h in range(2))
            return tuple(r), r_w, r_e, r_s, r_n

        def sweep(n, r, edge_r, last):
            r_all = factors(r, edge_r)
            scale = (
                tuple(jnp.broadcast_to(x[7:8], (8, 128)) for x in edge_r),
                tuple(jnp.broadcast_to(x[0:1], (8, 128)) for x in edge_r),
            )

            def chunk(c, sums, prepared):
                if not prepared:
                    halo_in(n, c, scale)

                def band(fc, sums):
                    f = c * FCH + fc
                    sgs = tab[0, f] * sgn
                    zero = jnp.zeros((8, 128), F32)
                    acc = [[zero, zero] for _ in range(5 if last else 1)]
                    half_way = {}
                    for d in (DIR_ORDER if last else range(DLOC)):
                        i = f * DLOC + d
                        rows = pl.ds(pl.multiple_of(i * 8, 8), 8)
                        if prepared:
                            five = [[r_all[q][h] * PT[q, h, rows, :] for h in range(2)] for q in range(5)]
                        else:
                            five = terms(n, i, rows, sgs * COS[d], sgs * SIN[d], r)
                        for h in range(2):
                            own, west, east, south, north = (five[q][h] for q in range(5))
                            adv = own + ((west - east) + (south - north))
                            new = adv * G[h, rows, :]
                            B[h, rows, :] = new
                            acc[0][h] += adv
                            if last:
                                mine = (new - adv, new)
                                if h not in half_way:
                                    half_way[h] = mine
                                    continue
                                for q, (a, b) in enumerate(zip(half_way.pop(h), mine)):
                                    acc[1 + 2 * q][h] += (a - b) * COS[DLOC - 1 - d]
                                    acc[2 + 2 * q][h] += (a + b) * SIN[d]
                    weights = [tab[2, f], tab[3, f], tab[3, f], tab[4, f], tab[4, f]]
                    if last:
                        weights = weights[:1] + [w * sgn for w in weights[1:]]
                    return tuple(
                        tuple(total[h] + acc[q][h] * weights[q] for h in range(2)) for q, total in enumerate(sums)
                    )

                sums = lax.fori_loop(0, FCH, band, sums, unroll=2)
                if not last:

                    @pl.when(c < CHUNKS - jnp.where(n > 0, HELD, HELD - 1))
                    def _():
                        edges_out(n + 1, c)

                return sums

            zero = jnp.zeros((8, 128), F32)
            sums = tuple((zero, zero) for _ in range(5 if last else 1))
            begun = PCH if last else jnp.where(n > 0, PCH, 0)
            sums = lax.fori_loop(0, begun, lambda c, x: chunk(c, x, True), sums)
            return lax.fori_loop(begun, CHUNKS, lambda c, x: chunk(c, x, False), sums)

        def total_copies(n):
            return [
                (None, mesh_copy(TS.at[n], TR.at[n, 0], t_send.at[n, 0], t_recv.at[n, 0], {"spec": other})),
                (has_hi, mesh_copy(TS.at[n], TR.at[n, 1], t_send.at[n, 1], t_recv.at[n, 1], {"tile": hi_t})),
                (has_hi, mesh_copy(TS.at[n], TR.at[n, 2], t_send.at[n, 2], t_recv.at[n, 2], {"tile": hi_t, "spec": other})),
                (has_lo, mesh_copy(TS.at[n], TR.at[n, 3], t_send.at[n, 3], t_recv.at[n, 3], {"tile": lo_t})),
                (has_lo, mesh_copy(TS.at[n], TR.at[n, 4], t_send.at[n, 4], t_recv.at[n, 4], {"tile": lo_t, "spec": other})),
            ]

        def gated(condition, action):
            if condition is None:
                action()
            else:
                pl.when(condition)(action)

        def one_step(n, carry):
            r, edge_r = carry
            (total,) = sweep(n, r, edge_r, False)
            for h, hs in enumerate(halves):
                TS[n, :, hs] = total[h]
            copies = total_copies(n)
            for condition, copy in copies:
                gated(condition, copy.start)

            def late(c, carry):
                edges_out(n + 1, c)
                return carry

            lax.fori_loop(CHUNKS - jnp.where(n > 0, HELD, HELD - 1), CHUNKS, late, 0)
            ahead(n + 1)
            for (_, copy), condition in zip(copies, [None, has_lo, has_lo, has_hi, has_hi]):
                gated(condition, copy.wait_recv)
            new_r, new_edge = [], []
            for h, hs in enumerate(halves):
                full = total[h] + TR[n, 0, :, hs]
                new_r.append(wet[h] / (1.0 + stiff[h] * full))
                lower = TR[n, 1, :, hs] + TR[n, 2, :, hs]
                upper = TR[n, 3, :, hs] + TR[n, 4, :, hs]
                edge = jnp.where(low_rows, upper, lower)
                new_edge.append(edge_wet[h] / (1.0 + edge_stiff[h] * edge))
            return tuple(new_r), tuple(new_edge)

        r, edge_r = lax.fori_loop(0, WSTEPS - 1, one_step, (wet, edge_wet))
        n = WSTEPS - 1
        sums = sweep(n, r, edge_r, True)
        for h, hs in enumerate(halves):
            TS[n, :, hs] = sums[0][h]
        swap = mesh_copy(TS.at[n], TR.at[n, 0], t_send.at[n, 0], t_recv.at[n, 0], {"spec": other})
        swap.start()
        turned = [circular(barrel(sums[q], shift), 1) for q in (0, 3, 4, 1, 2)]
        slots = [tuple(pltpu.roll(x, 16 * f, 1) if f else x for x in field) for f, field in enumerate(turned[:4])]
        slot = lax.broadcasted_iota(jnp.int32, (4, 128), 1) < 64
        for fields, out in ((slots, MSG2), (turned[4:], MSG3)):
            for u in range(TILES):
                wide = windows(fields, u, 16)
                wide = wide + pltpu.roll(wide, 64, 1)
                out[u] = jnp.where(slot, wide[0:4], wide[4:8])

        def bands_to(src, dst, send, recv, u, half):
            return mesh_copy(src.at[u], dst.at[sp, tile], send, recv, {"grp": 1, "tile": u, "spec": half})

        def send_bands(u, carry):
            bands_to(MSG2, BR, f_send, f_recv, u, sp).start()
            bands_to(MSG2, BR, f_send, f_recv, u, other).start()
            bands_to(MSG3, BT, g_send, g_recv, u, 0).start()
            return carry

        lax.fori_loop(0, TILES, send_bands, 0)
        swap.wait_recv()
        final = tuple(
            wet[h] / (1.0 + stiff[h] * (sums[0][h] + TR[n, 0, :, halves[h]])) for h in range(2)
        )

        def store(c):
            rows = pl.ds(pl.multiple_of(c * RCH * 8, 8), RCH * 8)
            return [
                pltpu.make_async_copy(B.at[h, rows, :], out_w.at[rows, hs], load_sem.at[c, h])
                for h, hs in enumerate(halves)
            ]

        def finish(c, carry):
            def scale_f(i, carry):
                for d in range(DLOC):
                    rows = pl.ds(pl.multiple_of((c * RCH + i * DLOC + d) * 8, 8), 8)
                    for h in range(2):
                        B[h, rows, :] = B[h, rows, :] * final[h]
                return carry

            lax.fori_loop(0, FCH, scale_f, 0)
            for copy in store(c):
                copy.start()
            return carry

        lax.fori_loop(0, CHUNKS, finish, 0)
        def drain(c, carry):
            for copy in store(c):
                copy.wait()

            @pl.when(has_hi)
            def _():
                for n in range(WSTEPS):
                    halo(n, 0, c).wait_send()

            @pl.when(has_lo)
            def _():
                for n in range(WSTEPS):
                    halo(n, 1, c).wait_send()

            return carry

        lax.fori_loop(0, CHUNKS, drain, 0)
        for m in range(WSTEPS - 1):
            for condition, copy in total_copies(m):
                gated(condition, copy.wait_send)
        swap.wait_send()
        gated(has_hi, neighbour(0).wait_send)
        gated(has_lo, neighbour(1).wait_send)
        settle(MMSG, m_send)
        settle(BR, f_send)
        settle(MSG3, g_send)

    @pl.when(grp == 1)
    def circulation():
        top = (1 - sp).astype(F32)
        deep = sp.astype(F32)
        down = jnp.where(sp == 0, 1.0, math.exp(-1.0)).astype(F32)
        loads = [
            pltpu.make_async_copy(ocean_h.at[:, halves[0]], Q.at[0], small_sem.at[0]),
            pltpu.make_async_copy(ocean_h.at[:, halves[1]], Q.at[1], small_sem.at[1]),
            pltpu.make_async_copy(sea_h, sea, small_sem.at[2]),
        ]
        for copy in loads:
            copy.start()
        for copy in loads:
            copy.wait()
        for c in range(2):
            for h, hs in enumerate(halves):
                acc = jnp.zeros((8, 128), F32)
                for k in range(KLOC):
                    acc += Q[h, pl.ds((c * KLOC + k) * 8, 8), :] * float(_wgt[k])
                CS[pl.ds(8 * c, 8), hs] = acc * down

        def edge(n, side):
            return mesh_copy(
                ES.at[n, side], EH.at[n, side], e_send.at[n, side], e_recv.at[n, side],
                {"tile": hi_t if side == 0 else lo_t},
            )

        def level(n):
            return mesh_copy(LS.at[n], LH.at[n], l_send.at[n], l_recv.at[n], {"spec": other})

        def rims_out(n, src):
            for c in range(3):
                for h, hs in enumerate(halves):
                    ES[n, 0, pl.ds(8 * c, 8), hs] = src[h, pl.ds(c * 64 + 7, 8, stride=8), :]
                    ES[n, 1, pl.ds(8 * c, 8), hs] = src[h, pl.ds(c * 64, 8, stride=8), :]
                    LS[n, pl.ds(8 * c, 8), hs] = jnp.where(
                        sp == 0, src[h, pl.ds(c * 64 + 56, 8), :], src[h, pl.ds(c * 64, 8), :]
                    )
            for side in range(2):
                ES[n, side, 24:32, :] = sea[...]
            pl.when(has_hi)(edge(n, 0).start)
            pl.when(has_lo)(edge(n, 1).start)
            level(n).start()

        SX[...] = jnp.zeros((128, 256), F32)
        put(SX, tuple(0.5 * x for x in pair(sea)), slice(16, 24))
        SX[0:16, :] = CS[...]
        ahead_rows = (lane & 7) < 4
        for c in range(2):
            src = tuple(SX[pl.ds(8 + 8 * c, 8), hs] for hs in halves)
            ahead, behind = circular(src, 120), circular(src, 8)
            ahead = (ahead[1], ahead[0])
            put(SX, tuple(jnp.where(ahead_rows, ahead[h], behind[h]) for h in range(2)), slice(24 + 8 * c, 32 + 8 * c))
        slot = lax.broadcasted_iota(jnp.int32, (4, 128), 1) < 64
        for h, hs in enumerate(halves):
            turned = pltpu.roll(SX[:, hs].T, tile % 8 * 8, 1)
            turned = turned + pltpu.roll(turned, 64, 1)
            for k in range(16):
                MSG[16 * h + k] = jnp.where(slot, turned[8 * k : 8 * k + 4], turned[8 * k + 4 : 8 * k + 8])
        everyone_in()

        def to_wave(u, half):
            return mesh_copy(
                MSG.at[u], QR.at[sp, tile], q_send, q_recv, {"grp": 0, "tile": u, "spec": half},
            )

        def send_q(u, carry):
            to_wave(u, sp).start()
            to_wave(u, other).start()
            return carry

        lax.fori_loop(0, TILES, send_q, 0)
        rims_out(0, Q)

        @pl.when(jnp.logical_not(has_lo))
        def _():
            EH[:, 0] = jnp.zeros((2, 32, 256), F32)

        @pl.when(jnp.logical_not(has_hi))
        def _():
            EH[:, 1] = jnp.zeros((2, 32, 256), F32)

        settle(MR, m_recv)
        flags = pltpu.make_async_copy(MR, out_m, small_sem.at[0])
        flags.start()
        (mask3,) = arrived(MR, BTS, tile, 1)
        mask = tuple(x[1] for x in mask3)

        def substep(n, src, dst):
            for c in range(3):
                for k in range(KLOC):
                    at = (c * KLOC + k) * 8
                    x = tuple(src[h, pl.ds(at, 8), :] for h in range(2))
                    row_at = 8 * c + k
                    lower = tuple(
                        jnp.where(first_row, EH[n, 0, row_at : row_at + 1, hs], pltpu.roll(x[h], 1, 0))
                        for h, hs in enumerate(halves)
                    )
                    upper = tuple(
                        jnp.where(last_row, EH[n, 1, row_at : row_at + 1, hs], pltpu.roll(x[h], 7, 0))
                        for h, hs in enumerate(halves)
                    )
                    side = lateral(x, lower, upper)
                    for h, hs in enumerate(halves):
                        if k > 0:
                            above = src[h, pl.ds(at - 8, 8), :]
                        else:
                            above = LH[n, pl.ds(8 * c, 8), hs] * deep
                        if k < KLOC - 1:
                            below = src[h, pl.ds(at + 8, 8), :]
                        else:
                            below = LH[n, pl.ds(8 * c, 8), hs] * top
                        value = x[h] + 0.1 * side[h] + 0.2 * (above + below - 2.0 * x[h])
                        if c == 0:
                            value = value + 0.1 * src[h, pl.ds(at + 64, 8), :]
                        if c == 1:
                            value = value - 0.1 * src[h, pl.ds(at - 64, 8), :]
                        dst[h, pl.ds(at, 8), :] = value * mask[h]

        def rims_in(n):
            pl.when(has_lo)(edge(n, 0).wait_recv)
            pl.when(has_hi)(edge(n, 1).wait_recv)
            level(n).wait_recv()

        rims_in(0)
        for h, hs in enumerate(halves):
            level_here = sea[:, hs]
            SEA3[0:8, hs] = jnp.where(first_row, EH[0, 0, 31:32, hs], pltpu.roll(level_here, 1, 0))
            SEA3[8:16, hs] = level_here
            SEA3[16:24, hs] = jnp.where(last_row, EH[0, 1, 24:25, hs], pltpu.roll(level_here, 7, 0))
        seas = pltpu.make_async_copy(SEA3, out_s, small_sem.at[1])
        seas.start()
        substep(0, Q, A1)
        rims_out(1, A1)
        rims_in(1)
        substep(1, A1, A2)

        results = [pltpu.make_async_copy(A2.at[h], out_o.at[:, hs], out_sem.at[h]) for h, hs in enumerate(halves)]
        for copy in results:
            copy.start()
        for n in range(2):
            pl.when(has_hi)(edge(n, 0).wait_send)
            pl.when(has_lo)(edge(n, 1).wait_send)
            level(n).wait_send()
        settle(QR, q_send)
        flags.wait()
        seas.wait()
        for copy in results:
            copy.wait()
        settle(BR, f_recv)
        pl.when(sp == 0)(lambda: settle(BT, g_recv))


def tail(wave_h, unforced_h, bands_h, north_h, flags_h, sea_h, out_w, out_o, zeros, A2, BR, BT, MR, U, sea, BTS, in_sem, w_sem, o_sem):
    grp = lax.axis_index("grp")
    tile = lax.axis_index("tile")
    sp = lax.axis_index("spec")

    @pl.when(grp == 0)
    def wave():
        copies = []
        for c in range(CHUNKS):
            rows = pl.ds(c * RCH * 8, RCH * 8)
            copies.append(pltpu.make_async_copy(wave_h.at[rows, :], out_w.at[rows, :], w_sem.at[c]))
            copies[-1].start()
        zeros[0:192, :] = jnp.zeros((192, 256), F32)
        copies.append(pltpu.make_async_copy(zeros.at[0:192, :], out_o, o_sem.at[0]))
        copies[-1].start()
        for copy in copies:
            copy.wait()

    @pl.when(grp == 1)
    def circulation():
        loads = [
            pltpu.make_async_copy(flags_h, MR, in_sem.at[0]),
            pltpu.make_async_copy(bands_h, BR, in_sem.at[1]),
            pltpu.make_async_copy(sea_h, sea, in_sem.at[4]),
        ] + [pltpu.make_async_copy(unforced_h.at[:, hs], A2.at[h], in_sem.at[2 + h]) for h, hs in enumerate(HALVES)]
        for copy in loads:
            copy.start()
        norths = pltpu.make_async_copy(north_h, BT, in_sem.at[5])

        @pl.when(sp == 0)
        def _():
            norths.start()

        zeros[...] = jnp.zeros(zeros.shape, F32)
        blanks = []
        for c in range(CHUNKS):
            rows = pl.ds(c * RCH * 8, RCH * 8)
            blanks.append(pltpu.make_async_copy(zeros, out_w.at[rows, :], w_sem.at[c]))
            blanks[-1].start()
        row = lax.broadcasted_iota(jnp.int32, (8, 128), 0)
        top = (1 - sp).astype(F32)
        deep = sp.astype(F32)
        down = jnp.where(sp == 0, 1.0, math.exp(-1.0)).astype(F32)
        at_lo = jnp.where(tile > 0, 1.0, 0.0).astype(F32)
        at_hi = jnp.where(tile < TILES - 1, 1.0, 0.0).astype(F32)
        loads[0].wait()
        (mask3,) = arrived(MR, BTS, tile, 1)
        mask = tuple(x[1] for x in mask3)
        mask_lo = tuple(jnp.where(row == 0, x[0] * at_lo, x[0]) for x in mask3)
        mask_hi = tuple(jnp.where(row == 7, x[2] * at_hi, x[2]) for x in mask3)
        for copy in loads[1:]:
            copy.wait()

        @pl.when(sp == 0)
        def _():
            norths.wait()

        @pl.when(sp == 1)
        def _():
            BT[...] = jnp.zeros(BT.shape, F32)

        def unpacked(buf, slots):
            for t in range(TILES):
                both = buf[0, t] + buf[1, t]
                U[8 * t : 8 * t + 8, :] = jnp.concatenate([both, pltpu.roll(both, 64, 1)], axis=0)
            for h in range(2):
                turned = U[pl.ds(128 * h, 128), :].T
                BTS[pl.ds(0, 64), HALVES[h]] = turned[0:64]
                BTS[pl.ds(64, 64), HALVES[h]] = turned[0:64]
            out = []
            for f in range(slots):
                start = pl.multiple_of((8 * tile + 16 * f) % 64, 8)
                wide = BTS[pl.ds(start, 16), :]
                out.append(tuple((wide[0:8, hs], wide[1:9, hs], wide[2:10, hs]) for hs in HALVES))
            return out

        total, drift_e, drift_n, stress_e = unpacked(BR, 4)
        (stress_n,) = unpacked(BT, 1)
        factor = []
        for h, hs in enumerate(HALVES):
            row_of = []
            for q, masked in enumerate((mask_lo, mask, mask_hi)):
                depth = 10.0 + 4.0 * sea[8 * q : 8 * q + 8, hs]
                row_of.append(masked[h] / (1.0 + 25.0 * total[h][q] / (depth * depth)))
            factor.append(row_of)
        forced, spread = [], []
        for three in (stress_e, stress_n, drift_e, drift_n):
            lower, own, upper = (tuple(three[h][q] * factor[h][q] for h in range(2)) for q in range(3))
            forced.append(own)
            spread.append(lateral(own, lower, upper))
        for k in range(KLOC):
            near, far = math.exp(0.125), math.exp(-0.125)
            prof = float(_prof[k]) * down
            above = near if k > 0 else near * deep
            below = far if k < KLOC - 1 else far * top
            stay = prof * (1.0 + 0.2 * (above + below - 2.0))
            for h, hs in enumerate(HALVES):
                east = (0.1 * prof) * forced[3][h]
                north = (-0.1 * prof) * forced[2][h]
                d_east = (0.1 * stay) * forced[3][h] + (0.01 * prof) * spread[3][h]
                d_north = (-0.1 * stay) * forced[2][h] - (0.01 * prof) * spread[2][h]
                if k == 0:
                    east = east + top * forced[0][h]
                    north = north + top * forced[1][h]
                    d_east = d_east + top * (0.6 * forced[0][h] + 0.1 * spread[0][h])
                    d_north = d_north + top * (0.6 * forced[1][h] + 0.1 * spread[1][h])
                if k == 1:
                    d_east = d_east + (0.2 * top) * forced[0][h]
                    d_north = d_north + (0.2 * top) * forced[1][h]
                A2[h, pl.ds(8 * k, 8), :] += mask[h] * (d_east + 0.1 * north) + east
                A2[h, pl.ds(64 + 8 * k, 8), :] += mask[h] * (d_north - 0.1 * east) + north
        results = [pltpu.make_async_copy(A2.at[h], out_o.at[:, hs], o_sem.at[h]) for h, hs in enumerate(HALVES)]
        for copy in results:
            copy.start()

        for copy in results + blanks:
            copy.wait()


def body(spectrum, wind, land_mask, intersection, ocean_state, sea_level):
    v = lambda *shape, dtype=F32: pltpu.VMEM(shape, dtype)
    dma = lambda *shape: pltpu.SemaphoreType.DMA(shape) if shape else pltpu.SemaphoreType.DMA
    anywhere = pl.BlockSpec(memory_space=pltpu.HBM)
    scratch = [
        pltpu.SMEM(TABLE.shape, F32),
        v(2, FD * 8, 128), v(2, FD * 8, 128), v(5, 2, PCH * RCH * 8, 128), v(DLOC, 8, 256), v(FD, 128),
        v(WSTEPS, 2, 2, FD, 128), v(WSTEPS, 2, 2, FD, 128),
        v(2, 8, 256), v(8, 256, dtype=jnp.int32), v(8, 256, dtype=jnp.int32),
        v(16, 256, dtype=jnp.int32), v(2, 16, 256, dtype=jnp.int32),
        v(2, TILES, 4, 128), v(WSTEPS, 8, 256), v(WSTEPS, 5, 8, 256), v(TILES, 4, 128), v(TILES, 4, 128), v(256, 128),
        v(2, 192, 128), v(2, 192, 128), v(2, 192, 128), v(8, 256), v(16, 256), v(128, 256),
        v(TILES, 4, 128), v(256, 128), v(256, 256),
        v(2, 2, 32, 256), v(2, 2, 32, 256), v(24, 256), v(2, 24, 256), v(2, 24, 256),
        dma(CHUNKS, 2), dma(3), dma(WSTEPS, 2, CHUNKS), dma(WSTEPS, 2, CHUNKS), dma(WSTEPS, 5), dma(WSTEPS, 5),
        dma(2), dma(2), dma(), dma(), dma(), dma(), dma(), dma(), dma(), dma(),
        dma(2, 2), dma(2, 2), dma(2), dma(2), dma(2),
    ]
    landed = pl.pallas_call(
        kernel,
        out_shape=(
            jax.ShapeDtypeStruct((FD * 8, 256), F32),
            jax.ShapeDtypeStruct((192, 256), F32),
            jax.ShapeDtypeStruct((2, TILES, 4, 128), F32),
            jax.ShapeDtypeStruct((2, TILES, 4, 128), F32),
            jax.ShapeDtypeStruct((256, 128), F32),
            jax.ShapeDtypeStruct((24, 256), F32),
        ),
        in_specs=[anywhere] * 6,
        out_specs=(pl.BlockSpec(memory_space=pl.ANY),) * 6,
        scratch_shapes=scratch,
        compiler_params=pltpu.CompilerParams(collective_id=0, has_side_effects=True, vmem_limit_bytes=48 << 20),
    )(
        *(
            pltpu.with_memory_space_constraint(x, pltpu.HBM)
            for x in (
                spectrum.reshape(FD * 8, 256),
                wind,
                land_mask,
                intersection,
                ocean_state.reshape(192, 256),
                sea_level.reshape(8, 256),
            )
        )
    )
    waves, ocean = pl.pallas_call(
        tail,
        out_shape=(jax.ShapeDtypeStruct((FD * 8, 256), F32), jax.ShapeDtypeStruct((192, 256), F32)),
        in_specs=[pl.BlockSpec(memory_space=pl.ANY)] * 6,
        out_specs=(pl.BlockSpec(memory_space=pl.ANY),) * 2,
        scratch_shapes=[
            v(RCH * 8, 256), v(2, 192, 128), v(2, TILES, 4, 128), v(2, TILES, 4, 128), v(256, 128), v(256, 128),
            v(24, 256), v(256, 256), dma(6), dma(CHUNKS), dma(2),
        ],
        compiler_params=pltpu.CompilerParams(vmem_limit_bytes=6 << 20),
    )(*landed)
    return waves.reshape(spectrum.shape), ocean.reshape(ocean_state.shape)


def solution(mesh):
    return jax.shard_map(
        body,
        mesh=mesh,
        in_specs=(
            P("grp", None, "spec", "tile", None),
            P(None, "tile", None),
            P("tile", None),
            P("tile", None),
            P("grp", None, "spec", "tile", None),
            P("grp", "tile", None),
        ),
        out_specs=(P("grp", None, "spec", "tile", None), P("grp", None, "spec", "tile", None)),
        check_vma=False,
    )
```
